32 devices in a mesh: grp: 2 (over core), dp: 16 (over z, y, x).
Axes of the slice: x: 2, y: 2, z: 4, core: 2. Of those that a mesh axis runs over, the one named last changes fastest.
Arguments:
- incoming_vectors: bfloat16 [20480, 768], P(('grp', 'dp')), may hold values from -6 to 6
- sequence_extents: int32 [256], P(('grp', 'dp')), may hold values from 1 to 633, as said below
- matching_document_index: int32 [128], replicated, may hold values from 0 to 127, each once
- softmax_sharpness: float32 [1], replicated, may hold values from 0.02 to 0.03
- optimizer_iteration_number: int32 [1], replicated, may hold values from 1 to 20
- attention_entry_master: float32 [2, 768, 2304], P(None, 'dp'), may hold values from -0.21875 to 0.21875
- attention_entry_first_moment: float32 [2, 768, 2304], P(None, 'dp'), may hold values from -0.0048828125 to 0.0048828125
- attention_entry_second_moment: float32 [2, 768, 2304], P(None, 'dp'), may hold values from 5.2981908e-09 to 8.477105e-08
- attention_exit_master: float32 [2, 768, 768], P(None, 'dp'), may hold values from -0.625 to 0.625
- attention_exit_first_moment: float32 [2, 768, 768], P(None, 'dp'), may hold values from -0.0048828125 to 0.0048828125
- attention_exit_second_moment: float32 [2, 768, 768], P(None, 'dp'), may hold values from 5.2981908e-09 to 8.477105e-08
- widening_projection_master: float32 [2, 768, 6144], P(None, 'dp'), may hold values from -0.21875 to 0.21875
- widening_first_moment: float32 [2, 768, 6144], P(None, 'dp'), may hold values from -0.0048828125 to 0.0048828125
- widening_second_moment: float32 [2, 768, 6144], P(None, 'dp'), may hold values from 5.2981908e-09 to 8.477105e-08
- lowering_projection_master: float32 [2, 3072, 768], P(None, 'dp'), may hold values from -0.109375 to 0.109375
- lowering_first_moment: float32 [2, 3072, 768], P(None, 'dp'), may hold values from -0.0048828125 to 0.0048828125
- lowering_second_moment: float32 [2, 3072, 768], P(None, 'dp'), may hold values from 5.2981908e-09 to 8.477105e-08
- layernorm_affine_master: float32 [2, 4, 768], P(None, None, 'dp'), may hold values from -0.1 to 1.4, as said below
- layernorm_affine_first_moment: float32 [2, 4, 768], P(None, None, 'dp'), may hold values from -0.01953125 to 0.01953125
- layernorm_affine_second_moment: float32 [2, 4, 768], P(None, None, 'dp'), may hold values from 8.477105e-08 to 1.3245476e-06
Outputs:
- hidden_out: bfloat16 [20480, 768], P(('grp', 'dp'))
- input_grad: float32 [20480, 768], P(('grp', 'dp'))
- loss_value: float32 [1], replicated
- joint_weight: float32 [2, 768, 2304], P(None, 'dp')
- joint_moment: float32 [2, 768, 2304], P(None, 'dp')
- joint_square: float32 [2, 768, 2304], P(None, 'dp')
- joint_copy: bfloat16 [2, 768, 2304], P(None, 'dp')
- output_weight: float32 [2, 768, 768], P(None, 'dp')
- output_moment: float32 [2, 768, 768], P(None, 'dp')
- output_square: float32 [2, 768, 768], P(None, 'dp')
- output_copy: bfloat16 [2, 768, 768], P(None, 'dp')
- gateup_weight: float32 [2, 768, 6144], P(None, 'dp')
- gateup_moment: float32 [2, 768, 6144], P(None, 'dp')
- gateup_square: float32 [2, 768, 6144], P(None, 'dp')
- gateup_copy: bfloat16 [2, 768, 6144], P(None, 'dp')
- down_weight: float32 [2, 3072, 768], P(None, 'dp')
- down_moment: float32 [2, 3072, 768], P(None, 'dp')
- down_square: float32 [2, 3072, 768], P(None, 'dp')
- down_copy: bfloat16 [2, 3072, 768], P(None, 'dp')
- norms_weight: float32 [2, 4, 768], P(None, None, 'dp')
- norms_moment: float32 [2, 4, 768], P(None, None, 'dp')
- norms_square: float32 [2, 4, 768], P(None, None, 'dp')
- norms_copy: bfloat16 [2, 4, 768], P(None, None, 'dp')
The draws below stay inside these ranges and needn't reach their ends.
Inputs may be any that keep to these rules, and one draw needn't show every extreme that they name: `sequence_extents`: the first 128 lengths are queries, each at most 64 and one exactly 64; the 8 sequences of one device never hold more than 640 slots together, and some document device holds one document of 633 slots. `layernorm_affine_master`: rows 0 and 2 of each layer are gains, rows 1 and 3 biases.
All inputs are finite; a program needn't handle non-finite values.
Results may differ from the reference program's by a relative error of at most 0.025.
Values may be sent and summed in bfloat16 or wider, within the bound.
No kernel may reach another device: no remote copies, remote signals or barrier semaphores. Data moves between devices by JAX's collectives and lax.ppermute only.
A program may use at most 384 MiB of HBM per device.

```python
import math
import jax
import jax.numpy as jnp
from jax import lax

D = 768
HEADS = 12
FF = 3072
HDIM = 64
LAYERS = 2
TOK_DEV = 640
SEQ_DEV = 8
TOKENS = 20480
NSEQ = 256
PAIR_TOTAL = 128
QMAX = 64
MAXDOC = 633
N_GRP = 2
N_DP = 16


def draw_sequence_extents(key, part):
    key_query, key_spot, key_power, key_raw, key_device, key_slot = jax.random.split(key, 6)
    queries = jax.random.randint(key_query, (PAIR_TOTAL,), QMAX // 4 + 1, QMAX + 1)
    spot = jax.random.randint(key_spot, (), 0, PAIR_TOTAL)
    queries = jnp.where(jnp.arange(PAIR_TOTAL) == spot, QMAX, queries)
    powers = jax.random.randint(key_power, (PAIR_TOTAL,), 2, 11)
    raw_lengths = jax.random.randint(key_raw, (PAIR_TOTAL,), 1, jnp.left_shift(1, powers))
    doc_devices = PAIR_TOTAL // SEQ_DEV
    raw_lengths = raw_lengths.reshape(doc_devices, SEQ_DEV)
    totals = jnp.sum(raw_lengths, axis=1, keepdims=True)
    fitted = jnp.where(totals > TOK_DEV, raw_lengths * (TOK_DEV - SEQ_DEV) // totals + 1, raw_lengths)
    chosen = jax.random.randint(key_device, (), 0, doc_devices)
    slot_pick = jax.random.randint(key_slot, (), 0, SEQ_DEV)
    single = jnp.where(jnp.arange(SEQ_DEV) == slot_pick, MAXDOC, 1)
    fitted = jnp.where(jnp.arange(doc_devices)[:, None] == chosen, single[None, :], fitted)
    return jnp.concatenate([queries, fitted.reshape(PAIR_TOTAL)]).astype(jnp.int32)


def draw_layernorm_affine_master(key, part):
    key_gain, key_bias = jax.random.split(key, 2)
    gain_rows = jax.random.uniform(key_gain, (LAYERS, 2, D), jnp.float32, 0.6, 1.4)
    biases = jax.random.uniform(key_bias, (LAYERS, 2, D), jnp.float32, -0.1, 0.1)
    return jnp.stack([gain_rows[:, 0], biases[:, 0], gain_rows[:, 1], biases[:, 1]], axis=1)


def block_levels(rng, dims, pieces, low, largest):
    def one(dim, shards_of):
        heights = jax.random.uniform(jax.random.fold_in(jax.random.fold_in(rng, 6), dim), (shards_of,), jnp.float32, low / len(pieces), largest / len(pieces))
        return jnp.repeat(jnp.exp(heights), dims[dim] // shards_of).reshape((-1,) + (1,) * (len(dims) - dim - 1))

    level = one(*pieces[0])
    for cut in pieces[1:]:
        level = level * one(*cut)
    return level


def gaussian(key, shape, width, reach, shards=(), kind=jnp.bfloat16):
    entries = width * jax.random.normal(key, shape, jnp.float32)
    if shards:
        entries = entries * block_levels(key, shape, shards, -0.22, 0.18)
    return jnp.clip(entries, -reach, reach).astype(kind)


def setup_inputs(seed: int = 0) -> dict:
    arg_keys = jax.random.split(jax.random.key(seed), 21)
    incoming_vectors = gaussian(arg_keys[0], (TOKENS, D), 1.0, 6.0, ((0, 32),))
    sequence_extents = draw_sequence_extents(jax.random.fold_in(arg_keys[20], 71), 0)
    matching_document_index = jax.random.permutation(arg_keys[2], PAIR_TOTAL).astype(jnp.int32)
    softmax_sharpness = jnp.clip(jax.random.uniform(arg_keys[3], (1,), jnp.float32, 0.02, 0.03), 0.02, 0.03)
    optimizer_iteration_number = jax.random.randint(arg_keys[4], (1,), 1, 21).astype(jnp.int32)
    attention_entry_master = gaussian(arg_keys[5], (LAYERS, D, 3 * D), D ** -0.5, 0.21875, ((1, 16),), jnp.float32)
    attention_entry_first_moment = gaussian(arg_keys[6], (LAYERS, D, 3 * D), (3.0 / (D * PAIR_TOTAL ** 0.5)), 0.0048828125, ((1, 16),), jnp.float32)
    attention_entry_second_moment = jnp.clip(jnp.exp(math.log(8.477105239990124e-08) - 2.7725887 * jax.random.uniform(arg_keys[7], (LAYERS, D, 3 * D), jnp.float32) ** block_levels(arg_keys[7], (LAYERS, D, 3 * D), ((1, 16),), -0.2, 0.2)), 5.298190774993827e-09, 8.477105239990124e-08)
    attention_exit_master = gaussian(arg_keys[8], (LAYERS, D, D), (D // 8) ** -0.5, 0.625, ((1, 16),), jnp.float32)
    attention_exit_first_moment = gaussian(arg_keys[9], (LAYERS, D, D), (3.0 / (D * PAIR_TOTAL ** 0.5)), 0.0048828125, ((1, 16),), jnp.float32)
    attention_exit_second_moment = jnp.clip(jnp.exp(math.log(8.477105239990124e-08) - 2.7725887 * jax.random.uniform(arg_keys[10], (LAYERS, D, D), jnp.float32) ** block_levels(arg_keys[10], (LAYERS, D, D), ((1, 16),), -0.2, 0.2)), 5.298190774993827e-09, 8.477105239990124e-08)
    widening_projection_master = gaussian(arg_keys[11], (LAYERS, D, 2 * FF), D ** -0.5, 0.21875, ((1, 16),), jnp.float32)
    widening_first_moment = gaussian(arg_keys[12], (LAYERS, D, 2 * FF), (3.0 / (D * PAIR_TOTAL ** 0.5)), 0.0048828125, ((1, 16),), jnp.float32)
    widening_second_moment = jnp.clip(jnp.exp(math.log(8.477105239990124e-08) - 2.7725887 * jax.random.uniform(arg_keys[13], (LAYERS, D, 2 * FF), jnp.float32) ** block_levels(arg_keys[13], (LAYERS, D, 2 * FF), ((1, 16),), -0.2, 0.2)), 5.298190774993827e-09, 8.477105239990124e-08)
    lowering_projection_master = gaussian(arg_keys[14], (LAYERS, FF, D), FF ** -0.5, 0.109375, ((1, 16),), jnp.float32)
    lowering_first_moment = gaussian(arg_keys[15], (LAYERS, FF, D), (3.0 / (D * PAIR_TOTAL ** 0.5)), 0.0048828125, ((1, 16),), jnp.float32)
    lowering_second_moment = jnp.clip(jnp.exp(math.log(8.477105239990124e-08) - 2.7725887 * jax.random.uniform(arg_keys[16], (LAYERS, FF, D), jnp.float32) ** block_levels(arg_keys[16], (LAYERS, FF, D), ((1, 16),), -0.2, 0.2)), 5.298190774993827e-09, 8.477105239990124e-08)
    layernorm_affine_master = draw_layernorm_affine_master(jax.random.fold_in(arg_keys[20], 71), 0)
    layernorm_affine_first_moment = gaussian(arg_keys[18], (LAYERS, 4, D), (12.0 / (D * PAIR_TOTAL ** 0.5)), 0.01953125, ((2, 16),), jnp.float32)
    layernorm_affine_second_moment = jnp.clip(jnp.exp(math.log(1.3245476111478638e-06) - 2.748872 * jax.random.uniform(arg_keys[19], (LAYERS, 4, D), jnp.float32) ** block_levels(arg_keys[19], (LAYERS, 4, D), ((2, 16),), -0.2, 0.2)), 8.477105239990124e-08, 1.3245476111478638e-06)
    return {"incoming_vectors": incoming_vectors, "sequence_extents": sequence_extents, "matching_document_index": matching_document_index, "softmax_sharpness": softmax_sharpness, "optimizer_iteration_number": optimizer_iteration_number, "attention_entry_master": attention_entry_master, "attention_entry_first_moment": attention_entry_first_moment, "attention_entry_second_moment": attention_entry_second_moment, "attention_exit_master": attention_exit_master, "attention_exit_first_moment": attention_exit_first_moment, "attention_exit_second_moment": attention_exit_second_moment, "widening_projection_master": widening_projection_master, "widening_first_moment": widening_first_moment, "widening_second_moment": widening_second_moment, "lowering_projection_master": lowering_projection_master, "lowering_first_moment": lowering_first_moment, "lowering_second_moment": lowering_second_moment, "layernorm_affine_master": layernorm_affine_master, "layernorm_affine_first_moment": layernorm_affine_first_moment, "layernorm_affine_second_moment": layernorm_affine_second_moment}


@jax.custom_vjp
def low(v):
    return lax.optimization_barrier(v.astype(jnp.bfloat16)).astype(jnp.float32)

@jax.custom_vjp
def low_back(v):
    return v

def low_keep(v):
    return (low(v), None)

def low_pass(kept, grad):
    return (grad,)

def back_keep(v):
    return (v, None)

def back_low(kept, grad):
    return (low(grad),)
low.defvjp(low_keep, low_pass)
low_back.defvjp(back_keep, back_low)
beta_one = 0.9
beta_two = 0.999
adam_eps = 1e-08
decay_rate = 0.01
rate_matrix = 0.08
rate_norms = 1.0
norm_eps = 1e-05
embed_eps = 1e-06
masked_score = -1000000000.0
rotary_base = 1000.0
topmost_precision = lax.Precision.HIGHEST

def segment_info(seq_lengths, rows_here):
    seq_ends = jnp.cumsum(seq_lengths).astype(jnp.int32)
    row_ids = jnp.arange(rows_here, dtype=jnp.int32)
    past_end = (row_ids[:, None] >= seq_ends[None, :]).astype(jnp.int32)
    segment = lax.optimization_barrier(jnp.sum(past_end, axis=1)).astype(jnp.int32)
    positions = row_ids - lax.optimization_barrier(jnp.sum(past_end * seq_lengths[None, :], axis=1)).astype(jnp.int32)
    member = (segment[:, None] == jnp.arange(seq_lengths.shape[0], dtype=jnp.int32)[None, :]).astype(jnp.float32)
    same_seg = segment[:, None] == segment[None, :]
    return (positions, member, same_seg)

def rotary_tables(positions, head_dim):
    half_dim = head_dim // 2
    frequency = rotary_base ** (-2.0 * jnp.arange(half_dim, dtype=jnp.float32) / head_dim)
    angles = positions.astype(jnp.float32)[:, None] * frequency[None, :]
    return (jnp.cos(angles), jnp.sin(angles))

def rotate(values, cosine, sine_part):
    half_dim = values.shape[-1] // 2
    front_half = values[..., :half_dim]
    back_half = values[..., half_dim:]
    cos_wide = cosine[:, None, :]
    sin_wide = sine_part[:, None, :]
    return jnp.concatenate([front_half * cos_wide - back_half * sin_wide, back_half * cos_wide + front_half * sin_wide], axis=-1)

def layer_norm(values, gain, bias):
    centered = values - lax.optimization_barrier(jnp.mean(values, axis=-1, keepdims=True))
    inv_std = lax.rsqrt(lax.optimization_barrier(jnp.mean(centered * centered, axis=-1, keepdims=True)) + norm_eps)
    return centered * inv_std * gain + bias

def layer_ref(inputs, weight_set, rotary, same_seg):
    joint_w, output_w, gateup_w, down_w, norm_rows = weight_set
    rows_here = inputs.shape[0]
    score_scale = 1.0 / math.sqrt(HDIM)
    inputs_low = low(inputs)
    merged = low_back(jnp.dot(inputs_low, joint_w, precision=topmost_precision))
    query_rot = low(rotate(merged[:, :D].reshape(rows_here, HEADS, HDIM), rotary[0], rotary[1]))
    key_rot = low(rotate(merged[:, D:2 * D].reshape(rows_here, HEADS, HDIM), rotary[0], rotary[1]))
    value_low = low(merged[:, 2 * D:].reshape(rows_here, HEADS, HDIM))
    similarity_logits = low_back(jnp.einsum('thd,shd->hts', query_rot, key_rot, precision=topmost_precision) * score_scale)
    similarity_logits = jnp.where(same_seg[None], similarity_logits, masked_score)
    weights_p = jax.nn.softmax(similarity_logits, axis=-1)
    mixed = jnp.einsum('hts,shd->thd', low(weights_p), value_low, precision=topmost_precision).reshape(rows_here, D)
    mixed = low(low_back(mixed))
    attended = low_back(jnp.dot(mixed, output_w, precision=topmost_precision))
    hidden = layer_norm(inputs + attended, norm_rows[0], norm_rows[1])
    hidden_low = low(hidden)
    gate_up = low_back(jnp.dot(hidden_low, gateup_w, precision=topmost_precision))
    activated = low(jax.nn.silu(gate_up[:, :FF]) * gate_up[:, FF:])
    branch = low_back(jnp.dot(activated, down_w, precision=topmost_precision))
    return layer_norm(hidden + branch, norm_rows[2], norm_rows[3])

def adamw_update(grad, master, first, second, bias_first, bias_second, rate, decay):
    moment = beta_one * first + (1.0 - beta_one) * grad
    squared_values = beta_two * second + (1.0 - beta_two) * grad * grad
    newer = master - rate * (moment / bias_first / (jnp.sqrt(squared_values / bias_second) + adam_eps) + decay * master)
    return (newer, moment, squared_values, newer.astype(jnp.bfloat16))

def reference(incoming_vectors, sequence_extents, matching_document_index, softmax_sharpness, optimizer_iteration_number, attention_entry_master, attention_entry_first_moment, attention_entry_second_moment, attention_exit_master, attention_exit_first_moment, attention_exit_second_moment, widening_projection_master, widening_first_moment, widening_second_moment, lowering_projection_master, lowering_first_moment, lowering_second_moment, layernorm_affine_master, layernorm_affine_first_moment, layernorm_affine_second_moment):
    masters = (attention_entry_master, attention_exit_master, widening_projection_master, lowering_projection_master, layernorm_affine_master)
    weights = tuple((lax.optimization_barrier(master.astype(jnp.bfloat16)).astype(jnp.float32) for master in masters))
    inputs = incoming_vectors.astype(jnp.float32).reshape(N_GRP * N_DP, TOK_DEV, D)
    block_lengths = sequence_extents.reshape(N_GRP * N_DP, SEQ_DEV)
    logit_scale_factor = 1.0 / softmax_sharpness[0]
    targets = (jnp.arange(PAIR_TOTAL, dtype=jnp.int32)[None, :] == matching_document_index[:, None]).astype(jnp.float32)

    def loss_fn(weight_set, input_set):

        def one_block(block_pair):
            block_rows, seq_lengths = block_pair
            positions, member, same_seg = segment_info(seq_lengths, TOK_DEV)
            rotary = rotary_tables(positions, HDIM)
            hidden_state = block_rows
            for layer_idx in range(LAYERS):
                hidden_state = layer_ref(hidden_state, tuple((weight[layer_idx] for weight in weight_set)), rotary, same_seg)
            pooled = jnp.einsum('ts,td->sd', member, hidden_state, precision=topmost_precision) / seq_lengths.astype(jnp.float32)[:, None]
            embeds = pooled * lax.rsqrt(lax.optimization_barrier(jnp.sum(pooled * pooled, axis=-1, keepdims=True)) + embed_eps)
            return (hidden_state, embeds)
        states, embed_blocks = lax.map(jax.checkpoint(one_block), (input_set, block_lengths))
        every_pooled_vector = low(embed_blocks.reshape(NSEQ, D))
        similarity_logits = jnp.dot(every_pooled_vector[:PAIR_TOTAL], every_pooled_vector[PAIR_TOTAL:].T, precision=topmost_precision) * logit_scale_factor
        row_peak = lax.optimization_barrier(jnp.max(similarity_logits, axis=-1, keepdims=True))
        log_total = row_peak[:, 0] + jnp.log(lax.optimization_barrier(jnp.sum(jnp.exp(similarity_logits - row_peak), axis=-1)))
        loss_total = jnp.mean(log_total - lax.optimization_barrier(jnp.sum(similarity_logits * targets, axis=-1)))
        return (loss_total, states)
    loss_total, pullback, states = jax.vjp(loss_fn, weights, inputs, has_aux=True)
    weight_grads, input_grads = pullback(jnp.ones_like(loss_total))
    step_float = optimizer_iteration_number[0].astype(jnp.float32)
    bias_first = 1.0 - jnp.power(beta_one, step_float)
    bias_second = 1.0 - jnp.power(beta_two, step_float)
    joint_weight, joint_moment, joint_square, joint_copy = adamw_update(weight_grads[0], attention_entry_master, attention_entry_first_moment, attention_entry_second_moment, bias_first, bias_second, rate_matrix, decay_rate)
    output_weight, output_moment, output_square, output_copy = adamw_update(weight_grads[1], attention_exit_master, attention_exit_first_moment, attention_exit_second_moment, bias_first, bias_second, rate_matrix, decay_rate)
    gateup_weight, gateup_moment, gateup_square, gateup_copy = adamw_update(weight_grads[2], widening_projection_master, widening_first_moment, widening_second_moment, bias_first, bias_second, rate_matrix, decay_rate)
    down_weight, down_moment, down_square, down_copy = adamw_update(weight_grads[3], lowering_projection_master, lowering_first_moment, lowering_second_moment, bias_first, bias_second, rate_matrix, decay_rate)
    norms_weight, norms_moment, norms_square, norms_copy = adamw_update(weight_grads[4], layernorm_affine_master, layernorm_affine_first_moment, layernorm_affine_second_moment, bias_first, bias_second, rate_norms, 0.0)
    hidden_out = states.reshape(TOKENS, D).astype(jnp.bfloat16)
    input_grad = input_grads.reshape(TOKENS, D)
    loss_value = loss_total.reshape(1)
    return (hidden_out, input_grad, loss_value, joint_weight, joint_moment, joint_square, joint_copy, output_weight, output_moment, output_square, output_copy, gateup_weight, gateup_moment, gateup_square, gateup_copy, down_weight, down_moment, down_square, down_copy, norms_weight, norms_moment, norms_square, norms_copy)
```

```python
import math

import jax
import jax.numpy as jnp
from jax import lax
from jax.sharding import PartitionSpec as P

D = 768
HEADS = 12
FF = 3072
HDIM = 64
LAYERS = 2


beta_one = 0.9
beta_two = 0.999
adam_eps = 1e-08
decay_rate = 0.01
rate_matrix = 0.08
rate_norms = 1.0
norm_eps = 1e-05
embed_eps = 1e-06
masked_score = -1000000000.0
rotary_base = 1000.0
topmost_precision = lax.Precision.HIGHEST


def axis_bits(axis):
    return lax.axis_size(axis).bit_length() - 1


def swap_bit(value, axis, bit):
    count = lax.axis_size(axis)
    return lax.ppermute(value, axis, [(i, i ^ (1 << bit)) for i in range(count)])


def my_bit(axis, bit):
    return (lax.axis_index(axis) >> bit) & 1


def cube_gather(piece, axis, bits):
    held = []
    for bit in bits:
        other = swap_bit(piece, axis, bit)
        place = sum(1 for b in held if b > bit)
        first = my_bit(axis, bit) == 0
        piece = jnp.stack(
            [jnp.where(first, piece, other), jnp.where(first, other, piece)], axis=place
        )
        held.append(bit)
    return piece


def cube_scatter(whole, axis, bits):
    left = sorted(bits, reverse=True)
    for bit in bits:
        place = left.index(bit)
        mine = my_bit(axis, bit)
        away = lax.dynamic_index_in_dim(whole, 1 - mine, place, keepdims=False)
        keep = lax.dynamic_index_in_dim(whole, mine, place, keepdims=False)
        other = swap_bit(away, axis, bit)
        whole = (keep.astype(jnp.float32) + other.astype(jnp.float32)).astype(whole.dtype)
        left.remove(bit)
    return whole


def bit_order(color):
    order = list(range(axis_bits("dp") - 1, -1, -1))
    if color and len(order) > 1:
        order[-1], order[-2] = order[-2], order[-1]
    return order


def core_half(value, core, axis):
    half = value.shape[axis] // 2
    return lax.dynamic_slice_in_dim(value, core * half, half, axis)


def gather_half(shard, core, color):
    piece = core_half(shard, core, 1).astype(jnp.bfloat16)
    mine = cube_gather(piece, "dp", bit_order(color))
    mine = mine.reshape(-1, piece.shape[1])
    return mine, swap_bit(mine, "grp", 0)


def in_order(mine, other, first):
    return jnp.concatenate(
        [jnp.where(first, mine, other), jnp.where(first, other, mine)], axis=1
    )


def own_and_far(value, first):
    half = value.shape[1] // 2
    low, high = value[:, :half], value[:, half:]
    return jnp.where(first, low, high), jnp.where(first, high, low)


def scatter_half(mine, other, color):
    both = mine + swap_bit(other.astype(jnp.bfloat16), "grp", 0).astype(jnp.float32)
    both = both.astype(jnp.bfloat16)
    bits = bit_order(color)[::-1]
    cube = both.reshape((2,) * len(bits) + (-1, both.shape[1]))
    rows = cube_scatter(cube, "dp", bits)
    for bit in range(1, axis_bits("grp")):
        rows = (
            rows.astype(jnp.float32) + swap_bit(rows, "grp", bit).astype(jnp.float32)
        ).astype(jnp.bfloat16)
    return rows, swap_bit(rows, "grp", 0)


def segment_info(seq_lengths, rows_here):
    seq_ends = jnp.cumsum(seq_lengths)
    row_ids = jnp.arange(rows_here, dtype=jnp.int32)
    past_end = (row_ids[:, None] >= seq_ends[None, :]).astype(jnp.int32)
    segment = jnp.sum(past_end, axis=1)
    positions = row_ids - jnp.sum(past_end * seq_lengths[None, :], axis=1)
    member = (
        segment[:, None] == jnp.arange(seq_lengths.shape[0], dtype=jnp.int32)[None, :]
    ).astype(jnp.float32)
    same_seg = segment[:, None] == segment[None, :]
    return (positions, member, same_seg)


def rotary_tables(positions, head_dim):
    half_dim = head_dim // 2
    frequency = rotary_base ** (-2.0 * jnp.arange(half_dim, dtype=jnp.float32) / head_dim)
    angles = positions.astype(jnp.float32)[:, None] * frequency[None, :]
    return (jnp.cos(angles), jnp.sin(angles))


def rotate(values, cosine, sine_part):
    half_dim = values.shape[-1] // 2
    front_half = values[..., :half_dim]
    back_half = values[..., half_dim:]
    cos_wide = cosine[:, None, :]
    sin_wide = sine_part[:, None, :]
    return jnp.concatenate(
        [
            front_half * cos_wide - back_half * sin_wide,
            back_half * cos_wide + front_half * sin_wide,
        ],
        axis=-1,
    )


def rotate_back(values, cosine, sine_part):
    half_dim = values.shape[-1] // 2
    front_half = values[..., :half_dim]
    back_half = values[..., half_dim:]
    cos_wide = cosine[:, None, :]
    sin_wide = sine_part[:, None, :]
    return jnp.concatenate(
        [
            front_half * cos_wide + back_half * sin_wide,
            back_half * cos_wide - front_half * sin_wide,
        ],
        axis=-1,
    )


def normalize(values):
    centered = values - jnp.mean(values, axis=-1, keepdims=True)
    inv_std = lax.rsqrt(jnp.mean(centered * centered, axis=-1, keepdims=True) + norm_eps)
    return (centered * inv_std, inv_std)


def norm_back(grad, normed, inv_std, gain):
    scaled = grad * gain
    inner = inv_std * (
        scaled
        - jnp.mean(scaled, axis=-1, keepdims=True)
        - normed * jnp.mean(scaled * normed, axis=-1, keepdims=True)
    )
    return (inner, jnp.sum(grad * normed, axis=0), jnp.sum(grad, axis=0))


def score_block(query_rot, key_rot, same_seg):
    similarity_logits = jnp.einsum(
        "thd,shd->hts", query_rot, key_rot, preferred_element_type=jnp.float32
    ) * (1.0 / math.sqrt(HDIM))
    return jnp.where(same_seg[None], similarity_logits, masked_score)


def layer_forward(inputs, weight_set, rotary, same_seg, first_core):
    joint_w, output_w, gateup_w, down_w, norm_rows = weight_set
    rows_here = inputs.shape[0]
    gain_rows = norm_rows.astype(jnp.float32)
    inputs_low = inputs.astype(jnp.bfloat16)
    merged = in_order(
        jnp.dot(inputs_low, joint_w[0], preferred_element_type=jnp.float32),
        jnp.dot(inputs_low, joint_w[1], preferred_element_type=jnp.float32),
        first_core,
    )
    query_rot = rotate(merged[:, :D].reshape(rows_here, HEADS, HDIM), rotary[0], rotary[1]).astype(
        jnp.bfloat16
    )
    key_rot = rotate(
        merged[:, D : 2 * D].reshape(rows_here, HEADS, HDIM), rotary[0], rotary[1]
    ).astype(jnp.bfloat16)
    value_low = merged[:, 2 * D :].reshape(rows_here, HEADS, HDIM).astype(jnp.bfloat16)
    similarity_logits = score_block(query_rot, key_rot, same_seg)
    row_peak = jnp.max(similarity_logits, axis=-1, keepdims=True)
    exp_scores = jnp.exp(similarity_logits - row_peak)
    softmax_sum = jnp.sum(exp_scores, axis=-1, keepdims=True)
    weights_p = exp_scores / softmax_sum
    log_total = row_peak + jnp.log(softmax_sum)
    mixed = jnp.einsum(
        "hts,shd->thd",
        weights_p.astype(jnp.bfloat16),
        value_low,
        preferred_element_type=jnp.float32,
    )
    mixed = mixed.reshape(rows_here, D).astype(jnp.bfloat16)
    attended = jnp.dot(mixed, output_w, preferred_element_type=jnp.float32)
    first_normed, first_inv = normalize(inputs + attended)
    hidden = first_normed * gain_rows[0] + gain_rows[1]
    hidden_low = hidden.astype(jnp.bfloat16)
    own_part = jnp.dot(hidden_low, gateup_w[0], preferred_element_type=jnp.float32)
    far_part = jnp.dot(hidden_low, gateup_w[1], preferred_element_type=jnp.float32)
    gate_part = jnp.where(first_core, own_part, far_part)
    up_part = jnp.where(first_core, far_part, own_part)
    act_low = (jax.nn.silu(gate_part) * up_part).astype(jnp.bfloat16)
    branch = jnp.dot(act_low, down_w, preferred_element_type=jnp.float32)
    second_normed, second_inv = normalize(hidden + branch)
    result = second_normed * gain_rows[2] + gain_rows[3]
    kept = (
        inputs_low,
        query_rot,
        key_rot,
        value_low,
        log_total,
        mixed,
        first_normed,
        first_inv,
        hidden_low,
        own_part,
        far_part,
        act_low,
        second_normed,
        second_inv,
    )
    return (result, kept)


def layer_backward(grad_out, weight_set, kept, rotary, same_seg, first_core):
    joint_w, output_w, gateup_w, down_w, norm_rows = weight_set
    (
        inputs_low,
        query_rot,
        key_rot,
        value_low,
        log_total,
        mixed,
        first_normed,
        first_inv,
        hidden_low,
        own_part,
        far_part,
        act_low,
        second_normed,
        second_inv,
    ) = kept
    rows_here = inputs_low.shape[0]
    score_scale = 1.0 / math.sqrt(HDIM)
    gain_rows = norm_rows.astype(jnp.float32)
    second_in, gain_two, bias_two = norm_back(grad_out, second_normed, second_inv, gain_rows[2])
    branch_grad = second_in.astype(jnp.bfloat16)
    down_grad = tuple(
        jnp.einsum("tf,td->fd", act_low, part, preferred_element_type=jnp.float32)
        for part in own_and_far(branch_grad, first_core)
    )
    act_grad = jnp.einsum("td,fd->tf", branch_grad, down_w, preferred_element_type=jnp.float32)
    gate_part = jnp.where(first_core, own_part, far_part)
    up_part = jnp.where(first_core, far_part, own_part)
    sigmoid_g = jax.nn.sigmoid(gate_part)
    gate_grad = act_grad * up_part * sigmoid_g * (1.0 + gate_part * (1.0 - sigmoid_g))
    up_grad = act_grad * gate_part * sigmoid_g
    own_grad = jnp.where(first_core, gate_grad, up_grad).astype(jnp.bfloat16)
    far_grad = jnp.where(first_core, up_grad, gate_grad).astype(jnp.bfloat16)
    gateup_grad = tuple(
        jnp.einsum("td,tf->df", hidden_low, part, preferred_element_type=jnp.float32)
        for part in (own_grad, far_grad)
    )
    hidden_grad = (
        second_in
        + jnp.einsum("tf,df->td", own_grad, gateup_w[0], preferred_element_type=jnp.float32)
        + jnp.einsum("tf,df->td", far_grad, gateup_w[1], preferred_element_type=jnp.float32)
    )
    first_in, gain_one, bias_one = norm_back(hidden_grad, first_normed, first_inv, gain_rows[0])
    attended_grad = first_in.astype(jnp.bfloat16)
    output_grad = tuple(
        jnp.einsum("tc,td->cd", mixed, part, preferred_element_type=jnp.float32)
        for part in own_and_far(attended_grad, first_core)
    )
    mixed_grad = jnp.einsum(
        "td,cd->tc", attended_grad, output_w, preferred_element_type=jnp.float32
    )
    mixed_grad = mixed_grad.astype(jnp.bfloat16).reshape(rows_here, HEADS, HDIM)
    similarity_logits = score_block(query_rot, key_rot, same_seg)
    weights_p = jnp.exp(similarity_logits - log_total)
    prob_grad = jnp.einsum(
        "thd,shd->hts", mixed_grad, value_low, preferred_element_type=jnp.float32
    )
    center = jnp.sum(prob_grad * weights_p, axis=-1, keepdims=True)
    score_grad = (weights_p * (prob_grad - center)).astype(jnp.bfloat16)
    value_grad = jnp.einsum(
        "hts,thd->shd",
        weights_p.astype(jnp.bfloat16),
        mixed_grad,
        preferred_element_type=jnp.float32,
    )
    query_grad = (
        jnp.einsum("hts,shd->thd", score_grad, key_rot, preferred_element_type=jnp.float32)
        * score_scale
    )
    key_grad = (
        jnp.einsum("hts,thd->shd", score_grad, query_rot, preferred_element_type=jnp.float32)
        * score_scale
    )
    merged_grad = jnp.concatenate(
        [
            rotate_back(query_grad, rotary[0], rotary[1]).reshape(rows_here, D),
            rotate_back(key_grad, rotary[0], rotary[1]).reshape(rows_here, D),
            value_grad.reshape(rows_here, D),
        ],
        axis=1,
    ).astype(jnp.bfloat16)
    merged_own, merged_far = own_and_far(merged_grad, first_core)
    joint_grad = tuple(
        jnp.einsum("tc,tf->cf", inputs_low, part, preferred_element_type=jnp.float32)
        for part in (merged_own, merged_far)
    )
    input_grad = (
        first_in
        + jnp.einsum("tf,cf->tc", merged_own, joint_w[0], preferred_element_type=jnp.float32)
        + jnp.einsum("tf,cf->tc", merged_far, joint_w[1], preferred_element_type=jnp.float32)
    )
    norms_grad = jnp.stack([gain_one, bias_one, gain_two, bias_two])
    return (input_grad, (joint_grad, output_grad, gateup_grad, down_grad, norms_grad))


def adamw_update(grad, master, first, second, bias_first, bias_second, rate, decay):
    moment = beta_one * first + (1.0 - beta_one) * grad
    squared_values = beta_two * second + (1.0 - beta_two) * grad * grad
    newer = master - rate * (
        moment / bias_first / (jnp.sqrt(squared_values / bias_second) + adam_eps) + decay * master
    )
    return (newer, moment, squared_values, newer.astype(jnp.bfloat16))


def body(
    incoming_vectors,
    sequence_extents,
    matching_document_index,
    softmax_sharpness,
    optimizer_iteration_number,
    attention_entry_master,
    attention_entry_first_moment,
    attention_entry_second_moment,
    attention_exit_master,
    attention_exit_first_moment,
    attention_exit_second_moment,
    widening_projection_master,
    widening_first_moment,
    widening_second_moment,
    lowering_projection_master,
    lowering_first_moment,
    lowering_second_moment,
    layernorm_affine_master,
    layernorm_affine_first_moment,
    layernorm_affine_second_moment,
):
    core = lax.axis_index("grp") & 1
    first_core = core == 0
    norm_cube = cube_gather(layernorm_affine_master.astype(jnp.bfloat16), "dp", bit_order(0))
    norm_cube = norm_cube.reshape((-1,) + layernorm_affine_master.shape)
    norm_full = jnp.moveaxis(norm_cube, 0, 2).reshape(LAYERS, 4, D)
    full = []
    for layer_idx in range(LAYERS):
        joint_pair = gather_half(attention_entry_master[layer_idx], core, 1)
        output_pair = gather_half(attention_exit_master[layer_idx], core, 1)
        gateup_pair = gather_half(widening_projection_master[layer_idx], core, 0)
        down_pair = gather_half(lowering_projection_master[layer_idx], core, 1)
        full.append(
            (
                joint_pair,
                in_order(*output_pair, first_core),
                gateup_pair,
                in_order(*down_pair, first_core),
                norm_full[layer_idx],
            )
        )
    rows_here = incoming_vectors.shape[0]
    seqs_here = sequence_extents.shape[0]
    positions, member, same_seg = segment_info(sequence_extents, rows_here)
    rotary = rotary_tables(positions, HDIM)
    length_float = sequence_extents.astype(jnp.float32)[:, None]
    hidden_state = incoming_vectors.astype(jnp.float32)
    kept_list = []
    for layer_idx in range(LAYERS):
        layer_weights = full[layer_idx]
        hidden_state, kept = layer_forward(hidden_state, layer_weights, rotary, same_seg, first_core)
        kept_list.append(kept)
    hidden_out = hidden_state.astype(jnp.bfloat16)
    pooled = (
        jnp.einsum("ts,td->sd", member, hidden_state, precision=topmost_precision) / length_float
    )
    inv_norm = lax.rsqrt(jnp.sum(pooled * pooled, axis=-1, keepdims=True) + embed_eps)
    embed_low = (pooled * inv_norm).astype(jnp.bfloat16)
    every = cube_gather(embed_low, "dp", bit_order(0))
    every = cube_gather(every, "grp", list(range(axis_bits("grp") - 1, -1, -1)))
    every = every.reshape(-1, D)
    query_count = every.shape[0] // 2
    queries = every[:query_count]
    documents = every[query_count:]
    my_index = lax.axis_index("grp") * lax.axis_size("dp") + lax.axis_index("dp")
    is_query = lax.axis_index("grp") < lax.axis_size("grp") // 2
    logit_scale_factor = 1.0 / softmax_sharpness[0]
    similarity_logits = (
        jnp.einsum("qd,kd->qk", queries, documents, preferred_element_type=jnp.float32)
        * logit_scale_factor
    )
    target_rows = (
        jnp.arange(query_count, dtype=jnp.int32)[None, :] == matching_document_index[:, None]
    ).astype(jnp.float32)
    row_peak = jnp.max(similarity_logits, axis=-1, keepdims=True)
    exp_scores = jnp.exp(similarity_logits - row_peak)
    softmax_sum = jnp.sum(exp_scores, axis=-1, keepdims=True)
    row_loss = (
        row_peak[:, 0]
        + jnp.log(softmax_sum[:, 0])
        - jnp.sum(similarity_logits * target_rows, axis=-1)
    )
    loss_total = jnp.sum(row_loss) / query_count
    score_grad = (exp_scores / softmax_sum - target_rows) / query_count
    score_side = jnp.where(is_query, score_grad, score_grad.T)
    start_own = (my_index % (query_count // seqs_here)) * seqs_here
    score_own = lax.dynamic_slice_in_dim(score_side, start_own, seqs_here, axis=0)
    facing = jnp.where(is_query, documents, queries).astype(jnp.float32)
    embed_grad = (
        jnp.einsum("sk,kd->sd", score_own, facing, precision=topmost_precision)
        * logit_scale_factor
    )
    pooled_grad = inv_norm * embed_grad - pooled * inv_norm * inv_norm * inv_norm * jnp.sum(
        pooled * embed_grad, axis=-1, keepdims=True
    )
    state_grad = jnp.einsum(
        "ts,sd->td", member, pooled_grad / length_float, precision=topmost_precision
    )
    layer_grads = [None] * LAYERS
    for layer_idx in range(LAYERS - 1, -1, -1):
        layer_weights = full[layer_idx]
        state_grad, layer_grads[layer_idx] = layer_backward(
            state_grad, layer_weights, kept_list[layer_idx], rotary, same_seg, first_core
        )
    shards = []
    for kind, color in enumerate((1, 1, 0, 1)):
        rows = [
            in_order(*scatter_half(*layer_grads[layer_idx][kind], color), first_core)
            for layer_idx in range(LAYERS)
        ]
        shards.append(jnp.stack(rows).astype(jnp.float32))
    norm_grads = jnp.stack([layer_grads[layer_idx][4] for layer_idx in range(LAYERS)])
    dp_bits = bit_order(0)[::-1]
    norm_grads = jnp.moveaxis(norm_grads.reshape(LAYERS, 4, lax.axis_size("dp"), -1), 2, 0)
    norm_grads = norm_grads.reshape((2,) * len(dp_bits) + norm_grads.shape[1:])
    norm_grads = cube_scatter(norm_grads, "dp", dp_bits)
    for bit in range(axis_bits("grp")):
        norm_grads = norm_grads + swap_bit(norm_grads, "grp", bit)
    shards.append(norm_grads)
    step_float = optimizer_iteration_number[0].astype(jnp.float32)
    bias_first = 1.0 - jnp.power(beta_one, step_float)
    bias_second = 1.0 - jnp.power(beta_two, step_float)
    joint_weight, joint_moment, joint_square, joint_copy = adamw_update(
        shards[0],
        attention_entry_master,
        attention_entry_first_moment,
        attention_entry_second_moment,
        bias_first,
        bias_second,
        rate_matrix,
        decay_rate,
    )
    output_weight, output_moment, output_square, output_copy = adamw_update(
        shards[1],
        attention_exit_master,
        attention_exit_first_moment,
        attention_exit_second_moment,
        bias_first,
        bias_second,
        rate_matrix,
        decay_rate,
    )
    gateup_weight, gateup_moment, gateup_square, gateup_copy = adamw_update(
        shards[2],
        widening_projection_master,
        widening_first_moment,
        widening_second_moment,
        bias_first,
        bias_second,
        rate_matrix,
        decay_rate,
    )
    down_weight, down_moment, down_square, down_copy = adamw_update(
        shards[3],
        lowering_projection_master,
        lowering_first_moment,
        lowering_second_moment,
        bias_first,
        bias_second,
        rate_matrix,
        decay_rate,
    )
    norms_weight, norms_moment, norms_square, norms_copy = adamw_update(
        shards[4],
        layernorm_affine_master,
        layernorm_affine_first_moment,
        layernorm_affine_second_moment,
        bias_first,
        bias_second,
        rate_norms,
        0.0,
    )
    loss_value = jnp.reshape(loss_total, (1,))
    return (
        hidden_out,
        state_grad,
        loss_value,
        joint_weight,
        joint_moment,
        joint_square,
        joint_copy,
        output_weight,
        output_moment,
        output_square,
        output_copy,
        gateup_weight,
        gateup_moment,
        gateup_square,
        gateup_copy,
        down_weight,
        down_moment,
        down_square,
        down_copy,
        norms_weight,
        norms_moment,
        norms_square,
        norms_copy,
    )


def solution(mesh):
    return jax.shard_map(
        body,
        mesh=mesh,
        in_specs=(
            P(("grp", "dp"), None),
            P(("grp", "dp")),
            P(),
            P(),
            P(),
            P(None, "dp", None),
            P(None, "dp", None),
            P(None, "dp", None),
            P(None, "dp", None),
            P(None, "dp", None),
            P(None, "dp", None),
            P(None, "dp", None),
            P(None, "dp", None),
            P(None, "dp", None),
            P(None, "dp", None),
            P(None, "dp", None),
            P(None, "dp", None),
            P(None, None, "dp"),
            P(None, None, "dp"),
            P(None, None, "dp"),
        ),
        out_specs=(
            P(("grp", "dp"), None),
            P(("grp", "dp"), None),
            P(),
            P(None, "dp", None),
            P(None, "dp", None),
            P(None, "dp", None),
            P(None, "dp", None),
            P(None, "dp", None),
            P(None, "dp", None),
            P(None, "dp", None),
            P(None, "dp", None),
            P(None, "dp", None),
            P(None, "dp", None),
            P(None, "dp", None),
            P(None, "dp", None),
            P(None, "dp", None),
            P(None, "dp", None),
            P(None, "dp", None),
            P(None, "dp", None),
            P(None, None, "dp"),
            P(None, None, "dp"),
            P(None, None, "dp"),
            P(None, None, "dp"),
        ),
        check_vma=False,
    )
```

```python
import math

import jax
import jax.numpy as jnp
from jax import lax
from jax.sharding import PartitionSpec as P

D = 768
HEADS = 12
FF = 3072
HDIM = 64
LAYERS = 2


beta_one = 0.9
beta_two = 0.999
adam_eps = 1e-08
decay_rate = 0.01
rate_matrix = 0.08
rate_norms = 1.0
norm_eps = 1e-05
embed_eps = 1e-06
masked_score = -1000000000.0
rotary_base = 1000.0
topmost_precision = lax.Precision.HIGHEST


def axis_bits(axis):
    return lax.axis_size(axis).bit_length() - 1


def swap_bit(value, axis, bit):
    count = lax.axis_size(axis)
    return lax.ppermute(value, axis, [(i, i ^ (1 << bit)) for i in range(count)])


def my_bit(axis, bit):
    return (lax.axis_index(axis) >> bit) & 1


def cube_gather(piece, axis, bits):
    held = []
    for bit in bits:
        other = swap_bit(piece, axis, bit)
        place = sum(1 for b in held if b > bit)
        first = my_bit(axis, bit) == 0
        piece = jnp.stack(
            [jnp.where(first, piece, other), jnp.where(first, other, piece)], axis=place
        )
        held.append(bit)
    return piece


def bit_order(color):
    order = list(range(axis_bits("dp") - 1, -1, -1))
    if color and len(order) > 1:
        order[-1], order[-2] = order[-2], order[-1]
    return order


def core_half(value, core, axis):
    half = value.shape[axis] // 2
    return lax.dynamic_slice_in_dim(value, core * half, half, axis)


class Gather:
    def __init__(self, piece, color):
        self.piece = piece
        self.todo = bit_order(color)
        self.held = []
        self.moving = None
        self.far = None

    def start(self):
        if self.todo:
            self.moving = swap_bit(self.piece, "dp", self.todo[0])
        else:
            self.piece = self.piece.reshape(-1, self.piece.shape[-1])
            self.moving = swap_bit(self.piece, "grp", 0)

    def land(self):
        other, self.moving = self.moving, None
        if not self.todo:
            self.far = other
            return
        bit = self.todo.pop(0)
        place = sum(1 for b in self.held if b > bit)
        first = my_bit("dp", bit) == 0
        self.piece = jnp.stack(
            [jnp.where(first, self.piece, other), jnp.where(first, other, self.piece)], axis=place
        )
        self.held.append(bit)

    def complete(self):
        return self.far is not None


class Scatter:
    def __init__(self, mine, other, color):
        self.mine = mine
        self.piece = other
        self.todo = bit_order(color)[::-1]
        self.left = sorted(self.todo, reverse=True)
        self.rest = list(range(1, axis_bits("grp")))
        self.whole = None
        self.moving = None
        self.far = None

    def start(self):
        if self.whole is None:
            self.moving = swap_bit(self.piece, "grp", 0)
        elif self.todo:
            bit = self.todo[0]
            away = lax.dynamic_index_in_dim(
                self.whole, 1 - my_bit("dp", bit), self.left.index(bit), keepdims=False
            )
            self.moving = swap_bit(away, "dp", bit)
        elif self.rest:
            self.moving = swap_bit(self.whole, "grp", self.rest[0])
        else:
            self.moving = swap_bit(self.whole, "grp", 0)

    def land(self):
        other, self.moving = self.moving, None
        if self.whole is None:
            both = (self.mine + other.astype(jnp.float32)).astype(jnp.bfloat16)
            self.whole = both.reshape((2,) * len(self.left) + (-1, both.shape[1]))
        elif self.todo:
            bit = self.todo.pop(0)
            keep = lax.dynamic_index_in_dim(
                self.whole, my_bit("dp", bit), self.left.index(bit), keepdims=False
            )
            self.left.remove(bit)
            self.whole = (keep.astype(jnp.float32) + other.astype(jnp.float32)).astype(jnp.bfloat16)
        elif self.rest:
            self.rest.pop(0)
            self.whole = (
                self.whole.astype(jnp.float32) + other.astype(jnp.float32)
            ).astype(jnp.bfloat16)
        else:
            self.far = other

    def complete(self):
        return self.far is not None


def checkpoint(act, land=(), start=()):
    land = [move for move in land if move.moving is not None]
    start = list(start)
    if not land and not start:
        return act
    held = lax.optimization_barrier(
        (act, [move.moving for move in land], [move.piece for move in start])
    )
    act = held[0]
    for move, value in zip(land, held[1]):
        move.moving = value
        move.land()
    for move, value in zip(start, held[2]):
        move.piece = value
        move.start()
    for move in land:
        if not move.complete():
            move.start()
    return act


def finish(act, move):
    while not move.complete():
        act = checkpoint(act, [move])
    return act


def run_out(move):
    while not move.complete():
        move.land()
        if not move.complete():
            move.start()


def fold_rows(value, count):
    ratio = FF // D
    wide = value.reshape(-1, ratio, count, value.shape[1])
    return jnp.swapaxes(wide, 1, 2).reshape(-1, ratio * value.shape[1])


def unfold_rows(value, count):
    ratio = FF // D
    wide = value.reshape(-1, count, ratio, value.shape[1] // ratio)
    return jnp.swapaxes(wide, 1, 2).reshape(-1, value.shape[1] // ratio)


def in_order(mine, other, first):
    return jnp.concatenate(
        [jnp.where(first, mine, other), jnp.where(first, other, mine)], axis=1
    )


def own_and_far(value, first):
    half = value.shape[1] // 2
    low, high = value[:, :half], value[:, half:]
    return jnp.where(first, low, high), jnp.where(first, high, low)


def segment_info(seq_lengths, rows_here):
    seq_ends = jnp.cumsum(seq_lengths)
    row_ids = jnp.arange(rows_here, dtype=jnp.int32)
    past_end = (row_ids[:, None] >= seq_ends[None, :]).astype(jnp.int32)
    segment = jnp.sum(past_end, axis=1)
    positions = row_ids - jnp.sum(past_end * seq_lengths[None, :], axis=1)
    member = (
        segment[:, None] == jnp.arange(seq_lengths.shape[0], dtype=jnp.int32)[None, :]
    ).astype(jnp.float32)
    same_seg = segment[:, None] == segment[None, :]
    return (positions, member, same_seg)


def rotary_tables(positions, head_dim):
    half_dim = head_dim // 2
    frequency = rotary_base ** (-2.0 * jnp.arange(half_dim, dtype=jnp.float32) / head_dim)
    angles = positions.astype(jnp.float32)[:, None] * frequency[None, :]
    return (jnp.cos(angles), jnp.sin(angles))


def rotate(values, cosine, sine_part):
    half_dim = values.shape[-1] // 2
    front_half = values[..., :half_dim]
    back_half = values[..., half_dim:]
    cos_wide = cosine[:, None, :]
    sin_wide = sine_part[:, None, :]
    return jnp.concatenate(
        [
            front_half * cos_wide - back_half * sin_wide,
            back_half * cos_wide + front_half * sin_wide,
        ],
        axis=-1,
    )


def rotate_back(values, cosine, sine_part):
    half_dim = values.shape[-1] // 2
    front_half = values[..., :half_dim]
    back_half = values[..., half_dim:]
    cos_wide = cosine[:, None, :]
    sin_wide = sine_part[:, None, :]
    return jnp.concatenate(
        [
            front_half * cos_wide + back_half * sin_wide,
            back_half * cos_wide - front_half * sin_wide,
        ],
        axis=-1,
    )


def normalize(values):
    centered = values - jnp.mean(values, axis=-1, keepdims=True)
    inv_std = lax.rsqrt(jnp.mean(centered * centered, axis=-1, keepdims=True) + norm_eps)
    return (centered * inv_std, inv_std)


def norm_back(grad, normed, inv_std, gain):
    scaled = grad * gain
    inner = inv_std * (
        scaled
        - jnp.mean(scaled, axis=-1, keepdims=True)
        - normed * jnp.mean(scaled * normed, axis=-1, keepdims=True)
    )
    return (inner, jnp.sum(grad * normed, axis=0), jnp.sum(grad, axis=0))


def score_block(query_rot, key_rot, same_seg):
    similarity_logits = jnp.einsum(
        "thd,shd->hts", query_rot, key_rot, preferred_element_type=jnp.float32
    ) * (1.0 / math.sqrt(HDIM))
    return jnp.where(same_seg[None], similarity_logits, masked_score)


def layer_forward(inputs, weights, rotary, same_seg, first_core, hook):
    rows_here = inputs.shape[0]
    inputs = hook("joint", inputs)
    joint_w = weights["joint"]
    inputs_low = inputs.astype(jnp.bfloat16)
    merged = in_order(
        jnp.dot(inputs_low, joint_w[0], preferred_element_type=jnp.float32),
        jnp.dot(inputs_low, joint_w[1], preferred_element_type=jnp.float32),
        first_core,
    )
    query_rot = rotate(merged[:, :D].reshape(rows_here, HEADS, HDIM), rotary[0], rotary[1]).astype(
        jnp.bfloat16
    )
    key_rot = rotate(
        merged[:, D : 2 * D].reshape(rows_here, HEADS, HDIM), rotary[0], rotary[1]
    ).astype(jnp.bfloat16)
    value_low = merged[:, 2 * D :].reshape(rows_here, HEADS, HDIM).astype(jnp.bfloat16)
    query_rot, key_rot, value_low = hook("qkv", (query_rot, key_rot, value_low))
    similarity_logits = score_block(query_rot, key_rot, same_seg)
    row_peak = jnp.max(similarity_logits, axis=-1, keepdims=True)
    exp_scores = jnp.exp(similarity_logits - row_peak)
    softmax_sum = jnp.sum(exp_scores, axis=-1, keepdims=True)
    softmax_sum = hook("softmax", softmax_sum)
    weights_p = exp_scores / softmax_sum
    log_total = row_peak + jnp.log(softmax_sum)
    mixed = jnp.einsum(
        "hts,shd->thd",
        weights_p.astype(jnp.bfloat16),
        value_low,
        preferred_element_type=jnp.float32,
    )
    mixed = mixed.reshape(rows_here, D).astype(jnp.bfloat16)
    mixed = hook("mixed", mixed)
    output_w, gain_rows = weights["output"], weights["norms"]
    attended = jnp.dot(mixed, output_w, preferred_element_type=jnp.float32)
    first_normed, first_inv = normalize(inputs + attended)
    hidden = first_normed * gain_rows[0] + gain_rows[1]
    hidden = hook("gateup", hidden)
    hidden_low = hidden.astype(jnp.bfloat16)
    gateup_w = weights["gateup"]
    own_part = jnp.dot(hidden_low, gateup_w[0], preferred_element_type=jnp.float32)
    far_part = jnp.dot(hidden_low, gateup_w[1], preferred_element_type=jnp.float32)
    gate_part = jnp.where(first_core, own_part, far_part)
    up_part = jnp.where(first_core, far_part, own_part)
    act_low = (jax.nn.silu(gate_part) * up_part).astype(jnp.bfloat16)
    act_low = hook("down", act_low)
    branch = jnp.dot(act_low, weights["down"], preferred_element_type=jnp.float32)
    second_normed, second_inv = normalize(hidden + branch)
    result = second_normed * gain_rows[2] + gain_rows[3]
    kept = (
        inputs_low,
        query_rot,
        key_rot,
        value_low,
        log_total,
        mixed,
        first_normed,
        first_inv,
        hidden_low,
        own_part,
        far_part,
        act_low,
        second_normed,
        second_inv,
    )
    return (result, kept)


def layer_backward(grad_out, weights, kept, rotary, same_seg, first_core, hook):
    joint_w, output_w, gateup_w, down_w, gain_rows = (
        weights[name] for name in ("joint", "output", "gateup", "down", "norms")
    )
    (
        inputs_low,
        query_rot,
        key_rot,
        value_low,
        log_total,
        mixed,
        first_normed,
        first_inv,
        hidden_low,
        own_part,
        far_part,
        act_low,
        second_normed,
        second_inv,
    ) = kept
    rows_here = inputs_low.shape[0]
    score_scale = 1.0 / math.sqrt(HDIM)
    second_in, gain_two, bias_two = norm_back(grad_out, second_normed, second_inv, gain_rows[2])
    second_in = hook("second", second_in)
    branch_grad = second_in.astype(jnp.bfloat16)
    down_grad = tuple(
        jnp.einsum("tf,td->fd", act_low, part, preferred_element_type=jnp.float32)
        for part in own_and_far(branch_grad, first_core)
    )
    act_grad = jnp.einsum("td,fd->tf", branch_grad, down_w, preferred_element_type=jnp.float32)
    gate_part = jnp.where(first_core, own_part, far_part)
    up_part = jnp.where(first_core, far_part, own_part)
    sigmoid_g = jax.nn.sigmoid(gate_part)
    gate_grad = act_grad * up_part * sigmoid_g * (1.0 + gate_part * (1.0 - sigmoid_g))
    up_grad = act_grad * gate_part * sigmoid_g
    own_grad = jnp.where(first_core, gate_grad, up_grad).astype(jnp.bfloat16)
    far_grad = jnp.where(first_core, up_grad, gate_grad).astype(jnp.bfloat16)
    own_grad, far_grad = hook("act", (own_grad, far_grad))
    gateup_grad = tuple(
        jnp.einsum("td,tf->df", hidden_low, part, preferred_element_type=jnp.float32)
        for part in (own_grad, far_grad)
    )
    own_grad = hook("gateup", own_grad, gateup_grad, down_grad)
    hidden_grad = (
        second_in
        + jnp.einsum("tf,df->td", own_grad, gateup_w[0], preferred_element_type=jnp.float32)
        + jnp.einsum("tf,df->td", far_grad, gateup_w[1], preferred_element_type=jnp.float32)
    )
    first_in, gain_one, bias_one = norm_back(hidden_grad, first_normed, first_inv, gain_rows[0])
    first_in = hook("first", first_in)
    attended_grad = first_in.astype(jnp.bfloat16)
    output_grad = tuple(
        jnp.einsum("tc,td->cd", mixed, part, preferred_element_type=jnp.float32)
        for part in own_and_far(attended_grad, first_core)
    )
    mixed_grad = jnp.einsum(
        "td,cd->tc", attended_grad, output_w, preferred_element_type=jnp.float32
    )
    mixed_grad = mixed_grad.astype(jnp.bfloat16).reshape(rows_here, HEADS, HDIM)
    similarity_logits = score_block(query_rot, key_rot, same_seg)
    weights_p = jnp.exp(similarity_logits - log_total)
    prob_grad = jnp.einsum(
        "thd,shd->hts", mixed_grad, value_low, preferred_element_type=jnp.float32
    )
    center = jnp.sum(prob_grad * weights_p, axis=-1, keepdims=True)
    center = hook("center", center)
    score_grad = (weights_p * (prob_grad - center)).astype(jnp.bfloat16)
    value_grad = jnp.einsum(
        "hts,thd->shd",
        weights_p.astype(jnp.bfloat16),
        mixed_grad,
        preferred_element_type=jnp.float32,
    )
    query_grad = (
        jnp.einsum("hts,shd->thd", score_grad, key_rot, preferred_element_type=jnp.float32)
        * score_scale
    )
    key_grad = (
        jnp.einsum("hts,thd->shd", score_grad, query_rot, preferred_element_type=jnp.float32)
        * score_scale
    )
    merged_grad = jnp.concatenate(
        [
            rotate_back(query_grad, rotary[0], rotary[1]).reshape(rows_here, D),
            rotate_back(key_grad, rotary[0], rotary[1]).reshape(rows_here, D),
            value_grad.reshape(rows_here, D),
        ],
        axis=1,
    ).astype(jnp.bfloat16)
    merged_grad = hook("merged", merged_grad)
    merged_own, merged_far = own_and_far(merged_grad, first_core)
    joint_grad = tuple(
        jnp.einsum("tc,tf->cf", inputs_low, part, preferred_element_type=jnp.float32)
        for part in (merged_own, merged_far)
    )
    merged_own = hook("joint", merged_own, joint_grad, output_grad, down_grad)
    input_grad = (
        first_in
        + jnp.einsum("tf,cf->tc", merged_own, joint_w[0], preferred_element_type=jnp.float32)
        + jnp.einsum("tf,cf->tc", merged_far, joint_w[1], preferred_element_type=jnp.float32)
    )
    norms_grad = jnp.stack([gain_one, bias_one, gain_two, bias_two])
    return (input_grad, (joint_grad, output_grad, gateup_grad, down_grad, norms_grad))


def adamw_update(grad, master, first, second, bias_first, bias_second, rate, decay):
    moment = beta_one * first + (1.0 - beta_one) * grad
    squared_values = beta_two * second + (1.0 - beta_two) * grad * grad
    newer = master - rate * (
        moment / bias_first / (jnp.sqrt(squared_values / bias_second) + adam_eps) + decay * master
    )
    return (newer, moment, squared_values, newer.astype(jnp.bfloat16))


def body(
    incoming_vectors,
    sequence_extents,
    matching_document_index,
    softmax_sharpness,
    optimizer_iteration_number,
    attention_entry_master,
    attention_entry_first_moment,
    attention_entry_second_moment,
    attention_exit_master,
    attention_exit_first_moment,
    attention_exit_second_moment,
    widening_projection_master,
    widening_first_moment,
    widening_second_moment,
    lowering_projection_master,
    lowering_first_moment,
    lowering_second_moment,
    layernorm_affine_master,
    layernorm_affine_first_moment,
    layernorm_affine_second_moment,
):
    core = lax.axis_index("grp") & 1
    first_core = core == 0
    rows_shard = attention_entry_master.shape[1]
    halves = []
    for layer_idx in range(LAYERS):
        parts = {
            "joint": attention_entry_master[layer_idx],
            "output": attention_exit_master[layer_idx],
            "gateup": widening_projection_master[layer_idx],
            "down": lowering_projection_master[layer_idx],
        }
        parts = {k: core_half(v, core, 1).astype(jnp.bfloat16) for k, v in parts.items()}
        parts["down"] = fold_rows(parts["down"], rows_shard)
        halves.append(parts)
    norm_cols = layernorm_affine_master.reshape(LAYERS * 4, rows_shard).T.astype(jnp.bfloat16)
    norm_cols = jnp.pad(norm_cols, ((0, 0), (0, 128 - LAYERS * 4)))
    entry_zero = Gather(
        jnp.concatenate([halves[0]["joint"], halves[0]["output"], norm_cols], axis=1), 1
    )
    gateup_zero = Gather(halves[0]["gateup"], 1)
    down_zero = Gather(halves[0]["down"], 0)
    rest_one = Gather(
        jnp.concatenate([halves[1]["joint"], halves[1]["output"], halves[1]["down"]], axis=1), 1
    )
    gateup_one = Gather(halves[1]["gateup"], 0)
    half_joint = halves[0]["joint"].shape[1]
    half_output = halves[0]["output"].shape[1]
    weights = [{}, {}]

    def put_entry(layer_idx, move):
        pair = (move.piece, move.far)
        weights[layer_idx]["joint"] = tuple(part[:, :half_joint] for part in pair)
        weights[layer_idx]["output"] = in_order(
            *(part[:, half_joint : half_joint + half_output] for part in pair), first_core
        )

    def put_down(layer_idx, pair):
        pair = tuple(unfold_rows(part, rows_shard) for part in pair)
        weights[layer_idx]["down"] = in_order(*pair, first_core)

    def hook_zero(name, act):
        if name == "joint":
            act = checkpoint(act, start=[entry_zero])
            act = checkpoint(act, [entry_zero], [gateup_zero])
            act = checkpoint(act, [entry_zero])
            act = checkpoint(act, [entry_zero, gateup_zero], [down_zero])
            act = checkpoint(act, [entry_zero, gateup_zero, down_zero])
            act = finish(act, entry_zero)
            put_entry(0, entry_zero)
            norm_full = entry_zero.piece[:, half_joint + half_output :][:, : LAYERS * 4]
            norm_full = norm_full.T.reshape(LAYERS, 4, D).astype(jnp.float32)
            for layer_idx in range(LAYERS):
                weights[layer_idx]["norms"] = norm_full[layer_idx]
        elif name == "qkv":
            act = checkpoint(act, [down_zero], [rest_one])
        elif name == "softmax":
            act = checkpoint(act, [gateup_zero, down_zero, rest_one])
        elif name == "mixed":
            act = checkpoint(act, [rest_one], [gateup_one])
        elif name == "gateup":
            act = checkpoint(act, [down_zero])
            act = checkpoint(act, [gateup_zero, gateup_one])
            act = finish(act, gateup_zero)
            weights[0]["gateup"] = (gateup_zero.piece, gateup_zero.far)
        elif name == "down":
            act = finish(act, down_zero)
            put_down(0, (down_zero.piece, down_zero.far))
            act = checkpoint(act, [rest_one, gateup_one])
        return act

    def hook_one(name, act):
        if name == "joint":
            act = finish(act, rest_one)
            put_entry(1, rest_one)
            put_down(1, [v[:, half_joint + half_output :] for v in (rest_one.piece, rest_one.far)])
            act = checkpoint(act, [gateup_one])
        elif name == "mixed":
            act = checkpoint(act, [gateup_one])
        elif name == "gateup":
            act = finish(act, gateup_one)
            weights[1]["gateup"] = (gateup_one.piece, gateup_one.far)
        return act

    rows_here = incoming_vectors.shape[0]
    seqs_here = sequence_extents.shape[0]
    positions, member, same_seg = segment_info(sequence_extents, rows_here)
    rotary = rotary_tables(positions, HDIM)
    length_float = sequence_extents.astype(jnp.float32)[:, None]
    hidden_state = incoming_vectors.astype(jnp.float32)
    kept_list = []
    for layer_idx in range(LAYERS):
        hidden_state, kept = layer_forward(
            hidden_state,
            weights[layer_idx],
            rotary,
            same_seg,
            first_core,
            (hook_zero, hook_one)[layer_idx],
        )
        kept_list.append(kept)
    hidden_out = hidden_state.astype(jnp.bfloat16)
    pooled = (
        jnp.einsum("ts,td->sd", member, hidden_state, precision=topmost_precision) / length_float
    )
    inv_norm = lax.rsqrt(jnp.sum(pooled * pooled, axis=-1, keepdims=True) + embed_eps)
    embed_low = (pooled * inv_norm).astype(jnp.bfloat16)
    every = cube_gather(embed_low, "dp", bit_order(0))
    every = cube_gather(every, "grp", list(range(axis_bits("grp") - 1, -1, -1)))
    every = every.reshape(-1, D)
    query_count = every.shape[0] // 2
    queries = every[:query_count]
    documents = every[query_count:]
    my_index = lax.axis_index("grp") * lax.axis_size("dp") + lax.axis_index("dp")
    is_query = lax.axis_index("grp") < lax.axis_size("grp") // 2
    logit_scale_factor = 1.0 / softmax_sharpness[0]
    similarity_logits = (
        jnp.einsum("qd,kd->qk", queries, documents, preferred_element_type=jnp.float32)
        * logit_scale_factor
    )
    target_rows = (
        jnp.arange(query_count, dtype=jnp.int32)[None, :] == matching_document_index[:, None]
    ).astype(jnp.float32)
    row_peak = jnp.max(similarity_logits, axis=-1, keepdims=True)
    exp_scores = jnp.exp(similarity_logits - row_peak)
    softmax_sum = jnp.sum(exp_scores, axis=-1, keepdims=True)
    row_loss = (
        row_peak[:, 0]
        + jnp.log(softmax_sum[:, 0])
        - jnp.sum(similarity_logits * target_rows, axis=-1)
    )
    loss_total = jnp.sum(row_loss) / query_count
    score_grad = (exp_scores / softmax_sum - target_rows) / query_count
    score_side = jnp.where(is_query, score_grad, score_grad.T)
    start_own = (my_index % (query_count // seqs_here)) * seqs_here
    score_own = lax.dynamic_slice_in_dim(score_side, start_own, seqs_here, axis=0)
    facing = jnp.where(is_query, documents, queries).astype(jnp.float32)
    embed_grad = (
        jnp.einsum("sk,kd->sd", score_own, facing, precision=topmost_precision)
        * logit_scale_factor
    )
    pooled_grad = inv_norm * embed_grad - pooled * inv_norm * inv_norm * inv_norm * jnp.sum(
        pooled * embed_grad, axis=-1, keepdims=True
    )
    state_grad = jnp.einsum(
        "ts,sd->td", member, pooled_grad / length_float, precision=topmost_precision
    )
    sums = [{}, {}]

    def pair_of(columns):
        own = jnp.concatenate([pair[0] for pair in columns], axis=1)
        far = jnp.concatenate([pair[1].astype(jnp.bfloat16) for pair in columns], axis=1)
        return own, far

    def folded(pair):
        return tuple(fold_rows(part, rows_shard) for part in pair)

    def sum_gateup(layer_idx, pair, color):
        sums[layer_idx]["gateup"] = Scatter(pair[0], pair[1].astype(jnp.bfloat16), color)
        return sums[layer_idx]["gateup"]

    def back_one(name, act, *grads):
        moves = sums[1]
        if name == "gateup":
            act = checkpoint(act, start=[sum_gateup(1, grads[0], 0)])
        elif name == "first":
            act = checkpoint(act, [moves["gateup"]])
        elif name == "merged":
            act = checkpoint(act, [moves["gateup"]])
        elif name == "joint":
            columns = [grads[0], grads[1], folded(grads[2])]
            moves["rest"] = Scatter(*pair_of(columns), 1)
            act = checkpoint(act, start=[moves["rest"]])
        return act

    def back_zero(name, act, *grads):
        early, moves = sums[1], sums[0]
        if name == "second":
            act = checkpoint(act, [early["rest"], early["gateup"]])
        elif name == "act":
            act = checkpoint(act, [early["gateup"]])
        elif name == "gateup":
            moves["down"] = Scatter(*pair_of([folded(grads[1])]), 1)
            act = checkpoint(
                act, [early["gateup"]], [sum_gateup(0, grads[0], 0), moves["down"]]
            )
        elif name == "first":
            act = checkpoint(
                act, [early["rest"], early["gateup"], moves["gateup"], moves["down"]]
            )
        elif name == "center":
            act = checkpoint(act, [early["rest"], moves["down"]])
        elif name == "merged":
            act = checkpoint(act, [early["rest"], moves["gateup"], moves["down"]])
        return act

    state_grad, last_grads = layer_backward(
        state_grad, weights[1], kept_list[1], rotary, same_seg, first_core, back_one
    )
    state_grad, first_grads = layer_backward(
        state_grad, weights[0], kept_list[0], rotary, same_seg, first_core, back_zero
    )
    norm_grads = jnp.stack([first_grads[4], last_grads[4]]).reshape(LAYERS * 4, D).T
    norm_grads = jnp.pad(norm_grads, ((0, 0), (0, 128 - LAYERS * 4)))
    tail = Scatter(*pair_of([first_grads[0], first_grads[1], (norm_grads, norm_grads)]), 0)
    tail.start()
    for move in (tail, sums[0]["gateup"], sums[0]["down"], sums[1]["rest"], sums[1]["gateup"]):
        run_out(move)

    def columns_of(move, start, stop):
        return in_order(move.whole[:, start:stop], move.far[:, start:stop], first_core)

    half_entry = half_joint + half_output
    rest = sums[1]["rest"]

    def down_of(move, start):
        pair = tuple(unfold_rows(v[:, start:], rows_shard) for v in (move.whole, move.far))
        return in_order(*pair, first_core)

    rows = (
        (columns_of(tail, 0, half_joint), columns_of(rest, 0, half_joint)),
        (columns_of(tail, half_joint, half_entry), columns_of(rest, half_joint, half_entry)),
        tuple(columns_of(sums[i]["gateup"], 0, None) for i in range(LAYERS)),
        (down_of(sums[0]["down"], 0), down_of(rest, half_entry)),
    )
    shards = [jnp.stack(pair).astype(jnp.float32) for pair in rows]
    norm_shard = tail.whole[:, half_entry:][:, : LAYERS * 4].astype(jnp.float32)
    shards.append(norm_shard.T.reshape(LAYERS, 4, -1))
    step_float = optimizer_iteration_number[0].astype(jnp.float32)
    bias_first = 1.0 - jnp.power(beta_one, step_float)
    bias_second = 1.0 - jnp.power(beta_two, step_float)
    joint_weight, joint_moment, joint_square, joint_copy = adamw_update(
        shards[0],
        attention_entry_master,
        attention_entry_first_moment,
        attention_entry_second_moment,
        bias_first,
        bias_second,
        rate_matrix,
        decay_rate,
    )
    output_weight, output_moment, output_square, output_copy = adamw_update(
        shards[1],
        attention_exit_master,
        attention_exit_first_moment,
        attention_exit_second_moment,
        bias_first,
        bias_second,
        rate_matrix,
        decay_rate,
    )
    gateup_weight, gateup_moment, gateup_square, gateup_copy = adamw_update(
        shards[2],
        widening_projection_master,
        widening_first_moment,
        widening_second_moment,
        bias_first,
        bias_second,
        rate_matrix,
        decay_rate,
    )
    down_weight, down_moment, down_square, down_copy = adamw_update(
        shards[3],
        lowering_projection_master,
        lowering_first_moment,
        lowering_second_moment,
        bias_first,
        bias_second,
        rate_matrix,
        decay_rate,
    )
    norms_weight, norms_moment, norms_square, norms_copy = adamw_update(
        shards[4],
        layernorm_affine_master,
        layernorm_affine_first_moment,
        layernorm_affine_second_moment,
        bias_first,
        bias_second,
        rate_norms,
        0.0,
    )
    loss_value = jnp.reshape(loss_total, (1,))
    return (
        hidden_out,
        state_grad,
        loss_value,
        joint_weight,
        joint_moment,
        joint_square,
        joint_copy,
        output_weight,
        output_moment,
        output_square,
        output_copy,
        gateup_weight,
        gateup_moment,
        gateup_square,
        gateup_copy,
        down_weight,
        down_moment,
        down_square,
        down_copy,
        norms_weight,
        norms_moment,
        norms_square,
        norms_copy,
    )


def solution(mesh):
    return jax.shard_map(
        body,
        mesh=mesh,
        in_specs=(
            P(("grp", "dp"), None),
            P(("grp", "dp")),
            P(),
            P(),
            P(),
            P(None, "dp", None),
            P(None, "dp", None),
            P(None, "dp", None),
            P(None, "dp", None),
            P(None, "dp", None),
            P(None, "dp", None),
            P(None, "dp", None),
            P(None, "dp", None),
            P(None, "dp", None),
            P(None, "dp", None),
            P(None, "dp", None),
            P(None, "dp", None),
            P(None, None, "dp"),
            P(None, None, "dp"),
            P(None, None, "dp"),
        ),
        out_specs=(
            P(("grp", "dp"), None),
            P(("grp", "dp"), None),
            P(),
            P(None, "dp", None),
            P(None, "dp", None),
            P(None, "dp", None),
            P(None, "dp", None),
            P(None, "dp", None),
            P(None, "dp", None),
            P(None, "dp", None),
            P(None, "dp", None),
            P(None, "dp", None),
            P(None, "dp", None),
            P(None, "dp", None),
            P(None, "dp", None),
            P(None, "dp", None),
            P(None, "dp", None),
            P(None, "dp", None),
            P(None, "dp", None),
            P(None, None, "dp"),
            P(None, None, "dp"),
            P(None, None, "dp"),
            P(None, None, "dp"),
        ),
        check_vma=False,
    )
```

```python
import math

import jax
import jax.numpy as jnp
from jax import lax
from jax.sharding import PartitionSpec as P

D = 768
HEADS = 12
FF = 3072
HDIM = 64
LAYERS = 2


beta_one = 0.9
beta_two = 0.999
adam_eps = 1e-08
decay_rate = 0.01
rate_matrix = 0.08
rate_norms = 1.0
norm_eps = 1e-05
embed_eps = 1e-06
masked_score = -1000000000.0
rotary_base = 1000.0
topmost_precision = lax.Precision.HIGHEST


def axis_bits(axis):
    return lax.axis_size(axis).bit_length() - 1


def swap_bit(value, axis, bit):
    count = lax.axis_size(axis)
    return lax.ppermute(value, axis, [(i, i ^ (1 << bit)) for i in range(count)])


def my_bit(axis, bit):
    return (lax.axis_index(axis) >> bit) & 1


def cube_gather(piece, axis, bits):
    held = []
    for bit in bits:
        other = swap_bit(piece, axis, bit)
        place = sum(1 for b in held if b > bit)
        first = my_bit(axis, bit) == 0
        piece = jnp.stack(
            [jnp.where(first, piece, other), jnp.where(first, other, piece)], axis=place
        )
        held.append(bit)
    return piece


def bit_order(color):
    order = list(range(axis_bits("dp") - 1, -1, -1))
    if color and len(order) > 1:
        order[-1], order[-2] = order[-2], order[-1]
    return order


def core_half(value, core, axis):
    half = value.shape[axis] // 2
    return lax.dynamic_slice_in_dim(value, core * half, half, axis)


def lane_cut(width):
    return width // 256 * 128


def columns_between(lanes, start, stop):
    cut = lanes[0].shape[-1]
    held = []
    if start < cut:
        held.append(lanes[0][..., start : min(stop, cut)])
    if stop > cut:
        held.append(lanes[1][..., max(start - cut, 0) : stop - cut])
    return held[0] if len(held) == 1 else jnp.concatenate(held, axis=-1)


class Gather:
    def __init__(self, parts):
        self.widths = [part.shape[1] for part in parts]
        whole = jnp.concatenate(parts, axis=1)
        cut = lane_cut(whole.shape[1])
        self.piece = [whole[:, :cut], whole[:, cut:]]
        self.todo = [bit_order(0), bit_order(1)]
        self.held = [[], []]
        self.moving = None
        self.far = None

    def start(self):
        if self.todo[0]:
            self.moving = [
                swap_bit(lane, "dp", todo[0]) for lane, todo in zip(self.piece, self.todo)
            ]
        else:
            self.moving = [swap_bit(part, "grp", 0) for part in self.piece]

    def land(self):
        arrived, self.moving = self.moving, None
        if not self.todo[0]:
            self.far = arrived
            return
        for k in range(2):
            bit = self.todo[k].pop(0)
            place = sum(1 for b in self.held[k] if b > bit)
            first = my_bit("dp", bit) == 0
            here, other = self.piece[k], arrived[k]
            self.piece[k] = jnp.stack(
                [jnp.where(first, here, other), jnp.where(first, other, here)], axis=place
            )
            self.held[k].append(bit)
        if not self.todo[0]:
            lanes = [lane.reshape(-1, lane.shape[-1]) for lane in self.piece]
            self.piece = []
            start = 0
            for width in self.widths:
                self.piece.append(columns_between(lanes, start, start + width))
                start += width

    def complete(self):
        return self.far is not None

    def pair(self, index):
        return self.piece[index], self.far[index]


class Scatter:
    def __init__(self, pairs):
        self.mine = [pair[0] for pair in pairs]
        self.piece = [pair[1].astype(jnp.bfloat16) for pair in pairs]
        self.todo = [bit_order(0)[::-1], bit_order(1)[::-1]]
        self.left = [sorted(todo, reverse=True) for todo in self.todo]
        self.rest = list(range(1, axis_bits("grp")))
        self.whole = None
        self.rows = None
        self.moving = None
        self.far = None

    def start(self):
        if self.whole is None:
            self.moving = [swap_bit(part, "grp", 0) for part in self.piece]
        elif self.todo[0]:
            self.moving = []
            for lane, todo, left in zip(self.whole, self.todo, self.left):
                away = lax.dynamic_index_in_dim(
                    lane, 1 - my_bit("dp", todo[0]), left.index(todo[0]), keepdims=False
                )
                self.moving.append(swap_bit(away, "dp", todo[0]))
        elif self.rest:
            self.moving = [swap_bit(self.rows, "grp", self.rest[0])]
        else:
            self.moving = [swap_bit(self.rows, "grp", 0)]

    def land(self):
        arrived, self.moving = self.moving, None
        if self.whole is None:
            both = [
                (mine + other.astype(jnp.float32)).astype(jnp.bfloat16)
                for mine, other in zip(self.mine, arrived)
            ]
            both = [part.reshape((2,) * len(self.left[0]) + (-1, part.shape[1])) for part in both]
            width = sum(part.shape[-1] for part in both)
            cut = lane_cut(width)
            if len(both) == 1:
                self.whole = [both[0][..., :cut], both[0][..., cut:]]
            else:
                tail = jnp.concatenate([both[0][..., cut:]] + both[1:], axis=-1)
                self.whole = [both[0][..., :cut], tail]
        elif self.todo[0]:
            for k in range(2):
                bit = self.todo[k].pop(0)
                keep = lax.dynamic_index_in_dim(
                    self.whole[k], my_bit("dp", bit), self.left[k].index(bit), keepdims=False
                )
                self.left[k].remove(bit)
                self.whole[k] = (
                    keep.astype(jnp.float32) + arrived[k].astype(jnp.float32)
                ).astype(jnp.bfloat16)
            if not self.todo[0]:
                self.rows = jnp.concatenate(self.whole, axis=-1)
        elif self.rest:
            self.rest.pop(0)
            self.rows = (
                self.rows.astype(jnp.float32) + arrived[0].astype(jnp.float32)
            ).astype(jnp.bfloat16)
        else:
            self.far = arrived[0]

    def complete(self):
        return self.far is not None


def checkpoint(act, land=(), start=()):
    land = [move for move in land if move.moving is not None]
    start = list(start)
    if not land and not start:
        return act
    held = lax.optimization_barrier(
        (act, [move.moving for move in land], [move.piece for move in start])
    )
    act = held[0]
    for move, value in zip(land, held[1]):
        move.moving = value
        move.land()
    for move, value in zip(start, held[2]):
        move.piece = value
        move.start()
    for move in land:
        if not move.complete():
            move.start()
    return act


def finish(act, move):
    while not move.complete():
        act = checkpoint(act, [move])
    return act


def run_out(move):
    while not move.complete():
        move.land()
        if not move.complete():
            move.start()


def fold_rows(value, count):
    ratio = FF // D
    wide = value.reshape(-1, ratio, count, value.shape[1])
    return jnp.swapaxes(wide, 1, 2).reshape(-1, ratio * value.shape[1])


def unfold_rows(value, count):
    ratio = FF // D
    wide = value.reshape(-1, count, ratio, value.shape[1] // ratio)
    return jnp.swapaxes(wide, 1, 2).reshape(-1, value.shape[1] // ratio)


def in_order(mine, other, first):
    return jnp.concatenate(
        [jnp.where(first, mine, other), jnp.where(first, other, mine)], axis=1
    )


def own_and_far(value, first):
    half = value.shape[1] // 2
    low, high = value[:, :half], value[:, half:]
    return jnp.where(first, low, high), jnp.where(first, high, low)


def segment_info(seq_lengths, rows_here):
    seq_ends = jnp.cumsum(seq_lengths)
    row_ids = jnp.arange(rows_here, dtype=jnp.int32)
    past_end = (row_ids[:, None] >= seq_ends[None, :]).astype(jnp.int32)
    segment = jnp.sum(past_end, axis=1)
    positions = row_ids - jnp.sum(past_end * seq_lengths[None, :], axis=1)
    member = (
        segment[:, None] == jnp.arange(seq_lengths.shape[0], dtype=jnp.int32)[None, :]
    ).astype(jnp.float32)
    same_seg = segment[:, None] == segment[None, :]
    return (positions, member, same_seg)


def rotary_tables(positions, head_dim):
    half_dim = head_dim // 2
    frequency = rotary_base ** (-2.0 * jnp.arange(half_dim, dtype=jnp.float32) / head_dim)
    angles = positions.astype(jnp.float32)[:, None] * frequency[None, :]
    return (jnp.cos(angles), jnp.sin(angles))


def rotate(values, cosine, sine_part):
    half_dim = values.shape[-1] // 2
    front_half = values[..., :half_dim]
    back_half = values[..., half_dim:]
    cos_wide = cosine[:, None, :]
    sin_wide = sine_part[:, None, :]
    return jnp.concatenate(
        [
            front_half * cos_wide - back_half * sin_wide,
            back_half * cos_wide + front_half * sin_wide,
        ],
        axis=-1,
    )


def rotate_back(values, cosine, sine_part):
    half_dim = values.shape[-1] // 2
    front_half = values[..., :half_dim]
    back_half = values[..., half_dim:]
    cos_wide = cosine[:, None, :]
    sin_wide = sine_part[:, None, :]
    return jnp.concatenate(
        [
            front_half * cos_wide + back_half * sin_wide,
            back_half * cos_wide - front_half * sin_wide,
        ],
        axis=-1,
    )


def normalize(values):
    centered = values - jnp.mean(values, axis=-1, keepdims=True)
    inv_std = lax.rsqrt(jnp.mean(centered * centered, axis=-1, keepdims=True) + norm_eps)
    return (centered * inv_std, inv_std)


def norm_back(grad, normed, inv_std, gain):
    scaled = grad * gain
    inner = inv_std * (
        scaled
        - jnp.mean(scaled, axis=-1, keepdims=True)
        - normed * jnp.mean(scaled * normed, axis=-1, keepdims=True)
    )
    return (inner, jnp.sum(grad * normed, axis=0), jnp.sum(grad, axis=0))


def score_block(query_rot, key_rot, same_seg):
    similarity_logits = jnp.einsum(
        "thd,shd->hts", query_rot, key_rot, preferred_element_type=jnp.float32
    ) * (1.0 / math.sqrt(HDIM))
    return jnp.where(same_seg[None], similarity_logits, masked_score)


def layer_forward(inputs, weights, rotary, same_seg, first_core, hook):
    rows_here = inputs.shape[0]
    inputs = hook("joint", inputs)
    joint_w = weights["joint"]
    inputs_low = inputs.astype(jnp.bfloat16)
    merged = in_order(
        jnp.dot(inputs_low, joint_w[0], preferred_element_type=jnp.float32),
        jnp.dot(inputs_low, joint_w[1], preferred_element_type=jnp.float32),
        first_core,
    )
    query_rot = rotate(merged[:, :D].reshape(rows_here, HEADS, HDIM), rotary[0], rotary[1]).astype(
        jnp.bfloat16
    )
    key_rot = rotate(
        merged[:, D : 2 * D].reshape(rows_here, HEADS, HDIM), rotary[0], rotary[1]
    ).astype(jnp.bfloat16)
    value_low = merged[:, 2 * D :].reshape(rows_here, HEADS, HDIM).astype(jnp.bfloat16)
    query_rot, key_rot, value_low = hook("qkv", (query_rot, key_rot, value_low))
    similarity_logits = score_block(query_rot, key_rot, same_seg)
    row_peak = jnp.max(similarity_logits, axis=-1, keepdims=True)
    exp_scores = jnp.exp(similarity_logits - row_peak)
    softmax_sum = jnp.sum(exp_scores, axis=-1, keepdims=True)
    softmax_sum = hook("softmax", softmax_sum)
    weights_p = exp_scores / softmax_sum
    log_total = row_peak + jnp.log(softmax_sum)
    mixed = jnp.einsum(
        "hts,shd->thd",
        weights_p.astype(jnp.bfloat16),
        value_low,
        preferred_element_type=jnp.float32,
    )
    mixed = mixed.reshape(rows_here, D).astype(jnp.bfloat16)
    mixed = hook("mixed", mixed)
    output_w, gain_rows = weights["output"], weights["norms"]
    attended = jnp.dot(mixed, output_w, preferred_element_type=jnp.float32)
    first_normed, first_inv = normalize(inputs + attended)
    hidden = first_normed * gain_rows[0] + gain_rows[1]
    hidden = hook("gateup", hidden)
    hidden_low = hidden.astype(jnp.bfloat16)
    gateup_w = weights["gateup"]
    own_part = jnp.dot(hidden_low, gateup_w[0], preferred_element_type=jnp.float32)
    far_part = jnp.dot(hidden_low, gateup_w[1], preferred_element_type=jnp.float32)
    gate_part = jnp.where(first_core, own_part, far_part)
    up_part = jnp.where(first_core, far_part, own_part)
    act_low = (jax.nn.silu(gate_part) * up_part).astype(jnp.bfloat16)
    act_low = hook("down", act_low)
    branch = jnp.dot(act_low, weights["down"], preferred_element_type=jnp.float32)
    second_normed, second_inv = normalize(hidden + branch)
    result = second_normed * gain_rows[2] + gain_rows[3]
    kept = (
        inputs_low,
        query_rot,
        key_rot,
        value_low,
        log_total,
        mixed,
        first_normed,
        first_inv,
        hidden_low,
        own_part,
        far_part,
        act_low,
        second_normed,
        second_inv,
    )
    return (result, kept)


def layer_backward(grad_out, weights, kept, rotary, same_seg, first_core, hook):
    joint_w, output_w, gateup_w, down_w, gain_rows = (
        weights[name] for name in ("joint", "output", "gateup", "down", "norms")
    )
    (
        inputs_low,
        query_rot,
        key_rot,
        value_low,
        log_total,
        mixed,
        first_normed,
        first_inv,
        hidden_low,
        own_part,
        far_part,
        act_low,
        second_normed,
        second_inv,
    ) = kept
    rows_here = inputs_low.shape[0]
    score_scale = 1.0 / math.sqrt(HDIM)
    second_in, gain_two, bias_two = norm_back(grad_out, second_normed, second_inv, gain_rows[2])
    second_in = hook("second", second_in)
    branch_grad = second_in.astype(jnp.bfloat16)
    down_grad = tuple(
        jnp.einsum("tf,td->fd", act_low, part, preferred_element_type=jnp.float32)
        for part in own_and_far(branch_grad, first_core)
    )
    act_grad = jnp.einsum("td,fd->tf", branch_grad, down_w, preferred_element_type=jnp.float32)
    gate_part = jnp.where(first_core, own_part, far_part)
    up_part = jnp.where(first_core, far_part, own_part)
    sigmoid_g = jax.nn.sigmoid(gate_part)
    gate_grad = act_grad * up_part * sigmoid_g * (1.0 + gate_part * (1.0 - sigmoid_g))
    up_grad = act_grad * gate_part * sigmoid_g
    own_grad = jnp.where(first_core, gate_grad, up_grad).astype(jnp.bfloat16)
    far_grad = jnp.where(first_core, up_grad, gate_grad).astype(jnp.bfloat16)
    own_grad, far_grad = hook("act", (own_grad, far_grad))
    gateup_grad = tuple(
        jnp.einsum("td,tf->df", hidden_low, part, preferred_element_type=jnp.float32)
        for part in (own_grad, far_grad)
    )
    own_grad = hook("gateup", own_grad, gateup_grad, down_grad)
    hidden_grad = (
        second_in
        + jnp.einsum("tf,df->td", own_grad, gateup_w[0], preferred_element_type=jnp.float32)
        + jnp.einsum("tf,df->td", far_grad, gateup_w[1], preferred_element_type=jnp.float32)
    )
    first_in, gain_one, bias_one = norm_back(hidden_grad, first_normed, first_inv, gain_rows[0])
    first_in = hook("first", first_in)
    attended_grad = first_in.astype(jnp.bfloat16)
    output_grad = tuple(
        jnp.einsum("tc,td->cd", mixed, part, preferred_element_type=jnp.float32)
        for part in own_and_far(attended_grad, first_core)
    )
    mixed_grad = jnp.einsum(
        "td,cd->tc", attended_grad, output_w, preferred_element_type=jnp.float32
    )
    mixed_grad = mixed_grad.astype(jnp.bfloat16).reshape(rows_here, HEADS, HDIM)
    similarity_logits = score_block(query_rot, key_rot, same_seg)
    weights_p = jnp.exp(similarity_logits - log_total)
    prob_grad = jnp.einsum(
        "thd,shd->hts", mixed_grad, value_low, preferred_element_type=jnp.float32
    )
    center = jnp.sum(prob_grad * weights_p, axis=-1, keepdims=True)
    center = hook("center", center)
    score_grad = (weights_p * (prob_grad - center)).astype(jnp.bfloat16)
    value_grad = jnp.einsum(
        "hts,thd->shd",
        weights_p.astype(jnp.bfloat16),
        mixed_grad,
        preferred_element_type=jnp.float32,
    )
    query_grad = (
        jnp.einsum("hts,shd->thd", score_grad, key_rot, preferred_element_type=jnp.float32)
        * score_scale
    )
    key_grad = (
        jnp.einsum("hts,thd->shd", score_grad, query_rot, preferred_element_type=jnp.float32)
        * score_scale
    )
    merged_grad = jnp.concatenate(
        [
            rotate_back(query_grad, rotary[0], rotary[1]).reshape(rows_here, D),
            rotate_back(key_grad, rotary[0], rotary[1]).reshape(rows_here, D),
            value_grad.reshape(rows_here, D),
        ],
        axis=1,
    ).astype(jnp.bfloat16)
    merged_grad = hook("merged", merged_grad)
    merged_own, merged_far = own_and_far(merged_grad, first_core)
    joint_grad = tuple(
        jnp.einsum("tc,tf->cf", inputs_low, part, preferred_element_type=jnp.float32)
        for part in (merged_own, merged_far)
    )
    merged_own = hook("joint", merged_own, joint_grad, output_grad)
    input_grad = (
        first_in
        + jnp.einsum("tf,cf->tc", merged_own, joint_w[0], preferred_element_type=jnp.float32)
        + jnp.einsum("tf,cf->tc", merged_far, joint_w[1], preferred_element_type=jnp.float32)
    )
    norms_grad = jnp.stack([gain_one, bias_one, gain_two, bias_two])
    return (input_grad, (joint_grad, output_grad, gateup_grad, down_grad, norms_grad))


def adamw_update(grad, master, first, second, bias_first, bias_second, rate, decay):
    moment = beta_one * first + (1.0 - beta_one) * grad
    squared_values = beta_two * second + (1.0 - beta_two) * grad * grad
    newer = master - rate * (
        moment / bias_first / (jnp.sqrt(squared_values / bias_second) + adam_eps) + decay * master
    )
    return (newer, moment, squared_values, newer.astype(jnp.bfloat16))


def body(
    incoming_vectors,
    sequence_extents,
    matching_document_index,
    softmax_sharpness,
    optimizer_iteration_number,
    attention_entry_master,
    attention_entry_first_moment,
    attention_entry_second_moment,
    attention_exit_master,
    attention_exit_first_moment,
    attention_exit_second_moment,
    widening_projection_master,
    widening_first_moment,
    widening_second_moment,
    lowering_projection_master,
    lowering_first_moment,
    lowering_second_moment,
    layernorm_affine_master,
    layernorm_affine_first_moment,
    layernorm_affine_second_moment,
):
    core = lax.axis_index("grp") & 1
    first_core = core == 0
    rows_shard = attention_entry_master.shape[1]
    halves = []
    for layer_idx in range(LAYERS):
        parts = {
            "joint": attention_entry_master[layer_idx],
            "output": attention_exit_master[layer_idx],
            "gateup": widening_projection_master[layer_idx],
            "down": lowering_projection_master[layer_idx],
        }
        parts = {k: core_half(v, core, 1).astype(jnp.bfloat16) for k, v in parts.items()}
        parts["down"] = fold_rows(parts["down"], rows_shard)
        halves.append(parts)
    norm_cols = layernorm_affine_master.reshape(LAYERS * 4, rows_shard).T.astype(jnp.bfloat16)
    norm_cols = jnp.pad(norm_cols, ((0, 0), (0, 128 - LAYERS * 4)))
    entries = [
        Gather([halves[0]["joint"], halves[0]["output"], norm_cols]),
        Gather([halves[1]["joint"], halves[1]["output"]]),
    ]
    wides = [Gather([half["gateup"], half["down"]]) for half in halves]
    half_joint = halves[0]["joint"].shape[1]
    half_output = halves[0]["output"].shape[1]
    weights = [{}, {}]

    def put_entry(layer_idx, act):
        act = finish(act, entries[layer_idx])
        weights[layer_idx]["joint"] = entries[layer_idx].pair(0)
        weights[layer_idx]["output"] = in_order(*entries[layer_idx].pair(1), first_core)
        return act

    def put_wide(layer_idx, act):
        act = finish(act, wides[layer_idx])
        weights[layer_idx]["gateup"] = wides[layer_idx].pair(0)
        pair = (unfold_rows(part, rows_shard) for part in wides[layer_idx].pair(1))
        weights[layer_idx]["down"] = in_order(*pair, first_core)
        return act

    def hook_zero(name, act):
        if name == "joint":
            act = checkpoint(act, start=[entries[0]])
            act = checkpoint(act, [entries[0]], [wides[0]])
            act = checkpoint(act, [entries[0]])
            act = checkpoint(act, [entries[0], wides[0]])
            act = checkpoint(act, [entries[0], wides[0]])
            act = put_entry(0, act)
            norm_full = entries[0].piece[2][:, : LAYERS * 4]
            norm_full = norm_full.T.reshape(LAYERS, 4, D).astype(jnp.float32)
            for layer_idx in range(LAYERS):
                weights[layer_idx]["norms"] = norm_full[layer_idx]
        elif name == "qkv":
            act = checkpoint(act, [wides[0]], [entries[1], wides[1]])
        elif name == "softmax":
            act = checkpoint(act, [entries[1], wides[1]])
        elif name == "mixed":
            act = checkpoint(act, [entries[1]])
        elif name == "gateup":
            act = checkpoint(act, [wides[0], entries[1], wides[1]])
            act = put_wide(0, act)
        elif name == "down":
            act = checkpoint(act, [entries[1]])
        return act

    def hook_one(name, act):
        if name == "joint":
            act = checkpoint(act, [entries[1], wides[1]])
            act = put_entry(1, act)
        elif name == "mixed":
            act = checkpoint(act, [wides[1]])
        elif name == "gateup":
            act = put_wide(1, act)
        return act

    rows_here = incoming_vectors.shape[0]
    seqs_here = sequence_extents.shape[0]
    positions, member, same_seg = segment_info(sequence_extents, rows_here)
    rotary = rotary_tables(positions, HDIM)
    length_float = sequence_extents.astype(jnp.float32)[:, None]
    hidden_state = incoming_vectors.astype(jnp.float32)
    kept_list = []
    for layer_idx in range(LAYERS):
        hidden_state, kept = layer_forward(
            hidden_state,
            weights[layer_idx],
            rotary,
            same_seg,
            first_core,
            (hook_zero, hook_one)[layer_idx],
        )
        kept_list.append(kept)
    hidden_out = hidden_state.astype(jnp.bfloat16)
    pooled = (
        jnp.einsum("ts,td->sd", member, hidden_state, precision=topmost_precision) / length_float
    )
    inv_norm = lax.rsqrt(jnp.sum(pooled * pooled, axis=-1, keepdims=True) + embed_eps)
    embed_low = (pooled * inv_norm).astype(jnp.bfloat16)
    every = cube_gather(embed_low, "dp", bit_order(0))
    every = cube_gather(every, "grp", list(range(axis_bits("grp") - 1, -1, -1)))
    every = every.reshape(-1, D)
    query_count = every.shape[0] // 2
    queries = every[:query_count]
    documents = every[query_count:]
    my_index = lax.axis_index("grp") * lax.axis_size("dp") + lax.axis_index("dp")
    is_query = lax.axis_index("grp") < lax.axis_size("grp") // 2
    logit_scale_factor = 1.0 / softmax_sharpness[0]
    similarity_logits = (
        jnp.einsum("qd,kd->qk", queries, documents, preferred_element_type=jnp.float32)
        * logit_scale_factor
    )
    target_rows = (
        jnp.arange(query_count, dtype=jnp.int32)[None, :] == matching_document_index[:, None]
    ).astype(jnp.float32)
    row_peak = jnp.max(similarity_logits, axis=-1, keepdims=True)
    exp_scores = jnp.exp(similarity_logits - row_peak)
    softmax_sum = jnp.sum(exp_scores, axis=-1, keepdims=True)
    row_loss = (
        row_peak[:, 0]
        + jnp.log(softmax_sum[:, 0])
        - jnp.sum(similarity_logits * target_rows, axis=-1)
    )
    loss_total = jnp.sum(row_loss) / query_count
    score_grad = (exp_scores / softmax_sum - target_rows) / query_count
    score_side = jnp.where(is_query, score_grad, score_grad.T)
    start_own = (my_index % (query_count // seqs_here)) * seqs_here
    score_own = lax.dynamic_slice_in_dim(score_side, start_own, seqs_here, axis=0)
    facing = jnp.where(is_query, documents, queries).astype(jnp.float32)
    embed_grad = (
        jnp.einsum("sk,kd->sd", score_own, facing, precision=topmost_precision)
        * logit_scale_factor
    )
    pooled_grad = inv_norm * embed_grad - pooled * inv_norm * inv_norm * inv_norm * jnp.sum(
        pooled * embed_grad, axis=-1, keepdims=True
    )
    state_grad = jnp.einsum(
        "ts,sd->td", member, pooled_grad / length_float, precision=topmost_precision
    )
    sums = [{}, {}]

    def pair_of(columns):
        own = jnp.concatenate([pair[0] for pair in columns], axis=1)
        far = jnp.concatenate([pair[1].astype(jnp.bfloat16) for pair in columns], axis=1)
        return own, far

    def folded(pair):
        return tuple(fold_rows(part, rows_shard) for part in pair)

    def wide_sum(gateup_pair, down_pair):
        return Scatter([gateup_pair, folded(down_pair)])

    def back_one(name, act, *grads):
        moves = sums[1]
        if name == "gateup":
            moves["wide"] = wide_sum(*grads)
            act = checkpoint(act, start=[moves["wide"]])
        elif name in ("first", "merged"):
            act = checkpoint(act, [moves["wide"]])
        elif name == "joint":
            moves["entry"] = Scatter([pair_of(grads[:2])])
            act = checkpoint(act, start=[moves["entry"]])
        return act

    def back_zero(name, act, *grads):
        early, moves = [sums[1]["wide"], sums[1]["entry"]], sums[0]
        if name in ("second", "act"):
            act = checkpoint(act, early)
        elif name == "gateup":
            moves["wide"] = wide_sum(*grads)
            act = checkpoint(act, early, [moves["wide"]])
        elif name == "first":
            act = checkpoint(act, [moves["wide"]] + early)
        elif name == "center":
            act = checkpoint(act, early)
        elif name == "merged":
            act = checkpoint(act, [moves["wide"]])
        return act

    state_grad, last_grads = layer_backward(
        state_grad, weights[1], kept_list[1], rotary, same_seg, first_core, back_one
    )
    state_grad, first_grads = layer_backward(
        state_grad, weights[0], kept_list[0], rotary, same_seg, first_core, back_zero
    )
    norm_grads = jnp.stack([first_grads[4], last_grads[4]]).reshape(LAYERS * 4, D).T
    norm_grads = jnp.pad(norm_grads, ((0, 0), (0, 128 - LAYERS * 4)))
    sums[0]["entry"] = Scatter(
        [pair_of([first_grads[0], first_grads[1], (norm_grads, norm_grads)])]
    )
    sums[0]["entry"].start()
    for move in (sums[0]["wide"], sums[0]["entry"], sums[1]["entry"], sums[1]["wide"]):
        run_out(move)

    def columns_of(kind, start, stop):
        return [
            in_order(layer[kind].rows[:, start:stop], layer[kind].far[:, start:stop], first_core)
            for layer in sums
        ]

    def down_of(layer):
        move = layer["wide"]
        pair = (unfold_rows(v[:, FF:], rows_shard) for v in (move.rows, move.far))
        return in_order(*pair, first_core)

    half_entry = half_joint + half_output
    rows = (
        columns_of("entry", 0, half_joint),
        columns_of("entry", half_joint, half_entry),
        columns_of("wide", 0, FF),
        [down_of(layer) for layer in sums],
    )
    shards = [jnp.stack(pair).astype(jnp.float32) for pair in rows]
    norm_shard = sums[0]["entry"].rows[:, half_entry:][:, : LAYERS * 4].astype(jnp.float32)
    shards.append(norm_shard.T.reshape(LAYERS, 4, -1))
    step_float = optimizer_iteration_number[0].astype(jnp.float32)
    bias_first = 1.0 - jnp.power(beta_one, step_float)
    bias_second = 1.0 - jnp.power(beta_two, step_float)
    joint_weight, joint_moment, joint_square, joint_copy = adamw_update(
        shards[0],
        attention_entry_master,
        attention_entry_first_moment,
        attention_entry_second_moment,
        bias_first,
        bias_second,
        rate_matrix,
        decay_rate,
    )
    output_weight, output_moment, output_square, output_copy = adamw_update(
        shards[1],
        attention_exit_master,
        attention_exit_first_moment,
        attention_exit_second_moment,
        bias_first,
        bias_second,
        rate_matrix,
        decay_rate,
    )
    gateup_weight, gateup_moment, gateup_square, gateup_copy = adamw_update(
        shards[2],
        widening_projection_master,
        widening_first_moment,
        widening_second_moment,
        bias_first,
        bias_second,
        rate_matrix,
        decay_rate,
    )
    down_weight, down_moment, down_square, down_copy = adamw_update(
        shards[3],
        lowering_projection_master,
        lowering_first_moment,
        lowering_second_moment,
        bias_first,
        bias_second,
        rate_matrix,
        decay_rate,
    )
    norms_weight, norms_moment, norms_square, norms_copy = adamw_update(
        shards[4],
        layernorm_affine_master,
        layernorm_affine_first_moment,
        layernorm_affine_second_moment,
        bias_first,
        bias_second,
        rate_norms,
        0.0,
    )
    loss_value = jnp.reshape(loss_total, (1,))
    return (
        hidden_out,
        state_grad,
        loss_value,
        joint_weight,
        joint_moment,
        joint_square,
        joint_copy,
        output_weight,
        output_moment,
        output_square,
        output_copy,
        gateup_weight,
        gateup_moment,
        gateup_square,
        gateup_copy,
        down_weight,
        down_moment,
        down_square,
        down_copy,
        norms_weight,
        norms_moment,
        norms_square,
        norms_copy,
    )


def solution(mesh):
    return jax.shard_map(
        body,
        mesh=mesh,
        in_specs=(
            P(("grp", "dp"), None),
            P(("grp", "dp")),
            P(),
            P(),
            P(),
            P(None, "dp", None),
            P(None, "dp", None),
            P(None, "dp", None),
            P(None, "dp", None),
            P(None, "dp", None),
            P(None, "dp", None),
            P(None, "dp", None),
            P(None, "dp", None),
            P(None, "dp", None),
            P(None, "dp", None),
            P(None, "dp", None),
            P(None, "dp", None),
            P(None, None, "dp"),
            P(None, None, "dp"),
            P(None, None, "dp"),
        ),
        out_specs=(
            P(("grp", "dp"), None),
            P(("grp", "dp"), None),
            P(),
            P(None, "dp", None),
            P(None, "dp", None),
            P(None, "dp", None),
            P(None, "dp", None),
            P(None, "dp", None),
            P(None, "dp", None),
            P(None, "dp", None),
            P(None, "dp", None),
            P(None, "dp", None),
            P(None, "dp", None),
            P(None, "dp", None),
            P(None, "dp", None),
            P(None, "dp", None),
            P(None, "dp", None),
            P(None, "dp", None),
            P(None, "dp", None),
            P(None, None, "dp"),
            P(None, None, "dp"),
            P(None, None, "dp"),
            P(None, None, "dp"),
        ),
        check_vma=False,
    )
```

```python
import math

import jax
import jax.numpy as jnp
from jax import lax
from jax.sharding import PartitionSpec as P

D = 768
HEADS = 12
FF = 3072
HDIM = 64
LAYERS = 2


beta_one = 0.9
beta_two = 0.999
adam_eps = 1e-08
decay_rate = 0.01
rate_matrix = 0.08
rate_norms = 1.0
norm_eps = 1e-05
embed_eps = 1e-06
masked_score = -1000000000.0
rotary_base = 1000.0
topmost_precision = lax.Precision.HIGHEST


def axis_bits(axis):
    return lax.axis_size(axis).bit_length() - 1


def swap_bit(value, axis, bit):
    count = lax.axis_size(axis)
    return lax.ppermute(value, axis, [(i, i ^ (1 << bit)) for i in range(count)])


def my_bit(axis, bit):
    return (lax.axis_index(axis) >> bit) & 1


def cube_gather(piece, axis, bits):
    held = []
    for bit in bits:
        other = swap_bit(piece, axis, bit)
        place = sum(1 for b in held if b > bit)
        first = my_bit(axis, bit) == 0
        piece = jnp.stack(
            [jnp.where(first, piece, other), jnp.where(first, other, piece)], axis=place
        )
        held.append(bit)
    return piece


def bit_order(color):
    order = list(range(axis_bits("dp") - 1, -1, -1))
    if color and len(order) > 1:
        order[-1], order[-2] = order[-2], order[-1]
    return order


def core_half(value, core, axis):
    half = value.shape[axis] // 2
    return lax.dynamic_slice_in_dim(value, core * half, half, axis)


def lane_cut(width):
    return width // 256 * 128


def columns_between(lanes, start, stop):
    cut = lanes[0].shape[-1]
    held = []
    if start < cut:
        held.append(lanes[0][..., start : min(stop, cut)])
    if stop > cut:
        held.append(lanes[1][..., max(start - cut, 0) : stop - cut])
    return held[0] if len(held) == 1 else jnp.concatenate(held, axis=-1)


class Gather:
    def __init__(self, parts):
        self.widths = [part.shape[1] for part in parts]
        self.piece = [jnp.concatenate(parts, axis=1)]
        order = bit_order(0)
        self.todo = [order, bit_order(1)]
        self.held = [[], []]
        self.moving = None
        self.far = None
        self.split()

    def split(self):
        if len(self.piece) == 1 and len(self.todo[0]) <= 2:
            cut = lane_cut(self.piece[0].shape[-1])
            self.piece = [self.piece[0][..., :cut], self.piece[0][..., cut:]]

    def sends(self):
        return list(self.piece)

    def start(self, sends):
        if self.todo[0]:
            self.moving = [
                swap_bit(lane, "dp", todo[0]) for lane, todo in zip(sends, self.todo)
            ]
        else:
            self.moving = [swap_bit(part, "grp", 0) for part in sends]

    def land(self):
        arrived, self.moving = self.moving, None
        if not self.todo[0]:
            self.far = arrived
            return
        for k in range(2):
            bit = self.todo[k].pop(0)
            if k < len(arrived):
                place = sum(1 for b in self.held[k] if b > bit)
                first = my_bit("dp", bit) == 0
                here, other = self.piece[k], arrived[k]
                self.piece[k] = jnp.stack(
                    [jnp.where(first, here, other), jnp.where(first, other, here)], axis=place
                )
            self.held[k].append(bit)
        self.split()
        if not self.todo[0]:
            lanes = [lane.reshape(-1, lane.shape[-1]) for lane in self.piece]
            self.piece = []
            start = 0
            for width in self.widths:
                self.piece.append(columns_between(lanes, start, start + width))
                start += width

    def complete(self):
        return self.far is not None

    def pair(self, index):
        return self.piece[index], self.far[index]


class Scatter:
    def __init__(self, pairs):
        self.mine = [pair[0] for pair in pairs]
        self.piece = [pair[1].astype(jnp.bfloat16) for pair in pairs]
        self.todo = [bit_order(0)[::-1], bit_order(1)[::-1]]
        self.left = [sorted(todo, reverse=True) for todo in self.todo]
        self.rest = list(range(1, axis_bits("grp")))
        self.whole = None
        self.rows = None
        self.moving = None
        self.far = None

    def sends(self):
        if self.whole is None:
            return list(self.piece)
        if self.todo[0]:
            return [
                lax.dynamic_index_in_dim(
                    lane, 1 - my_bit("dp", todo[0]), left.index(todo[0]), keepdims=False
                )
                for lane, todo, left in zip(self.whole, self.todo, self.left)
            ]
        return [self.rows]

    def start(self, sends):
        if self.whole is None:
            self.moving = [swap_bit(part, "grp", 0) for part in sends]
        elif self.todo[0]:
            self.moving = [
                swap_bit(away, "dp", todo[0]) for away, todo in zip(sends, self.todo)
            ]
        else:
            self.moving = [swap_bit(sends[0], "grp", self.rest[0] if self.rest else 0)]

    def land(self):
        arrived, self.moving = self.moving, None
        if self.whole is None:
            both = [
                (mine + other.astype(jnp.float32)).astype(jnp.bfloat16)
                for mine, other in zip(self.mine, arrived)
            ]
            both = [part.reshape((2,) * len(self.left[0]) + (-1, part.shape[1])) for part in both]
            width = sum(part.shape[-1] for part in both)
            cut = lane_cut(width)
            if len(both) == 1:
                self.whole = [both[0][..., :cut], both[0][..., cut:]]
            else:
                tail = jnp.concatenate([both[0][..., cut:]] + both[1:], axis=-1)
                self.whole = [both[0][..., :cut], tail]
        elif self.todo[0]:
            for k in range(2):
                bit = self.todo[k].pop(0)
                if k < len(arrived):
                    keep = lax.dynamic_index_in_dim(
                        self.whole[k], my_bit("dp", bit), self.left[k].index(bit), keepdims=False
                    )
                    self.whole[k] = (
                        keep.astype(jnp.float32) + arrived[k].astype(jnp.float32)
                    ).astype(jnp.bfloat16)
                self.left[k].remove(bit)
            if len(self.whole) == 2 and self.left[0] == self.left[1]:
                self.whole = [jnp.concatenate(self.whole, axis=-1)]
            if not self.todo[0]:
                self.rows = self.whole[0]
        elif self.rest:
            self.rest.pop(0)
            self.rows = (
                self.rows.astype(jnp.float32) + arrived[0].astype(jnp.float32)
            ).astype(jnp.bfloat16)
        else:
            self.far = arrived[0]

    def complete(self):
        return self.far is not None


def checkpoint(act, land=(), start=()):
    land = [move for move in land if move.moving is not None]
    if not land and not start:
        return act
    act, arrived = lax.optimization_barrier((act, [move.moving for move in land]))
    for move, value in zip(land, arrived):
        move.moving = value
        move.land()
    going = [move for move in land if not move.complete()] + list(start)
    act, sends = lax.optimization_barrier((act, [move.sends() for move in going]))
    for move, value in zip(going, sends):
        move.start(value)
    return act


def finish(act, move):
    while not move.complete():
        act = checkpoint(act, [move])
    return act


def fold_rows(value, count):
    ratio = FF // D
    wide = value.reshape(-1, ratio, count, value.shape[1])
    return jnp.swapaxes(wide, 1, 2).reshape(-1, ratio * value.shape[1])


def unfold_rows(value, count):
    ratio = FF // D
    wide = value.reshape(-1, count, ratio, value.shape[1] // ratio)
    return jnp.swapaxes(wide, 1, 2).reshape(-1, value.shape[1] // ratio)


def in_order(mine, other, first):
    return jnp.concatenate(
        [jnp.where(first, mine, other), jnp.where(first, other, mine)], axis=1
    )


def own_and_far(value, first):
    half = value.shape[1] // 2
    low, high = value[:, :half], value[:, half:]
    return jnp.where(first, low, high), jnp.where(first, high, low)


def segment_info(seq_lengths, rows_here):
    seq_ends = jnp.cumsum(seq_lengths)
    row_ids = jnp.arange(rows_here, dtype=jnp.int32)
    past_end = (row_ids[:, None] >= seq_ends[None, :]).astype(jnp.int32)
    segment = jnp.sum(past_end, axis=1)
    positions = row_ids - jnp.sum(past_end * seq_lengths[None, :], axis=1)
    member = (
        segment[:, None] == jnp.arange(seq_lengths.shape[0], dtype=jnp.int32)[None, :]
    ).astype(jnp.float32)
    same_seg = segment[:, None] == segment[None, :]
    return (positions, member, same_seg)


def rotary_tables(positions, head_dim):
    half_dim = head_dim // 2
    frequency = rotary_base ** (-2.0 * jnp.arange(half_dim, dtype=jnp.float32) / head_dim)
    angles = positions.astype(jnp.float32)[:, None] * frequency[None, :]
    return (jnp.cos(angles), jnp.sin(angles))


def rotate(values, cosine, sine_part):
    half_dim = values.shape[-1] // 2
    front_half = values[..., :half_dim]
    back_half = values[..., half_dim:]
    cos_wide = cosine[:, None, :]
    sin_wide = sine_part[:, None, :]
    return jnp.concatenate(
        [
            front_half * cos_wide - back_half * sin_wide,
            back_half * cos_wide + front_half * sin_wide,
        ],
        axis=-1,
    )


def rotate_back(values, cosine, sine_part):
    half_dim = values.shape[-1] // 2
    front_half = values[..., :half_dim]
    back_half = values[..., half_dim:]
    cos_wide = cosine[:, None, :]
    sin_wide = sine_part[:, None, :]
    return jnp.concatenate(
        [
            front_half * cos_wide + back_half * sin_wide,
            back_half * cos_wide - front_half * sin_wide,
        ],
        axis=-1,
    )


def normalize(values):
    centered = values - jnp.mean(values, axis=-1, keepdims=True)
    inv_std = lax.rsqrt(jnp.mean(centered * centered, axis=-1, keepdims=True) + norm_eps)
    return (centered * inv_std, inv_std)


def norm_back(grad, normed, inv_std, gain):
    scaled = grad * gain
    inner = inv_std * (
        scaled
        - jnp.mean(scaled, axis=-1, keepdims=True)
        - normed * jnp.mean(scaled * normed, axis=-1, keepdims=True)
    )
    return (inner, jnp.sum(grad * normed, axis=0), jnp.sum(grad, axis=0))


def score_block(query_rot, key_rot, same_seg):
    similarity_logits = jnp.einsum(
        "thd,shd->hts", query_rot, key_rot, preferred_element_type=jnp.float32
    ) * (1.0 / math.sqrt(HDIM))
    return jnp.where(same_seg[None], similarity_logits, masked_score)


def layer_forward(inputs, weights, rotary, same_seg, first_core, hook):
    rows_here = inputs.shape[0]
    inputs = hook("joint", inputs)
    joint_w = weights["joint"]
    inputs_low = inputs.astype(jnp.bfloat16)
    merged = in_order(
        jnp.dot(inputs_low, joint_w[0], preferred_element_type=jnp.float32),
        jnp.dot(inputs_low, joint_w[1], preferred_element_type=jnp.float32),
        first_core,
    )
    query_rot = rotate(merged[:, :D].reshape(rows_here, HEADS, HDIM), rotary[0], rotary[1]).astype(
        jnp.bfloat16
    )
    key_rot = rotate(
        merged[:, D : 2 * D].reshape(rows_here, HEADS, HDIM), rotary[0], rotary[1]
    ).astype(jnp.bfloat16)
    value_low = merged[:, 2 * D :].reshape(rows_here, HEADS, HDIM).astype(jnp.bfloat16)
    query_rot, key_rot, value_low = hook("qkv", (query_rot, key_rot, value_low))
    similarity_logits = score_block(query_rot, key_rot, same_seg)
    row_peak = jnp.max(similarity_logits, axis=-1, keepdims=True)
    exp_scores = jnp.exp(similarity_logits - row_peak)
    softmax_sum = jnp.sum(exp_scores, axis=-1, keepdims=True)
    softmax_sum = hook("softmax", softmax_sum)
    weights_p = exp_scores / softmax_sum
    log_total = row_peak + jnp.log(softmax_sum)
    mixed = jnp.einsum(
        "hts,shd->thd",
        weights_p.astype(jnp.bfloat16),
        value_low,
        preferred_element_type=jnp.float32,
    )
    mixed = mixed.reshape(rows_here, D).astype(jnp.bfloat16)
    mixed = hook("mixed", mixed)
    output_w, gain_rows = weights["output"], weights["norms"]
    attended = jnp.dot(mixed, output_w, preferred_element_type=jnp.float32)
    first_normed, first_inv = normalize(inputs + attended)
    hidden = first_normed * gain_rows[0] + gain_rows[1]
    hidden = hook("gateup", hidden)
    hidden_low = hidden.astype(jnp.bfloat16)
    gateup_w = weights["gateup"]
    own_part = jnp.dot(hidden_low, gateup_w[0], preferred_element_type=jnp.float32)
    far_part = jnp.dot(hidden_low, gateup_w[1], preferred_element_type=jnp.float32)
    gate_part = jnp.where(first_core, own_part, far_part)
    up_part = jnp.where(first_core, far_part, own_part)
    act_low = (jax.nn.silu(gate_part) * up_part).astype(jnp.bfloat16)
    act_low = hook("down", act_low)
    branch = jnp.dot(act_low, weights["down"], preferred_element_type=jnp.float32)
    second_normed, second_inv = normalize(hidden + branch)
    result = second_normed * gain_rows[2] + gain_rows[3]
    kept = (
        inputs_low,
        query_rot,
        key_rot,
        value_low,
        log_total,
        mixed,
        first_normed,
        first_inv,
        hidden_low,
        own_part,
        far_part,
        act_low,
        second_normed,
        second_inv,
    )
    return (result, kept)


def layer_backward(grad_out, weights, kept, rotary, same_seg, first_core, hook):
    joint_w, output_w, gateup_w, down_w, gain_rows = (
        weights[name] for name in ("joint", "output", "gateup", "down", "norms")
    )
    (
        inputs_low,
        query_rot,
        key_rot,
        value_low,
        log_total,
        mixed,
        first_normed,
        first_inv,
        hidden_low,
        own_part,
        far_part,
        act_low,
        second_normed,
        second_inv,
    ) = kept
    rows_here = inputs_low.shape[0]
    score_scale = 1.0 / math.sqrt(HDIM)
    second_in, gain_two, bias_two = norm_back(grad_out, second_normed, second_inv, gain_rows[2])
    second_in = hook("second", second_in)
    branch_grad = second_in.astype(jnp.bfloat16)
    down_grad = tuple(
        jnp.einsum("tf,td->fd", act_low, part, preferred_element_type=jnp.float32)
        for part in own_and_far(branch_grad, first_core)
    )
    act_grad = jnp.einsum("td,fd->tf", branch_grad, down_w, preferred_element_type=jnp.float32)
    gate_part = jnp.where(first_core, own_part, far_part)
    up_part = jnp.where(first_core, far_part, own_part)
    sigmoid_g = jax.nn.sigmoid(gate_part)
    gate_grad = act_grad * up_part * sigmoid_g * (1.0 + gate_part * (1.0 - sigmoid_g))
    up_grad = act_grad * gate_part * sigmoid_g
    own_grad = jnp.where(first_core, gate_grad, up_grad).astype(jnp.bfloat16)
    far_grad = jnp.where(first_core, up_grad, gate_grad).astype(jnp.bfloat16)
    own_grad, far_grad = hook("act", (own_grad, far_grad))
    gateup_grad = tuple(
        jnp.einsum("td,tf->df", hidden_low, part, preferred_element_type=jnp.float32)
        for part in (own_grad, far_grad)
    )
    own_grad = hook("gateup", own_grad, gateup_grad, down_grad)
    hidden_grad = (
        second_in
        + jnp.einsum("tf,df->td", own_grad, gateup_w[0], preferred_element_type=jnp.float32)
        + jnp.einsum("tf,df->td", far_grad, gateup_w[1], preferred_element_type=jnp.float32)
    )
    first_in, gain_one, bias_one = norm_back(hidden_grad, first_normed, first_inv, gain_rows[0])
    first_in = hook("first", first_in)
    attended_grad = first_in.astype(jnp.bfloat16)
    output_grad = tuple(
        jnp.einsum("tc,td->cd", mixed, part, preferred_element_type=jnp.float32)
        for part in own_and_far(attended_grad, first_core)
    )
    mixed_grad = jnp.einsum(
        "td,cd->tc", attended_grad, output_w, preferred_element_type=jnp.float32
    )
    mixed_grad = mixed_grad.astype(jnp.bfloat16).reshape(rows_here, HEADS, HDIM)
    similarity_logits = score_block(query_rot, key_rot, same_seg)
    weights_p = jnp.exp(similarity_logits - log_total)
    prob_grad = jnp.einsum(
        "thd,shd->hts", mixed_grad, value_low, preferred_element_type=jnp.float32
    )
    center = jnp.sum(prob_grad * weights_p, axis=-1, keepdims=True)
    center = hook("center", center)
    score_grad = (weights_p * (prob_grad - center)).astype(jnp.bfloat16)
    value_grad = jnp.einsum(
        "hts,thd->shd",
        weights_p.astype(jnp.bfloat16),
        mixed_grad,
        preferred_element_type=jnp.float32,
    )
    query_grad = (
        jnp.einsum("hts,shd->thd", score_grad, key_rot, preferred_element_type=jnp.float32)
        * score_scale
    )
    key_grad = (
        jnp.einsum("hts,thd->shd", score_grad, query_rot, preferred_element_type=jnp.float32)
        * score_scale
    )
    merged_grad = jnp.concatenate(
        [
            rotate_back(query_grad, rotary[0], rotary[1]).reshape(rows_here, D),
            rotate_back(key_grad, rotary[0], rotary[1]).reshape(rows_here, D),
            value_grad.reshape(rows_here, D),
        ],
        axis=1,
    ).astype(jnp.bfloat16)
    merged_grad = hook("merged", merged_grad)
    merged_own, merged_far = own_and_far(merged_grad, first_core)
    joint_grad = tuple(
        jnp.einsum("tc,tf->cf", inputs_low, part, preferred_element_type=jnp.float32)
        for part in (merged_own, merged_far)
    )
    norms_grad = jnp.stack([gain_one, bias_one, gain_two, bias_two])
    merged_own = hook("joint", merged_own, joint_grad, output_grad, norms_grad)
    input_grad = (
        first_in
        + jnp.einsum("tf,cf->tc", merged_own, joint_w[0], preferred_element_type=jnp.float32)
        + jnp.einsum("tf,cf->tc", merged_far, joint_w[1], preferred_element_type=jnp.float32)
    )
    return (input_grad, (joint_grad, output_grad, gateup_grad, down_grad, norms_grad))


def adamw_update(grad, master, first, second, bias_first, bias_second, rate, decay):
    moment = beta_one * first + (1.0 - beta_one) * grad
    squared_values = beta_two * second + (1.0 - beta_two) * grad * grad
    newer = master - rate * (
        moment / bias_first / (jnp.sqrt(squared_values / bias_second) + adam_eps) + decay * master
    )
    return (newer, moment, squared_values, newer.astype(jnp.bfloat16))


def body(
    incoming_vectors,
    sequence_extents,
    matching_document_index,
    softmax_sharpness,
    optimizer_iteration_number,
    attention_entry_master,
    attention_entry_first_moment,
    attention_entry_second_moment,
    attention_exit_master,
    attention_exit_first_moment,
    attention_exit_second_moment,
    widening_projection_master,
    widening_first_moment,
    widening_second_moment,
    lowering_projection_master,
    lowering_first_moment,
    lowering_second_moment,
    layernorm_affine_master,
    layernorm_affine_first_moment,
    layernorm_affine_second_moment,
):
    core = lax.axis_index("grp") & 1
    first_core = core == 0
    rows_shard = attention_entry_master.shape[1]
    halves = []
    for layer_idx in range(LAYERS):
        parts = {
            "joint": attention_entry_master[layer_idx],
            "output": attention_exit_master[layer_idx],
            "gateup": widening_projection_master[layer_idx],
            "down": lowering_projection_master[layer_idx],
        }
        parts = {k: core_half(v, core, 1).astype(jnp.bfloat16) for k, v in parts.items()}
        parts["down"] = fold_rows(parts["down"], rows_shard)
        halves.append(parts)
    norm_cols = layernorm_affine_master.reshape(LAYERS * 4, rows_shard).T.astype(jnp.bfloat16)
    norm_cols = jnp.pad(norm_cols, ((0, 0), (0, 128 - LAYERS * 4)))
    entries = [
        Gather([halves[0]["joint"], halves[0]["output"], norm_cols]),
        Gather([halves[1]["joint"], halves[1]["output"]]),
    ]
    wides = [Gather([half["gateup"], half["down"]]) for half in halves]
    half_joint = halves[0]["joint"].shape[1]
    half_output = halves[0]["output"].shape[1]
    weights = [{}, {}]

    def put_entry(layer_idx, act):
        act = finish(act, entries[layer_idx])
        weights[layer_idx]["joint"] = entries[layer_idx].pair(0)
        weights[layer_idx]["output"] = in_order(*entries[layer_idx].pair(1), first_core)
        return act

    def put_wide(layer_idx, act):
        act = finish(act, wides[layer_idx])
        weights[layer_idx]["gateup"] = wides[layer_idx].pair(0)
        pair = (unfold_rows(part, rows_shard) for part in wides[layer_idx].pair(1))
        weights[layer_idx]["down"] = in_order(*pair, first_core)
        return act

    def hook_zero(name, act):
        if name == "joint":
            act = checkpoint(act, start=[entries[0]])
            act = checkpoint(act, [entries[0]])
            act = checkpoint(act, [entries[0]], [wides[0]])
            act = checkpoint(act, [entries[0]])
            act = checkpoint(act, [entries[0], wides[0]])
            act = put_entry(0, act)
            norm_full = entries[0].piece[2][:, : LAYERS * 4]
            norm_full = norm_full.T.reshape(LAYERS, 4, D).astype(jnp.float32)
            for layer_idx in range(LAYERS):
                weights[layer_idx]["norms"] = norm_full[layer_idx]
        elif name == "qkv":
            act = checkpoint(act, [wides[0]], [entries[1]])
        elif name == "softmax":
            act = checkpoint(act, [wides[0], entries[1]], [wides[1]])
        elif name == "mixed":
            act = checkpoint(act, [entries[1], wides[1]])
        elif name == "gateup":
            act = checkpoint(act, [wides[0], entries[1], wides[1]])
            act = put_wide(0, act)
        elif name == "down":
            act = checkpoint(act, [entries[1]])
        return act

    def hook_one(name, act):
        if name == "joint":
            act = checkpoint(act, [entries[1], wides[1]])
            act = put_entry(1, act)
        elif name == "mixed":
            act = checkpoint(act, [wides[1]])
        elif name == "gateup":
            act = put_wide(1, act)
        return act

    rows_here = incoming_vectors.shape[0]
    seqs_here = sequence_extents.shape[0]
    positions, member, same_seg = segment_info(sequence_extents, rows_here)
    rotary = rotary_tables(positions, HDIM)
    length_float = sequence_extents.astype(jnp.float32)[:, None]
    hidden_state = incoming_vectors.astype(jnp.float32)
    kept_list = []
    for layer_idx in range(LAYERS):
        hidden_state, kept = layer_forward(
            hidden_state,
            weights[layer_idx],
            rotary,
            same_seg,
            first_core,
            (hook_zero, hook_one)[layer_idx],
        )
        kept_list.append(kept)
    hidden_out = hidden_state.astype(jnp.bfloat16)
    pooled = (
        jnp.einsum("ts,td->sd", member, hidden_state, precision=topmost_precision) / length_float
    )
    inv_norm = lax.rsqrt(jnp.sum(pooled * pooled, axis=-1, keepdims=True) + embed_eps)
    embed_low = (pooled * inv_norm).astype(jnp.bfloat16)
    every = cube_gather(embed_low, "dp", bit_order(0))
    every = cube_gather(every, "grp", list(range(axis_bits("grp") - 1, -1, -1)))
    every = every.reshape(-1, D)
    query_count = every.shape[0] // 2
    queries = every[:query_count]
    documents = every[query_count:]
    my_index = lax.axis_index("grp") * lax.axis_size("dp") + lax.axis_index("dp")
    is_query = lax.axis_index("grp") < lax.axis_size("grp") // 2
    logit_scale_factor = 1.0 / softmax_sharpness[0]
    similarity_logits = (
        jnp.einsum("qd,kd->qk", queries, documents, preferred_element_type=jnp.float32)
        * logit_scale_factor
    )
    target_rows = (
        jnp.arange(query_count, dtype=jnp.int32)[None, :] == matching_document_index[:, None]
    ).astype(jnp.float32)
    row_peak = jnp.max(similarity_logits, axis=-1, keepdims=True)
    exp_scores = jnp.exp(similarity_logits - row_peak)
    softmax_sum = jnp.sum(exp_scores, axis=-1, keepdims=True)
    row_loss = (
        row_peak[:, 0]
        + jnp.log(softmax_sum[:, 0])
        - jnp.sum(similarity_logits * target_rows, axis=-1)
    )
    loss_total = jnp.sum(row_loss) / query_count
    score_grad = (exp_scores / softmax_sum - target_rows) / query_count
    score_side = jnp.where(is_query, score_grad, score_grad.T)
    start_own = (my_index % (query_count // seqs_here)) * seqs_here
    score_own = lax.dynamic_slice_in_dim(score_side, start_own, seqs_here, axis=0)
    facing = jnp.where(is_query, documents, queries).astype(jnp.float32)
    embed_grad = (
        jnp.einsum("sk,kd->sd", score_own, facing, precision=topmost_precision)
        * logit_scale_factor
    )
    pooled_grad = inv_norm * embed_grad - pooled * inv_norm * inv_norm * inv_norm * jnp.sum(
        pooled * embed_grad, axis=-1, keepdims=True
    )
    state_grad = jnp.einsum(
        "ts,sd->td", member, pooled_grad / length_float, precision=topmost_precision
    )
    sums = [{}, {}]

    def pair_of(columns):
        own = jnp.concatenate([pair[0] for pair in columns], axis=1)
        far = jnp.concatenate([pair[1].astype(jnp.bfloat16) for pair in columns], axis=1)
        return own, far

    def folded(pair):
        return tuple(fold_rows(part, rows_shard) for part in pair)

    def wide_sum(gateup_pair, down_pair):
        return Scatter([gateup_pair, folded(down_pair)])

    def back_one(name, act, *grads):
        moves = sums[1]
        if name == "gateup":
            moves["wide"] = wide_sum(*grads)
            act = checkpoint(act, start=[moves["wide"]])
        elif name in ("first", "merged"):
            act = checkpoint(act, [moves["wide"]])
        elif name == "joint":
            moves["entry"] = Scatter([pair_of(grads[:2])])
            moves["norms"] = grads[2]
            act = checkpoint(act, start=[moves["entry"]])
        return act

    def back_zero(name, act, *grads):
        early, moves = [sums[1]["wide"], sums[1]["entry"]], sums[0]
        if name in ("second", "act"):
            act = checkpoint(act, early)
        elif name == "gateup":
            moves["wide"] = wide_sum(*grads)
            act = checkpoint(act, early, [moves["wide"]])
        elif name == "first":
            act = checkpoint(act, [moves["wide"]] + early)
        elif name == "center":
            act = checkpoint(act, early)
        elif name == "merged":
            act = checkpoint(act, [moves["wide"]])
        elif name == "joint":
            norm_cols = jnp.stack([grads[2], sums[1]["norms"]]).reshape(LAYERS * 4, D).T
            norm_cols = jnp.pad(norm_cols, ((0, 0), (0, 128 - LAYERS * 4)))
            moves["entry"] = Scatter([pair_of([grads[0], grads[1], (norm_cols, norm_cols)])])
            act = checkpoint(act, [moves["wide"]] + early, [moves["entry"]])
        return act

    state_grad, _ = layer_backward(
        state_grad, weights[1], kept_list[1], rotary, same_seg, first_core, back_one
    )
    state_grad, _ = layer_backward(
        state_grad, weights[0], kept_list[0], rotary, same_seg, first_core, back_zero
    )
    last = [layer[kind] for layer in sums[::-1] for kind in ("wide", "entry")]
    while not all(move.complete() for move in last):
        state_grad = checkpoint(state_grad, last)

    def columns_of(kind, start, stop):
        return [
            in_order(layer[kind].rows[:, start:stop], layer[kind].far[:, start:stop], first_core)
            for layer in sums
        ]

    def down_of(layer):
        move = layer["wide"]
        pair = (unfold_rows(v[:, FF:], rows_shard) for v in (move.rows, move.far))
        return in_order(*pair, first_core)

    half_entry = half_joint + half_output
    rows = (
        columns_of("entry", 0, half_joint),
        columns_of("entry", half_joint, half_entry),
        columns_of("wide", 0, FF),
        [down_of(layer) for layer in sums],
    )
    shards = [jnp.stack(pair).astype(jnp.float32) for pair in rows]
    norm_shard = sums[0]["entry"].rows[:, half_entry:][:, : LAYERS * 4].astype(jnp.float32)
    shards.append(norm_shard.T.reshape(LAYERS, 4, -1))
    step_float = optimizer_iteration_number[0].astype(jnp.float32)
    bias_first = 1.0 - jnp.power(beta_one, step_float)
    bias_second = 1.0 - jnp.power(beta_two, step_float)
    joint_weight, joint_moment, joint_square, joint_copy = adamw_update(
        shards[0],
        attention_entry_master,
        attention_entry_first_moment,
        attention_entry_second_moment,
        bias_first,
        bias_second,
        rate_matrix,
        decay_rate,
    )
    output_weight, output_moment, output_square, output_copy = adamw_update(
        shards[1],
        attention_exit_master,
        attention_exit_first_moment,
        attention_exit_second_moment,
        bias_first,
        bias_second,
        rate_matrix,
        decay_rate,
    )
    gateup_weight, gateup_moment, gateup_square, gateup_copy = adamw_update(
        shards[2],
        widening_projection_master,
        widening_first_moment,
        widening_second_moment,
        bias_first,
        bias_second,
        rate_matrix,
        decay_rate,
    )
    down_weight, down_moment, down_square, down_copy = adamw_update(
        shards[3],
        lowering_projection_master,
        lowering_first_moment,
        lowering_second_moment,
        bias_first,
        bias_second,
        rate_matrix,
        decay_rate,
    )
    norms_weight, norms_moment, norms_square, norms_copy = adamw_update(
        shards[4],
        layernorm_affine_master,
        layernorm_affine_first_moment,
        layernorm_affine_second_moment,
        bias_first,
        bias_second,
        rate_norms,
        0.0,
    )
    loss_value = jnp.reshape(loss_total, (1,))
    return (
        hidden_out,
        state_grad,
        loss_value,
        joint_weight,
        joint_moment,
        joint_square,
        joint_copy,
        output_weight,
        output_moment,
        output_square,
        output_copy,
        gateup_weight,
        gateup_moment,
        gateup_square,
        gateup_copy,
        down_weight,
        down_moment,
        down_square,
        down_copy,
        norms_weight,
        norms_moment,
        norms_square,
        norms_copy,
    )


def solution(mesh):
    return jax.shard_map(
        body,
        mesh=mesh,
        in_specs=(
            P(("grp", "dp"), None),
            P(("grp", "dp")),
            P(),
            P(),
            P(),
            P(None, "dp", None),
            P(None, "dp", None),
            P(None, "dp", None),
            P(None, "dp", None),
            P(None, "dp", None),
            P(None, "dp", None),
            P(None, "dp", None),
            P(None, "dp", None),
            P(None, "dp", None),
            P(None, "dp", None),
            P(None, "dp", None),
            P(None, "dp", None),
            P(None, None, "dp"),
            P(None, None, "dp"),
            P(None, None, "dp"),
        ),
        out_specs=(
            P(("grp", "dp"), None),
            P(("grp", "dp"), None),
            P(),
            P(None, "dp", None),
            P(None, "dp", None),
            P(None, "dp", None),
            P(None, "dp", None),
            P(None, "dp", None),
            P(None, "dp", None),
            P(None, "dp", None),
            P(None, "dp", None),
            P(None, "dp", None),
            P(None, "dp", None),
            P(None, "dp", None),
            P(None, "dp", None),
            P(None, "dp", None),
            P(None, "dp", None),
            P(None, "dp", None),
            P(None, "dp", None),
            P(None, None, "dp"),
            P(None, None, "dp"),
            P(None, None, "dp"),
            P(None, None, "dp"),
        ),
        check_vma=False,
    )
```

```python
import math

import jax
import jax.numpy as jnp
from jax import lax
from jax.experimental import pallas as pl
from jax.experimental.pallas import tpu as pltpu
from jax.sharding import PartitionSpec as P

D = 768
HEADS = 12
FF = 3072
HDIM = 64
LAYERS = 2


beta_one = 0.9
beta_two = 0.999
adam_eps = 1e-08
decay_rate = 0.01
rate_matrix = 0.08
rate_norms = 1.0
norm_eps = 1e-05
embed_eps = 1e-06
masked_score = -1000000000.0
rotary_base = 1000.0
topmost_precision = lax.Precision.HIGHEST


def axis_bits(axis):
    return lax.axis_size(axis).bit_length() - 1


def swap_bit(value, axis, bit):
    count = lax.axis_size(axis)
    return lax.ppermute(value, axis, [(i, i ^ (1 << bit)) for i in range(count)])


def my_bit(axis, bit):
    return (lax.axis_index(axis) >> bit) & 1


def cube_gather(piece, axis, bits):
    held = []
    for bit in bits:
        other = swap_bit(piece, axis, bit)
        place = sum(1 for b in held if b > bit)
        first = my_bit(axis, bit) == 0
        piece = jnp.stack(
            [jnp.where(first, piece, other), jnp.where(first, other, piece)], axis=place
        )
        held.append(bit)
    return piece


def bit_order(color):
    order = list(range(axis_bits("dp") - 1, -1, -1))
    if color and len(order) > 1:
        order[-1], order[-2] = order[-2], order[-1]
    return order


def core_half(value, core, axis):
    half = value.shape[axis] // 2
    return lax.dynamic_slice_in_dim(value, core * half, half, axis)


def lane_cut(width):
    return width // 256 * 128


def columns_between(lanes, start, stop):
    cut = lanes[0].shape[-1]
    held = []
    if start < cut:
        held.append(lanes[0][..., start : min(stop, cut)])
    if stop > cut:
        held.append(lanes[1][..., max(start - cut, 0) : stop - cut])
    return held[0] if len(held) == 1 else jnp.concatenate(held, axis=-1)


class Gather:
    def __init__(self, parts):
        self.widths = [part.shape[1] for part in parts]
        self.piece = [jnp.concatenate(parts, axis=1)]
        order = bit_order(0)
        self.todo = [order, bit_order(1)]
        self.held = [[], []]
        self.moving = None
        self.far = None
        self.split()

    def split(self):
        if len(self.piece) == 1 and len(self.todo[0]) <= 2:
            cut = lane_cut(self.piece[0].shape[-1])
            self.piece = [self.piece[0][..., :cut], self.piece[0][..., cut:]]

    def sends(self):
        return list(self.piece)

    def start(self, sends):
        if self.todo[0]:
            self.moving = [
                swap_bit(lane, "dp", todo[0]) for lane, todo in zip(sends, self.todo)
            ]
        else:
            self.moving = [swap_bit(part, "grp", 0) for part in sends]

    def land(self):
        arrived, self.moving = self.moving, None
        if not self.todo[0]:
            self.far = arrived
            return
        for k in range(2):
            bit = self.todo[k].pop(0)
            if k < len(arrived):
                place = sum(1 for b in self.held[k] if b > bit)
                first = my_bit("dp", bit) == 0
                here, other = self.piece[k], arrived[k]
                self.piece[k] = jnp.stack(
                    [jnp.where(first, here, other), jnp.where(first, other, here)], axis=place
                )
            self.held[k].append(bit)
        self.split()
        if not self.todo[0]:
            lanes = [lane.reshape(-1, lane.shape[-1]) for lane in self.piece]
            self.piece = []
            start = 0
            for width in self.widths:
                self.piece.append(columns_between(lanes, start, start + width))
                start += width

    def complete(self):
        return self.far is not None

    def pair(self, index):
        return self.piece[index], self.far[index]


class Scatter:
    def __init__(self, pairs):
        self.mine = [pair[0] for pair in pairs]
        self.piece = [pair[1].astype(jnp.bfloat16) for pair in pairs]
        self.todo = [bit_order(0)[::-1], bit_order(1)[::-1]]
        self.left = [sorted(todo, reverse=True) for todo in self.todo]
        self.rest = list(range(1, axis_bits("grp")))
        self.whole = None
        self.rows = None
        self.moving = None
        self.far = None

    def sends(self):
        if self.whole is None:
            return list(self.piece)
        if self.todo[0]:
            return [
                lax.dynamic_index_in_dim(
                    lane, 1 - my_bit("dp", todo[0]), left.index(todo[0]), keepdims=False
                )
                for lane, todo, left in zip(self.whole, self.todo, self.left)
            ]
        return [self.rows]

    def start(self, sends):
        if self.whole is None:
            self.moving = [swap_bit(part, "grp", 0) for part in sends]
        elif self.todo[0]:
            self.moving = [
                swap_bit(away, "dp", todo[0]) for away, todo in zip(sends, self.todo)
            ]
        else:
            self.moving = [swap_bit(sends[0], "grp", self.rest[0] if self.rest else 0)]

    def land(self):
        arrived, self.moving = self.moving, None
        if self.whole is None:
            both = [
                (mine + other.astype(jnp.float32)).astype(jnp.bfloat16)
                for mine, other in zip(self.mine, arrived)
            ]
            both = [part.reshape((2,) * len(self.left[0]) + (-1, part.shape[1])) for part in both]
            width = sum(part.shape[-1] for part in both)
            cut = lane_cut(width)
            if len(both) == 1:
                self.whole = [both[0][..., :cut], both[0][..., cut:]]
            else:
                tail = jnp.concatenate([both[0][..., cut:]] + both[1:], axis=-1)
                self.whole = [both[0][..., :cut], tail]
        elif self.todo[0]:
            for k in range(2):
                bit = self.todo[k].pop(0)
                if k < len(arrived):
                    keep = lax.dynamic_index_in_dim(
                        self.whole[k], my_bit("dp", bit), self.left[k].index(bit), keepdims=False
                    )
                    self.whole[k] = (
                        keep.astype(jnp.float32) + arrived[k].astype(jnp.float32)
                    ).astype(jnp.bfloat16)
                self.left[k].remove(bit)
            if len(self.whole) == 2 and self.left[0] == self.left[1]:
                self.whole = [jnp.concatenate(self.whole, axis=-1)]
            if not self.todo[0]:
                self.rows = self.whole[0]
        elif self.rest:
            self.rest.pop(0)
            self.rows = (
                self.rows.astype(jnp.float32) + arrived[0].astype(jnp.float32)
            ).astype(jnp.bfloat16)
        else:
            self.far = arrived[0]

    def complete(self):
        return self.far is not None


def checkpoint(act, land=(), start=()):
    land = [move for move in land if move.moving is not None]
    if not land and not start:
        return act
    act, arrived = lax.optimization_barrier((act, [move.moving for move in land]))
    for move, value in zip(land, arrived):
        move.moving = value
        move.land()
    going = [move for move in land if not move.complete()] + list(start)
    act, sends = lax.optimization_barrier((act, [move.sends() for move in going]))
    for move, value in zip(going, sends):
        move.start(value)
    return act


def finish(act, move):
    while not move.complete():
        act = checkpoint(act, [move])
    return act


def fold_rows(value, count):
    ratio = FF // D
    wide = value.reshape(-1, ratio, count, value.shape[1])
    return jnp.swapaxes(wide, 1, 2).reshape(-1, ratio * value.shape[1])


def unfold_rows(value, count):
    ratio = FF // D
    wide = value.reshape(-1, count, ratio, value.shape[1] // ratio)
    return jnp.swapaxes(wide, 1, 2).reshape(-1, value.shape[1] // ratio)


def in_order(mine, other, first):
    return jnp.concatenate(
        [jnp.where(first, mine, other), jnp.where(first, other, mine)], axis=1
    )


def own_and_far(value, first):
    half = value.shape[1] // 2
    low, high = value[:, :half], value[:, half:]
    return jnp.where(first, low, high), jnp.where(first, high, low)


def segment_info(seq_lengths, rows_here):
    seq_ends = jnp.cumsum(seq_lengths)
    row_ids = jnp.arange(rows_here, dtype=jnp.int32)
    past_end = (row_ids[:, None] >= seq_ends[None, :]).astype(jnp.int32)
    segment = jnp.sum(past_end, axis=1)
    positions = row_ids - jnp.sum(past_end * seq_lengths[None, :], axis=1)
    member = (
        segment[:, None] == jnp.arange(seq_lengths.shape[0], dtype=jnp.int32)[None, :]
    ).astype(jnp.float32)
    return (positions, member, segment)


PAIR = 2 * HDIM


def rotary_tables(positions):
    half_dim = HDIM // 2
    frequency = rotary_base ** (-2.0 * jnp.arange(half_dim, dtype=jnp.float32) / HDIM)
    angles = positions.astype(jnp.float32)[:, None] * frequency[None, :]
    cosine, sine = jnp.cos(angles), jnp.sin(angles)
    return (
        jnp.concatenate([cosine] * 4, axis=1),
        jnp.concatenate([-sine, sine, -sine, sine], axis=1),
    )


def half_swap(values):
    lane = lax.broadcasted_iota(jnp.int32, values.shape, 1)
    front = (lane % HDIM) < HDIM // 2
    return jnp.where(
        front,
        pltpu.roll(values, PAIR - HDIM // 2, 1),
        pltpu.roll(values, HDIM // 2, 1),
    )


def pair_dot(left, right, contract):
    return lax.dot_general(
        left, right, ((contract[:1], contract[1:]), ((), ())), preferred_element_type=jnp.float32
    )


def head_lanes(shape, head):
    return lax.broadcasted_iota(jnp.int32, shape, 1) // HDIM == head


def head_only(values, head):
    wide = values.astype(jnp.float32)
    return jnp.where(head_lanes(values.shape, head), wide, 0.0).astype(values.dtype)


def head_softmax(query, key, row_seg, col_seg, head):
    scores = pair_dot(head_only(query, head), key, (1, 1)) * (1.0 / math.sqrt(HDIM))
    scores = jnp.where(row_seg == col_seg, scores, masked_score)
    peak = jnp.max(scores, axis=1, keepdims=True)
    raised = jnp.exp(scores - peak)
    return raised / jnp.sum(raised, axis=1, keepdims=True)


def attend_kernel(q_in, k_in, v_in, cos_in, sin_in, row_in, col_in, q_out, k_out, v_out, o_out):
    cosine, sine = cos_in[...], sin_in[...]
    query = q_in[...]
    key = k_in[...]
    query = (query * cosine + half_swap(query) * sine).astype(jnp.bfloat16)
    key = (key * cosine + half_swap(key) * sine).astype(jnp.bfloat16)
    value = v_in[...].astype(jnp.bfloat16)
    q_out[...] = query
    k_out[...] = key
    v_out[...] = value
    parts = []
    for head in range(2):
        weights_p = head_softmax(query, key, row_in[...], col_in[...], head)
        parts.append(pair_dot(weights_p.astype(jnp.bfloat16), value, (1, 0)))
    mixed = jnp.where(head_lanes(parts[0].shape, 0), parts[0], parts[1])
    o_out[...] = mixed.astype(jnp.bfloat16)


def attend_back_kernel(
    q_in, k_in, v_in, do_in, cos_in, sin_in, row_in, col_in, dq_out, dk_out, dv_out
):
    query, key, value, grad = q_in[...], k_in[...], v_in[...], do_in[...]
    sides = []
    for head in range(2):
        weights_p = head_softmax(query, key, row_in[...], col_in[...], head)
        prob_grad = pair_dot(head_only(grad, head), value, (1, 1))
        center = jnp.sum(prob_grad * weights_p, axis=1, keepdims=True)
        score_grad = (weights_p * (prob_grad - center)).astype(jnp.bfloat16)
        low = weights_p.astype(jnp.bfloat16)
        sides.append(
            (
                pair_dot(score_grad, key, (1, 0)),
                pair_dot(score_grad, query, (0, 0)),
                pair_dot(low, grad, (0, 0)),
            )
        )
    first = head_lanes(query.shape, 0)
    dq, dk, dv = (jnp.where(first, one, two) for one, two in zip(*sides))
    cosine, sine = cos_in[...], sin_in[...]
    for out, side in ((dq_out, dq), (dk_out, dk)):
        side = side * (1.0 / math.sqrt(HDIM))
        out[...] = (side * cosine - half_swap(side) * sine).astype(jnp.bfloat16)
    dv_out[...] = dv.astype(jnp.bfloat16)


def pair_specs(rows_here):
    def block(offset):
        return pl.BlockSpec((rows_here, PAIR), lambda j, offset=offset: (0, j + offset))

    table = pl.BlockSpec((rows_here, PAIR), lambda j: (0, 0))
    row = pl.BlockSpec((rows_here, 1), lambda j: (0, 0))
    col = pl.BlockSpec((1, rows_here), lambda j: (0, 0))
    return block, [table, table, row, col]


def attend(merged, rotary, segment):
    rows_here = merged.shape[0]
    pairs = D // PAIR
    block, shared = pair_specs(rows_here)
    return pl.pallas_call(
        attend_kernel,
        grid=(pairs,),
        in_specs=[block(0), block(pairs), block(2 * pairs)] + shared,
        out_specs=[block(0)] * 4,
        out_shape=[jax.ShapeDtypeStruct((rows_here, D), jnp.bfloat16)] * 4,
        name="attend",
    )(merged, merged, merged, *rotary, segment[:, None], segment[None, :])


def attend_back(query, key, value, grad, rotary, segment):
    rows_here = query.shape[0]
    block, shared = pair_specs(rows_here)
    return pl.pallas_call(
        attend_back_kernel,
        grid=(D // PAIR,),
        in_specs=[block(0)] * 4 + shared,
        out_specs=[block(0)] * 3,
        out_shape=[jax.ShapeDtypeStruct((rows_here, D), jnp.bfloat16)] * 3,
        name="attend_back",
    )(query, key, value, grad, *rotary, segment[:, None], segment[None, :])


def normalize(values):
    centered = values - jnp.mean(values, axis=-1, keepdims=True)
    inv_std = lax.rsqrt(jnp.mean(centered * centered, axis=-1, keepdims=True) + norm_eps)
    return (centered * inv_std, inv_std)


def norm_back(grad, normed, inv_std, gain):
    scaled = grad * gain
    inner = inv_std * (
        scaled
        - jnp.mean(scaled, axis=-1, keepdims=True)
        - normed * jnp.mean(scaled * normed, axis=-1, keepdims=True)
    )
    return (inner, jnp.sum(grad * normed, axis=0), jnp.sum(grad, axis=0))


def layer_forward(inputs, weights, rotary, segment, first_core, hook):
    inputs = hook("joint", inputs)
    joint_w = weights["joint"]
    inputs_low = inputs.astype(jnp.bfloat16)
    merged = in_order(
        jnp.dot(inputs_low, joint_w[0], preferred_element_type=jnp.float32),
        jnp.dot(inputs_low, joint_w[1], preferred_element_type=jnp.float32),
        first_core,
    )
    merged = hook("qkv", merged)
    query_rot, key_rot, value_low, mixed = attend(merged, rotary, segment)
    mixed = hook("mixed", mixed)
    output_w, gain_rows = weights["output"], weights["norms"]
    attended = jnp.dot(mixed, output_w, preferred_element_type=jnp.float32)
    first_normed, first_inv = normalize(inputs + attended)
    hidden = first_normed * gain_rows[0] + gain_rows[1]
    hidden = hook("gateup", hidden)
    hidden_low = hidden.astype(jnp.bfloat16)
    gateup_w = weights["gateup"]
    own_part = jnp.dot(hidden_low, gateup_w[0], preferred_element_type=jnp.float32)
    far_part = jnp.dot(hidden_low, gateup_w[1], preferred_element_type=jnp.float32)
    gate_part = jnp.where(first_core, own_part, far_part)
    up_part = jnp.where(first_core, far_part, own_part)
    act_low = (jax.nn.silu(gate_part) * up_part).astype(jnp.bfloat16)
    act_low = hook("down", act_low)
    branch = jnp.dot(act_low, weights["down"], preferred_element_type=jnp.float32)
    second_normed, second_inv = normalize(hidden + branch)
    result = second_normed * gain_rows[2] + gain_rows[3]
    kept = (
        inputs_low,
        query_rot,
        key_rot,
        value_low,
        mixed,
        first_normed,
        first_inv,
        hidden_low,
        own_part,
        far_part,
        act_low,
        second_normed,
        second_inv,
    )
    return (result, kept)


def layer_backward(grad_out, weights, kept, rotary, segment, first_core, hook):
    joint_w, output_w, gateup_w, down_w, gain_rows = (
        weights[name] for name in ("joint", "output", "gateup", "down", "norms")
    )
    (
        inputs_low,
        query_rot,
        key_rot,
        value_low,
        mixed,
        first_normed,
        first_inv,
        hidden_low,
        own_part,
        far_part,
        act_low,
        second_normed,
        second_inv,
    ) = kept
    second_in, gain_two, bias_two = norm_back(grad_out, second_normed, second_inv, gain_rows[2])
    second_in = hook("second", second_in)
    branch_grad = second_in.astype(jnp.bfloat16)
    down_grad = tuple(
        jnp.einsum("tf,td->fd", act_low, part, preferred_element_type=jnp.float32)
        for part in own_and_far(branch_grad, first_core)
    )
    act_grad = jnp.einsum("td,fd->tf", branch_grad, down_w, preferred_element_type=jnp.float32)
    gate_part = jnp.where(first_core, own_part, far_part)
    up_part = jnp.where(first_core, far_part, own_part)
    sigmoid_g = jax.nn.sigmoid(gate_part)
    gate_grad = act_grad * up_part * sigmoid_g * (1.0 + gate_part * (1.0 - sigmoid_g))
    up_grad = act_grad * gate_part * sigmoid_g
    own_grad = jnp.where(first_core, gate_grad, up_grad).astype(jnp.bfloat16)
    far_grad = jnp.where(first_core, up_grad, gate_grad).astype(jnp.bfloat16)
    own_grad, far_grad = hook("act", (own_grad, far_grad))
    gateup_grad = tuple(
        jnp.einsum("td,tf->df", hidden_low, part, preferred_element_type=jnp.float32)
        for part in (own_grad, far_grad)
    )
    own_grad = hook("gateup", own_grad, gateup_grad, down_grad)
    hidden_grad = (
        second_in
        + jnp.einsum("tf,df->td", own_grad, gateup_w[0], preferred_element_type=jnp.float32)
        + jnp.einsum("tf,df->td", far_grad, gateup_w[1], preferred_element_type=jnp.float32)
    )
    first_in, gain_one, bias_one = norm_back(hidden_grad, first_normed, first_inv, gain_rows[0])
    first_in = hook("first", first_in)
    attended_grad = first_in.astype(jnp.bfloat16)
    output_grad = tuple(
        jnp.einsum("tc,td->cd", mixed, part, preferred_element_type=jnp.float32)
        for part in own_and_far(attended_grad, first_core)
    )
    mixed_grad = jnp.einsum(
        "td,cd->tc", attended_grad, output_w, preferred_element_type=jnp.float32
    )
    merged_grad = jnp.concatenate(
        attend_back(
            query_rot, key_rot, value_low, mixed_grad.astype(jnp.bfloat16), rotary, segment
        ),
        axis=1,
    )
    merged_grad = hook("merged", merged_grad)
    merged_own, merged_far = own_and_far(merged_grad, first_core)
    joint_grad = tuple(
        jnp.einsum("tc,tf->cf", inputs_low, part, preferred_element_type=jnp.float32)
        for part in (merged_own, merged_far)
    )
    norms_grad = jnp.stack([gain_one, bias_one, gain_two, bias_two])
    merged_own = hook("joint", merged_own, joint_grad, output_grad, norms_grad)
    input_grad = (
        first_in
        + jnp.einsum("tf,cf->tc", merged_own, joint_w[0], preferred_element_type=jnp.float32)
        + jnp.einsum("tf,cf->tc", merged_far, joint_w[1], preferred_element_type=jnp.float32)
    )
    return (input_grad, (joint_grad, output_grad, gateup_grad, down_grad, norms_grad))


def adamw_update(grad, master, first, second, bias_first, bias_second, rate, decay):
    moment = beta_one * first + (1.0 - beta_one) * grad
    squared_values = beta_two * second + (1.0 - beta_two) * grad * grad
    newer = master - rate * (
        moment / bias_first / (jnp.sqrt(squared_values / bias_second) + adam_eps) + decay * master
    )
    return (newer, moment, squared_values, newer.astype(jnp.bfloat16))


def body(
    incoming_vectors,
    sequence_extents,
    matching_document_index,
    softmax_sharpness,
    optimizer_iteration_number,
    attention_entry_master,
    attention_entry_first_moment,
    attention_entry_second_moment,
    attention_exit_master,
    attention_exit_first_moment,
    attention_exit_second_moment,
    widening_projection_master,
    widening_first_moment,
    widening_second_moment,
    lowering_projection_master,
    lowering_first_moment,
    lowering_second_moment,
    layernorm_affine_master,
    layernorm_affine_first_moment,
    layernorm_affine_second_moment,
):
    core = lax.axis_index("grp") & 1
    first_core = core == 0
    rows_shard = attention_entry_master.shape[1]
    halves = []
    for layer_idx in range(LAYERS):
        parts = {
            "joint": attention_entry_master[layer_idx],
            "output": attention_exit_master[layer_idx],
            "gateup": widening_projection_master[layer_idx],
            "down": lowering_projection_master[layer_idx],
        }
        parts = {k: core_half(v, core, 1).astype(jnp.bfloat16) for k, v in parts.items()}
        parts["down"] = fold_rows(parts["down"], rows_shard)
        halves.append(parts)
    norm_cols = layernorm_affine_master.reshape(LAYERS * 4, rows_shard).T.astype(jnp.bfloat16)
    norm_cols = jnp.pad(norm_cols, ((0, 0), (0, 128 - LAYERS * 4)))
    entries = [
        Gather([halves[0]["joint"], halves[0]["output"], norm_cols]),
        Gather([halves[1]["joint"], halves[1]["output"]]),
    ]
    wides = [Gather([half["gateup"], half["down"]]) for half in halves]
    half_joint = halves[0]["joint"].shape[1]
    half_output = halves[0]["output"].shape[1]
    weights = [{}, {}]

    def put_entry(layer_idx, act):
        act = finish(act, entries[layer_idx])
        weights[layer_idx]["joint"] = entries[layer_idx].pair(0)
        weights[layer_idx]["output"] = in_order(*entries[layer_idx].pair(1), first_core)
        return act

    def put_wide(layer_idx, act):
        act = finish(act, wides[layer_idx])
        weights[layer_idx]["gateup"] = wides[layer_idx].pair(0)
        pair = (unfold_rows(part, rows_shard) for part in wides[layer_idx].pair(1))
        weights[layer_idx]["down"] = in_order(*pair, first_core)
        return act

    def hook_zero(name, act):
        if name == "joint":
            act = checkpoint(act, start=[entries[0]])
            act = checkpoint(act, [entries[0]])
            act = checkpoint(act, [entries[0]], [wides[0]])
            act = checkpoint(act, [entries[0]])
            act = checkpoint(act, [entries[0], wides[0]])
            act = put_entry(0, act)
            norm_full = entries[0].piece[2][:, : LAYERS * 4]
            norm_full = norm_full.T.reshape(LAYERS, 4, D).astype(jnp.float32)
            for layer_idx in range(LAYERS):
                weights[layer_idx]["norms"] = norm_full[layer_idx]
        elif name == "qkv":
            act = checkpoint(act, [wides[0]], [entries[1]])
        elif name == "mixed":
            act = checkpoint(act, [wides[0], entries[1]], [wides[1]])
        elif name == "gateup":
            act = checkpoint(act, [entries[1], wides[1]])
            act = checkpoint(act, [wides[0]])
            act = put_wide(0, act)
        elif name == "down":
            act = checkpoint(act, [entries[1], wides[1]])
        return act

    def hook_one(name, act):
        if name == "joint":
            act = checkpoint(act, [entries[1], wides[1]])
            act = put_entry(1, act)
        elif name == "mixed":
            act = checkpoint(act, [wides[1]])
        elif name == "gateup":
            act = put_wide(1, act)
        return act

    rows_here = incoming_vectors.shape[0]
    seqs_here = sequence_extents.shape[0]
    positions, member, segment = segment_info(sequence_extents, rows_here)
    rotary = rotary_tables(positions)
    length_float = sequence_extents.astype(jnp.float32)[:, None]
    hidden_state = incoming_vectors.astype(jnp.float32)
    kept_list = []
    for layer_idx in range(LAYERS):
        hidden_state, kept = layer_forward(
            hidden_state,
            weights[layer_idx],
            rotary,
            segment,
            first_core,
            (hook_zero, hook_one)[layer_idx],
        )
        kept_list.append(kept)
    hidden_out = hidden_state.astype(jnp.bfloat16)
    pooled = (
        jnp.einsum("ts,td->sd", member, hidden_state, precision=topmost_precision) / length_float
    )
    inv_norm = lax.rsqrt(jnp.sum(pooled * pooled, axis=-1, keepdims=True) + embed_eps)
    embed_low = (pooled * inv_norm).astype(jnp.bfloat16)
    every = cube_gather(embed_low, "dp", bit_order(0))
    every = cube_gather(every, "grp", list(range(axis_bits("grp") - 1, -1, -1)))
    every = every.reshape(-1, D)
    query_count = every.shape[0] // 2
    queries = every[:query_count]
    documents = every[query_count:]
    my_index = lax.axis_index("grp") * lax.axis_size("dp") + lax.axis_index("dp")
    is_query = lax.axis_index("grp") < lax.axis_size("grp") // 2
    logit_scale_factor = 1.0 / softmax_sharpness[0]
    similarity_logits = (
        jnp.einsum("qd,kd->qk", queries, documents, preferred_element_type=jnp.float32)
        * logit_scale_factor
    )
    target_rows = (
        jnp.arange(query_count, dtype=jnp.int32)[None, :] == matching_document_index[:, None]
    ).astype(jnp.float32)
    row_peak = jnp.max(similarity_logits, axis=-1, keepdims=True)
    exp_scores = jnp.exp(similarity_logits - row_peak)
    softmax_sum = jnp.sum(exp_scores, axis=-1, keepdims=True)
    row_loss = (
        row_peak[:, 0]
        + jnp.log(softmax_sum[:, 0])
        - jnp.sum(similarity_logits * target_rows, axis=-1)
    )
    loss_total = jnp.sum(row_loss) / query_count
    score_grad = (exp_scores / softmax_sum - target_rows) / query_count
    score_side = jnp.where(is_query, score_grad, score_grad.T)
    start_own = (my_index % (query_count // seqs_here)) * seqs_here
    score_own = lax.dynamic_slice_in_dim(score_side, start_own, seqs_here, axis=0)
    facing = jnp.where(is_query, documents, queries).astype(jnp.float32)
    embed_grad = (
        jnp.einsum("sk,kd->sd", score_own, facing, precision=topmost_precision)
        * logit_scale_factor
    )
    pooled_grad = inv_norm * embed_grad - pooled * inv_norm * inv_norm * inv_norm * jnp.sum(
        pooled * embed_grad, axis=-1, keepdims=True
    )
    state_grad = jnp.einsum(
        "ts,sd->td", member, pooled_grad / length_float, precision=topmost_precision
    )
    sums = [{}, {}]

    def pair_of(columns):
        own = jnp.concatenate([pair[0] for pair in columns], axis=1)
        far = jnp.concatenate([pair[1].astype(jnp.bfloat16) for pair in columns], axis=1)
        return own, far

    def folded(pair):
        return tuple(fold_rows(part, rows_shard) for part in pair)

    def wide_sum(gateup_pair, down_pair):
        return Scatter([gateup_pair, folded(down_pair)])

    def back_one(name, act, *grads):
        moves = sums[1]
        if name == "gateup":
            moves["wide"] = wide_sum(*grads)
            act = checkpoint(act, start=[moves["wide"]])
        elif name in ("first", "merged"):
            act = checkpoint(act, [moves["wide"]])
        elif name == "joint":
            moves["entry"] = Scatter([pair_of(grads[:2])])
            moves["norms"] = grads[2]
            act = checkpoint(act, start=[moves["entry"]])
        return act

    def back_zero(name, act, *grads):
        early, moves = [sums[1]["wide"], sums[1]["entry"]], sums[0]
        if name in ("second", "act"):
            act = checkpoint(act, early)
        elif name == "gateup":
            moves["wide"] = wide_sum(*grads)
            act = checkpoint(act, early, [moves["wide"]])
        elif name == "first":
            act = checkpoint(act, [moves["wide"]] + early)
        elif name == "merged":
            act = checkpoint(act, [moves["wide"]] + early)
        elif name == "joint":
            norm_cols = jnp.stack([grads[2], sums[1]["norms"]]).reshape(LAYERS * 4, D).T
            norm_cols = jnp.pad(norm_cols, ((0, 0), (0, 128 - LAYERS * 4)))
            moves["entry"] = Scatter([pair_of([grads[0], grads[1], (norm_cols, norm_cols)])])
            act = checkpoint(act, [moves["wide"]] + early, [moves["entry"]])
        return act

    state_grad, _ = layer_backward(
        state_grad, weights[1], kept_list[1], rotary, segment, first_core, back_one
    )
    state_grad, _ = layer_backward(
        state_grad, weights[0], kept_list[0], rotary, segment, first_core, back_zero
    )
    last = [layer[kind] for layer in sums[::-1] for kind in ("wide", "entry")]
    while not all(move.complete() for move in last):
        state_grad = checkpoint(state_grad, last)

    def columns_of(kind, start, stop):
        return [
            in_order(layer[kind].rows[:, start:stop], layer[kind].far[:, start:stop], first_core)
            for layer in sums
        ]

    def down_of(layer):
        move = layer["wide"]
        pair = (unfold_rows(v[:, FF:], rows_shard) for v in (move.rows, move.far))
        return in_order(*pair, first_core)

    half_entry = half_joint + half_output
    rows = (
        columns_of("entry", 0, half_joint),
        columns_of("entry", half_joint, half_entry),
        columns_of("wide", 0, FF),
        [down_of(layer) for layer in sums],
    )
    shards = [jnp.stack(pair).astype(jnp.float32) for pair in rows]
    norm_shard = sums[0]["entry"].rows[:, half_entry:][:, : LAYERS * 4].astype(jnp.float32)
    shards.append(norm_shard.T.reshape(LAYERS, 4, -1))
    step_float = optimizer_iteration_number[0].astype(jnp.float32)
    bias_first = 1.0 - jnp.power(beta_one, step_float)
    bias_second = 1.0 - jnp.power(beta_two, step_float)
    joint_weight, joint_moment, joint_square, joint_copy = adamw_update(
        shards[0],
        attention_entry_master,
        attention_entry_first_moment,
        attention_entry_second_moment,
        bias_first,
        bias_second,
        rate_matrix,
        decay_rate,
    )
    output_weight, output_moment, output_square, output_copy = adamw_update(
        shards[1],
        attention_exit_master,
        attention_exit_first_moment,
        attention_exit_second_moment,
        bias_first,
        bias_second,
        rate_matrix,
        decay_rate,
    )
    gateup_weight, gateup_moment, gateup_square, gateup_copy = adamw_update(
        shards[2],
        widening_projection_master,
        widening_first_moment,
        widening_second_moment,
        bias_first,
        bias_second,
        rate_matrix,
        decay_rate,
    )
    down_weight, down_moment, down_square, down_copy = adamw_update(
        shards[3],
        lowering_projection_master,
        lowering_first_moment,
        lowering_second_moment,
        bias_first,
        bias_second,
        rate_matrix,
        decay_rate,
    )
    norms_weight, norms_moment, norms_square, norms_copy = adamw_update(
        shards[4],
        layernorm_affine_master,
        layernorm_affine_first_moment,
        layernorm_affine_second_moment,
        bias_first,
        bias_second,
        rate_norms,
        0.0,
    )
    loss_value = jnp.reshape(loss_total, (1,))
    return (
        hidden_out,
        state_grad,
        loss_value,
        joint_weight,
        joint_moment,
        joint_square,
        joint_copy,
        output_weight,
        output_moment,
        output_square,
        output_copy,
        gateup_weight,
        gateup_moment,
        gateup_square,
        gateup_copy,
        down_weight,
        down_moment,
        down_square,
        down_copy,
        norms_weight,
        norms_moment,
        norms_square,
        norms_copy,
    )


def solution(mesh):
    return jax.shard_map(
        body,
        mesh=mesh,
        in_specs=(
            P(("grp", "dp"), None),
            P(("grp", "dp")),
            P(),
            P(),
            P(),
            P(None, "dp", None),
            P(None, "dp", None),
            P(None, "dp", None),
            P(None, "dp", None),
            P(None, "dp", None),
            P(None, "dp", None),
            P(None, "dp", None),
            P(None, "dp", None),
            P(None, "dp", None),
            P(None, "dp", None),
            P(None, "dp", None),
            P(None, "dp", None),
            P(None, None, "dp"),
            P(None, None, "dp"),
            P(None, None, "dp"),
        ),
        out_specs=(
            P(("grp", "dp"), None),
            P(("grp", "dp"), None),
            P(),
            P(None, "dp", None),
            P(None, "dp", None),
            P(None, "dp", None),
            P(None, "dp", None),
            P(None, "dp", None),
            P(None, "dp", None),
            P(None, "dp", None),
            P(None, "dp", None),
            P(None, "dp", None),
            P(None, "dp", None),
            P(None, "dp", None),
            P(None, "dp", None),
            P(None, "dp", None),
            P(None, "dp", None),
            P(None, "dp", None),
            P(None, "dp", None),
            P(None, None, "dp"),
            P(None, None, "dp"),
            P(None, None, "dp"),
            P(None, None, "dp"),
        ),
        check_vma=False,
    )
```

```python
import math

import jax
import jax.numpy as jnp
from jax import lax
from jax.experimental import pallas as pl
from jax.experimental.pallas import tpu as pltpu
from jax.sharding import PartitionSpec as P

D = 768
HEADS = 12
FF = 3072
HDIM = 64
LAYERS = 2


beta_one = 0.9
beta_two = 0.999
adam_eps = 1e-08
decay_rate = 0.01
rate_matrix = 0.08
rate_norms = 1.0
norm_eps = 1e-05
embed_eps = 1e-06
masked_score = -1000000000.0
rotary_base = 1000.0
topmost_precision = lax.Precision.HIGHEST


def axis_bits(axis):
    return lax.axis_size(axis).bit_length() - 1


def swap_bit(value, axis, bit):
    count = lax.axis_size(axis)
    return lax.ppermute(value, axis, [(i, i ^ (1 << bit)) for i in range(count)])


def my_bit(axis, bit):
    return (lax.axis_index(axis) >> bit) & 1


def cube_gather(piece, axis, bits):
    held = []
    for bit in bits:
        other = swap_bit(piece, axis, bit)
        place = sum(1 for b in held if b > bit)
        first = my_bit(axis, bit) == 0
        piece = jnp.stack(
            [jnp.where(first, piece, other), jnp.where(first, other, piece)], axis=place
        )
        held.append(bit)
    return piece


def bit_order(color):
    order = list(range(axis_bits("dp") - 1, -1, -1))
    if color and len(order) > 1:
        order[-1], order[-2] = order[-2], order[-1]
    return order


def core_half(value, core, axis):
    half = value.shape[axis] // 2
    return lax.dynamic_slice_in_dim(value, core * half, half, axis)


def lane_cut(width):
    return width // 256 * 128


def columns_between(lanes, start, stop):
    cut = lanes[0].shape[-1]
    held = []
    if start < cut:
        held.append(lanes[0][..., start : min(stop, cut)])
    if stop > cut:
        held.append(lanes[1][..., max(start - cut, 0) : stop - cut])
    return held[0] if len(held) == 1 else jnp.concatenate(held, axis=-1)


class Gather:
    def __init__(self, parts):
        self.widths = [part.shape[1] for part in parts]
        self.piece = [jnp.concatenate(parts, axis=1)]
        order = bit_order(0)
        self.todo = [order, bit_order(1)]
        self.held = [[], []]
        self.moving = None
        self.far = None
        self.split()

    def split(self):
        if len(self.piece) == 1 and len(self.todo[0]) <= 2:
            cut = lane_cut(self.piece[0].shape[-1])
            self.piece = [self.piece[0][..., :cut], self.piece[0][..., cut:]]

    def sends(self):
        return list(self.piece)

    def start(self, sends):
        if self.todo[0]:
            self.moving = [
                swap_bit(lane, "dp", todo[0]) for lane, todo in zip(sends, self.todo)
            ]
        else:
            self.moving = [swap_bit(part, "grp", 0) for part in sends]

    def land(self):
        arrived, self.moving = self.moving, None
        if not self.todo[0]:
            self.far = arrived
            return
        for k in range(2):
            bit = self.todo[k].pop(0)
            if k < len(arrived):
                place = sum(1 for b in self.held[k] if b > bit)
                first = my_bit("dp", bit) == 0
                here, other = self.piece[k], arrived[k]
                self.piece[k] = jnp.stack(
                    [jnp.where(first, here, other), jnp.where(first, other, here)], axis=place
                )
            self.held[k].append(bit)
        self.split()
        if not self.todo[0]:
            lanes = [lane.reshape(-1, lane.shape[-1]) for lane in self.piece]
            self.piece = []
            start = 0
            for width in self.widths:
                self.piece.append(columns_between(lanes, start, start + width))
                start += width

    def complete(self):
        return self.far is not None

    def pair(self, index):
        return self.piece[index], self.far[index]


class Scatter:
    def __init__(self, pairs):
        self.mine = [pair[0] for pair in pairs]
        self.piece = [pair[1].astype(jnp.bfloat16) for pair in pairs]
        self.todo = [bit_order(0)[::-1], bit_order(1)[::-1]]
        self.left = [sorted(todo, reverse=True) for todo in self.todo]
        self.rest = list(range(1, axis_bits("grp")))
        self.whole = None
        self.rows = None
        self.moving = None
        self.far = None

    def sends(self):
        if self.whole is None:
            return list(self.piece)
        if self.todo[0]:
            return [
                lax.dynamic_index_in_dim(
                    lane, 1 - my_bit("dp", todo[0]), left.index(todo[0]), keepdims=False
                )
                for lane, todo, left in zip(self.whole, self.todo, self.left)
            ]
        return [self.rows]

    def start(self, sends):
        if self.whole is None:
            self.moving = [swap_bit(part, "grp", 0) for part in sends]
        elif self.todo[0]:
            self.moving = [
                swap_bit(away, "dp", todo[0]) for away, todo in zip(sends, self.todo)
            ]
        else:
            self.moving = [swap_bit(sends[0], "grp", self.rest[0] if self.rest else 0)]

    def land(self):
        arrived, self.moving = self.moving, None
        if self.whole is None:
            both = [
                (mine + other.astype(jnp.float32)).astype(jnp.bfloat16)
                for mine, other in zip(self.mine, arrived)
            ]
            both = [part.reshape((2,) * len(self.left[0]) + (-1, part.shape[1])) for part in both]
            width = sum(part.shape[-1] for part in both)
            cut = lane_cut(width)
            if len(both) == 1:
                self.whole = [both[0][..., :cut], both[0][..., cut:]]
            else:
                tail = jnp.concatenate([both[0][..., cut:]] + both[1:], axis=-1)
                self.whole = [both[0][..., :cut], tail]
        elif self.todo[0]:
            for k in range(2):
                bit = self.todo[k].pop(0)
                if k < len(arrived):
                    keep = lax.dynamic_index_in_dim(
                        self.whole[k], my_bit("dp", bit), self.left[k].index(bit), keepdims=False
                    )
                    self.whole[k] = (
                        keep.astype(jnp.float32) + arrived[k].astype(jnp.float32)
                    ).astype(jnp.bfloat16)
                self.left[k].remove(bit)
            if len(self.whole) == 2 and self.left[0] == self.left[1]:
                self.whole = [jnp.concatenate(self.whole, axis=-1)]
            if not self.todo[0]:
                self.rows = self.whole[0]
        elif self.rest:
            self.rest.pop(0)
            self.rows = (
                self.rows.astype(jnp.float32) + arrived[0].astype(jnp.float32)
            ).astype(jnp.bfloat16)
        else:
            self.far = arrived[0]

    def complete(self):
        return self.far is not None


def checkpoint(act, land=(), start=()):
    land = [move for move in land if move.moving is not None]
    if not land and not start:
        return act
    act, arrived = lax.optimization_barrier((act, [move.moving for move in land]))
    for move, value in zip(land, arrived):
        move.moving = value
        move.land()
    going = [move for move in land if not move.complete()] + list(start)
    act, sends = lax.optimization_barrier((act, [move.sends() for move in going]))
    for move, value in zip(going, sends):
        move.start(value)
    return act


def finish(act, move):
    while not move.complete():
        act = checkpoint(act, [move])
    return act


def fold_rows(value, count):
    ratio = FF // D
    wide = value.reshape(-1, ratio, count, value.shape[1])
    return jnp.swapaxes(wide, 1, 2).reshape(-1, ratio * value.shape[1])


def unfold_rows(value, count):
    ratio = FF // D
    wide = value.reshape(-1, count, ratio, value.shape[1] // ratio)
    return jnp.swapaxes(wide, 1, 2).reshape(-1, value.shape[1] // ratio)


def in_order(mine, other, first):
    return jnp.concatenate(
        [jnp.where(first, mine, other), jnp.where(first, other, mine)], axis=1
    )


def own_and_far(value, first):
    half = value.shape[1] // 2
    low, high = value[:, :half], value[:, half:]
    return jnp.where(first, low, high), jnp.where(first, high, low)


def segment_info(seq_lengths, rows_here):
    seq_ends = jnp.cumsum(seq_lengths)
    row_ids = jnp.arange(rows_here, dtype=jnp.int32)
    past_end = (row_ids[:, None] >= seq_ends[None, :]).astype(jnp.int32)
    segment = jnp.sum(past_end, axis=1)
    positions = row_ids - jnp.sum(past_end * seq_lengths[None, :], axis=1)
    member = (
        segment[:, None] == jnp.arange(seq_lengths.shape[0], dtype=jnp.int32)[None, :]
    ).astype(jnp.float32)
    return (positions, member, segment)


PAIR = 2 * HDIM


def rotary_tables(positions):
    half_dim = HDIM // 2
    frequency = rotary_base ** (-2.0 * jnp.arange(half_dim, dtype=jnp.float32) / HDIM)
    angles = positions.astype(jnp.float32)[:, None] * frequency[None, :]
    cosine, sine = jnp.cos(angles), jnp.sin(angles)
    return (
        jnp.concatenate([cosine] * 4, axis=1),
        jnp.concatenate([-sine, sine, -sine, sine], axis=1),
    )


def half_swap(values):
    lane = lax.broadcasted_iota(jnp.int32, values.shape, 1)
    front = (lane % HDIM) < HDIM // 2
    return jnp.where(
        front,
        pltpu.roll(values, PAIR - HDIM // 2, 1),
        pltpu.roll(values, HDIM // 2, 1),
    )


def pair_dot(left, right, contract):
    return lax.dot_general(
        left, right, ((contract[:1], contract[1:]), ((), ())), preferred_element_type=jnp.float32
    )


def head_lanes(shape, head):
    return lax.broadcasted_iota(jnp.int32, shape, 1) // HDIM == head


def head_only(values, head):
    wide = values.astype(jnp.float32)
    return jnp.where(head_lanes(values.shape, head), wide, 0.0).astype(values.dtype)


def head_softmax(query, key, row_seg, col_seg, head):
    scores = pair_dot(head_only(query, head), key, (1, 1)) * (1.0 / math.sqrt(HDIM))
    scores = jnp.where(row_seg == col_seg, scores, masked_score)
    peak = jnp.max(scores, axis=1, keepdims=True)
    raised = jnp.exp(scores - peak)
    return raised / jnp.sum(raised, axis=1, keepdims=True)


def attend_kernel(q_in, k_in, v_in, cos_in, sin_in, row_in, col_in, q_out, k_out, v_out, o_out):
    cosine, sine = cos_in[...], sin_in[...]
    query = q_in[...]
    key = k_in[...]
    query = (query * cosine + half_swap(query) * sine).astype(jnp.bfloat16)
    key = (key * cosine + half_swap(key) * sine).astype(jnp.bfloat16)
    value = v_in[...].astype(jnp.bfloat16)
    q_out[...] = query
    k_out[...] = key
    v_out[...] = value
    parts = []
    for head in range(2):
        weights_p = head_softmax(query, key, row_in[...], col_in[...], head)
        parts.append(pair_dot(weights_p.astype(jnp.bfloat16), value, (1, 0)))
    mixed = jnp.where(head_lanes(parts[0].shape, 0), parts[0], parts[1])
    o_out[...] = mixed.astype(jnp.bfloat16)


def attend_back_kernel(
    q_in, k_in, v_in, do_in, cos_in, sin_in, row_in, col_in, dq_out, dk_out, dv_out
):
    query, key, value, grad = q_in[...], k_in[...], v_in[...], do_in[...]
    sides = []
    for head in range(2):
        weights_p = head_softmax(query, key, row_in[...], col_in[...], head)
        prob_grad = pair_dot(head_only(grad, head), value, (1, 1))
        center = jnp.sum(prob_grad * weights_p, axis=1, keepdims=True)
        score_grad = (weights_p * (prob_grad - center)).astype(jnp.bfloat16)
        low = weights_p.astype(jnp.bfloat16)
        sides.append(
            (
                pair_dot(score_grad, key, (1, 0)),
                pair_dot(score_grad, query, (0, 0)),
                pair_dot(low, grad, (0, 0)),
            )
        )
    first = head_lanes(query.shape, 0)
    dq, dk, dv = (jnp.where(first, one, two) for one, two in zip(*sides))
    cosine, sine = cos_in[...], sin_in[...]
    for out, side in ((dq_out, dq), (dk_out, dk)):
        side = side * (1.0 / math.sqrt(HDIM))
        out[...] = (side * cosine - half_swap(side) * sine).astype(jnp.bfloat16)
    dv_out[...] = dv.astype(jnp.bfloat16)


def pair_specs(rows_here):
    def block(offset):
        return pl.BlockSpec((rows_here, PAIR), lambda j, offset=offset: (0, j + offset))

    table = pl.BlockSpec((rows_here, PAIR), lambda j: (0, 0))
    row = pl.BlockSpec((rows_here, 1), lambda j: (0, 0))
    col = pl.BlockSpec((1, rows_here), lambda j: (0, 0))
    return block, [table, table, row, col]


def attend(merged, rotary, segment):
    rows_here = merged.shape[0]
    pairs = D // PAIR
    block, shared = pair_specs(rows_here)
    return pl.pallas_call(
        attend_kernel,
        grid=(pairs,),
        in_specs=[block(0), block(pairs), block(2 * pairs)] + shared,
        out_specs=[block(0)] * 4,
        out_shape=[jax.ShapeDtypeStruct((rows_here, D), jnp.bfloat16)] * 4,
        name="attend",
    )(merged, merged, merged, *rotary, segment[:, None], segment[None, :])


def attend_back(query, key, value, grad, rotary, segment):
    rows_here = query.shape[0]
    block, shared = pair_specs(rows_here)
    return pl.pallas_call(
        attend_back_kernel,
        grid=(D // PAIR,),
        in_specs=[block(0)] * 4 + shared,
        out_specs=[block(0)] * 3,
        out_shape=[jax.ShapeDtypeStruct((rows_here, D), jnp.bfloat16)] * 3,
        name="attend_back",
    )(query, key, value, grad, *rotary, segment[:, None], segment[None, :])


def normalize(values):
    centered = values - jnp.mean(values, axis=-1, keepdims=True)
    inv_std = lax.rsqrt(jnp.mean(centered * centered, axis=-1, keepdims=True) + norm_eps)
    return (centered * inv_std, inv_std)


def norm_back(grad, normed, inv_std, gain):
    scaled = grad * gain
    inner = inv_std * (
        scaled
        - jnp.mean(scaled, axis=-1, keepdims=True)
        - normed * jnp.mean(scaled * normed, axis=-1, keepdims=True)
    )
    return (inner, jnp.sum(grad * normed, axis=0), jnp.sum(grad, axis=0))


def layer_forward(inputs, weights, rotary, segment, first_core, hook):
    inputs = hook("joint", inputs)
    joint_w = weights["joint"]
    inputs_low = inputs.astype(jnp.bfloat16)
    merged = in_order(
        jnp.dot(inputs_low, joint_w[0], preferred_element_type=jnp.float32),
        jnp.dot(inputs_low, joint_w[1], preferred_element_type=jnp.float32),
        first_core,
    )
    merged = hook("qkv", merged)
    query_rot, key_rot, value_low, mixed = attend(merged, rotary, segment)
    mixed = hook("mixed", mixed)
    output_w, gain_rows = weights["output"], weights["norms"]
    attended = jnp.dot(mixed, output_w, preferred_element_type=jnp.float32)
    first_normed, first_inv = normalize(inputs + attended)
    hidden = first_normed * gain_rows[0] + gain_rows[1]
    hidden = hook("gateup", hidden)
    hidden_low = hidden.astype(jnp.bfloat16)
    gateup_w = weights["gateup"]
    own_part = jnp.dot(hidden_low, gateup_w[0], preferred_element_type=jnp.float32)
    far_part = jnp.dot(hidden_low, gateup_w[1], preferred_element_type=jnp.float32)
    gate_part = jnp.where(first_core, own_part, far_part)
    up_part = jnp.where(first_core, far_part, own_part)
    act_low = (jax.nn.silu(gate_part) * up_part).astype(jnp.bfloat16)
    act_low = hook("down", act_low)
    branch = jnp.dot(act_low, weights["down"], preferred_element_type=jnp.float32)
    second_normed, second_inv = normalize(hidden + branch)
    result = second_normed * gain_rows[2] + gain_rows[3]
    kept = (
        inputs_low,
        query_rot,
        key_rot,
        value_low,
        mixed,
        first_normed,
        first_inv,
        hidden_low,
        own_part,
        far_part,
        act_low,
        second_normed,
        second_inv,
    )
    return (result, kept)


def layer_backward(grad_out, weights, kept, rotary, segment, first_core, hook):
    joint_w, output_w, gateup_w, down_w, gain_rows = (
        weights[name] for name in ("joint", "output", "gateup", "down", "norms")
    )
    (
        inputs_low,
        query_rot,
        key_rot,
        value_low,
        mixed,
        first_normed,
        first_inv,
        hidden_low,
        own_part,
        far_part,
        act_low,
        second_normed,
        second_inv,
    ) = kept
    second_in, gain_two, bias_two = norm_back(grad_out, second_normed, second_inv, gain_rows[2])
    second_in = hook("second", second_in)
    branch_grad = second_in.astype(jnp.bfloat16)
    down_grad = tuple(
        jnp.einsum("tf,td->fd", act_low, part, preferred_element_type=jnp.float32)
        for part in own_and_far(branch_grad, first_core)
    )
    act_grad = jnp.einsum("td,fd->tf", branch_grad, down_w, preferred_element_type=jnp.float32)
    gate_part = jnp.where(first_core, own_part, far_part)
    up_part = jnp.where(first_core, far_part, own_part)
    sigmoid_g = jax.nn.sigmoid(gate_part)
    gate_grad = act_grad * up_part * sigmoid_g * (1.0 + gate_part * (1.0 - sigmoid_g))
    up_grad = act_grad * gate_part * sigmoid_g
    own_grad = jnp.where(first_core, gate_grad, up_grad).astype(jnp.bfloat16)
    far_grad = jnp.where(first_core, up_grad, gate_grad).astype(jnp.bfloat16)
    own_grad, far_grad = hook("act", (own_grad, far_grad))
    gateup_grad = tuple(
        jnp.einsum("td,tf->df", hidden_low, part, preferred_element_type=jnp.float32)
        for part in (own_grad, far_grad)
    )
    own_grad = hook("gateup", own_grad, gateup_grad, down_grad)
    hidden_grad = (
        second_in
        + jnp.einsum("tf,df->td", own_grad, gateup_w[0], preferred_element_type=jnp.float32)
        + jnp.einsum("tf,df->td", far_grad, gateup_w[1], preferred_element_type=jnp.float32)
    )
    first_in, gain_one, bias_one = norm_back(hidden_grad, first_normed, first_inv, gain_rows[0])
    first_in = hook("first", first_in)
    attended_grad = first_in.astype(jnp.bfloat16)
    output_grad = tuple(
        jnp.einsum("tc,td->cd", mixed, part, preferred_element_type=jnp.float32)
        for part in own_and_far(attended_grad, first_core)
    )
    mixed_grad = jnp.einsum(
        "td,cd->tc", attended_grad, output_w, preferred_element_type=jnp.float32
    )
    merged_grad = jnp.concatenate(
        attend_back(
            query_rot, key_rot, value_low, mixed_grad.astype(jnp.bfloat16), rotary, segment
        ),
        axis=1,
    )
    merged_grad = hook("merged", merged_grad)
    merged_own, merged_far = own_and_far(merged_grad, first_core)
    joint_grad = tuple(
        jnp.einsum("tc,tf->cf", inputs_low, part, preferred_element_type=jnp.float32)
        for part in (merged_own, merged_far)
    )
    norms_grad = jnp.stack([gain_one, bias_one, gain_two, bias_two])
    merged_own = hook("joint", merged_own, joint_grad, output_grad, norms_grad)
    input_grad = (
        first_in
        + jnp.einsum("tf,cf->tc", merged_own, joint_w[0], preferred_element_type=jnp.float32)
        + jnp.einsum("tf,cf->tc", merged_far, joint_w[1], preferred_element_type=jnp.float32)
    )
    return (input_grad, (joint_grad, output_grad, gateup_grad, down_grad, norms_grad))


def adamw_update(grad, master, first, second, bias_first, bias_second, rate, decay):
    moment = beta_one * first + (1.0 - beta_one) * grad
    squared_values = beta_two * second + (1.0 - beta_two) * grad * grad
    newer = master - rate * (
        moment / bias_first / (jnp.sqrt(squared_values / bias_second) + adam_eps) + decay * master
    )
    return (newer, moment, squared_values, newer.astype(jnp.bfloat16))


def body(
    incoming_vectors,
    sequence_extents,
    matching_document_index,
    softmax_sharpness,
    optimizer_iteration_number,
    attention_entry_master,
    attention_entry_first_moment,
    attention_entry_second_moment,
    attention_exit_master,
    attention_exit_first_moment,
    attention_exit_second_moment,
    widening_projection_master,
    widening_first_moment,
    widening_second_moment,
    lowering_projection_master,
    lowering_first_moment,
    lowering_second_moment,
    layernorm_affine_master,
    layernorm_affine_first_moment,
    layernorm_affine_second_moment,
):
    core = lax.axis_index("grp") & 1
    first_core = core == 0
    rows_shard = attention_entry_master.shape[1]
    halves = []
    for layer_idx in range(LAYERS):
        parts = {
            "joint": attention_entry_master[layer_idx],
            "output": attention_exit_master[layer_idx],
            "gateup": widening_projection_master[layer_idx],
            "down": lowering_projection_master[layer_idx],
        }
        parts = {k: core_half(v, core, 1).astype(jnp.bfloat16) for k, v in parts.items()}
        parts["down"] = fold_rows(parts["down"], rows_shard)
        halves.append(parts)
    norm_cols = layernorm_affine_master.reshape(LAYERS * 4, rows_shard).T.astype(jnp.bfloat16)
    norm_cols = jnp.pad(norm_cols, ((0, 0), (0, 128 - LAYERS * 4)))
    entries = [
        Gather([halves[0]["joint"], halves[0]["output"], norm_cols]),
        Gather([halves[1]["joint"], halves[1]["output"]]),
    ]
    wides = [Gather([half["gateup"], half["down"]]) for half in halves]
    half_joint = halves[0]["joint"].shape[1]
    half_output = halves[0]["output"].shape[1]
    weights = [{}, {}]

    def put_entry(layer_idx, act):
        act = finish(act, entries[layer_idx])
        weights[layer_idx]["joint"] = entries[layer_idx].pair(0)
        weights[layer_idx]["output"] = in_order(*entries[layer_idx].pair(1), first_core)
        return act

    def put_wide(layer_idx, act):
        act = finish(act, wides[layer_idx])
        weights[layer_idx]["gateup"] = wides[layer_idx].pair(0)
        pair = (unfold_rows(part, rows_shard) for part in wides[layer_idx].pair(1))
        weights[layer_idx]["down"] = in_order(*pair, first_core)
        return act

    def hook_zero(name, act):
        if name == "joint":
            act = checkpoint(act, start=[entries[0]])
            act = checkpoint(act, [entries[0]], [wides[0]])
            act = checkpoint(act, [entries[0]])
            act = checkpoint(act, [entries[0], wides[0]])
            act = checkpoint(act, [entries[0], wides[0]])
            act = put_entry(0, act)
            norm_full = entries[0].piece[2][:, : LAYERS * 4]
            norm_full = norm_full.T.reshape(LAYERS, 4, D).astype(jnp.float32)
            for layer_idx in range(LAYERS):
                weights[layer_idx]["norms"] = norm_full[layer_idx]
        elif name == "qkv":
            act = checkpoint(act, [wides[0]], [entries[1], wides[1]])
        elif name == "mixed":
            act = checkpoint(act, [entries[1], wides[1]])
        elif name == "gateup":
            act = checkpoint(act, [wides[0]])
            act = checkpoint(act, [entries[1], wides[1]])
            act = put_wide(0, act)
        elif name == "down":
            act = checkpoint(act, [entries[1]])
        return act

    def hook_one(name, act):
        if name == "joint":
            act = checkpoint(act, [entries[1], wides[1]])
            act = put_entry(1, act)
        elif name == "mixed":
            act = checkpoint(act, [wides[1]])
        elif name == "gateup":
            act = put_wide(1, act)
        return act

    rows_here = incoming_vectors.shape[0]
    seqs_here = sequence_extents.shape[0]
    positions, member, segment = segment_info(sequence_extents, rows_here)
    rotary = rotary_tables(positions)
    length_float = sequence_extents.astype(jnp.float32)[:, None]
    hidden_state = incoming_vectors.astype(jnp.float32)
    kept_list = []
    for layer_idx in range(LAYERS):
        hidden_state, kept = layer_forward(
            hidden_state,
            weights[layer_idx],
            rotary,
            segment,
            first_core,
            (hook_zero, hook_one)[layer_idx],
        )
        kept_list.append(kept)
    hidden_out = hidden_state.astype(jnp.bfloat16)
    pooled = (
        jnp.einsum("ts,td->sd", member, hidden_state, precision=topmost_precision) / length_float
    )
    inv_norm = lax.rsqrt(jnp.sum(pooled * pooled, axis=-1, keepdims=True) + embed_eps)
    embed_low = (pooled * inv_norm).astype(jnp.bfloat16)
    every = cube_gather(embed_low, "dp", bit_order(0))
    every = cube_gather(every, "grp", list(range(axis_bits("grp") - 1, -1, -1)))
    every = every.reshape(-1, D)
    query_count = every.shape[0] // 2
    queries = every[:query_count]
    documents = every[query_count:]
    my_index = lax.axis_index("grp") * lax.axis_size("dp") + lax.axis_index("dp")
    is_query = lax.axis_index("grp") < lax.axis_size("grp") // 2
    logit_scale_factor = 1.0 / softmax_sharpness[0]
    similarity_logits = (
        jnp.einsum("qd,kd->qk", queries, documents, preferred_element_type=jnp.float32)
        * logit_scale_factor
    )
    target_rows = (
        jnp.arange(query_count, dtype=jnp.int32)[None, :] == matching_document_index[:, None]
    ).astype(jnp.float32)
    row_peak = jnp.max(similarity_logits, axis=-1, keepdims=True)
    exp_scores = jnp.exp(similarity_logits - row_peak)
    softmax_sum = jnp.sum(exp_scores, axis=-1, keepdims=True)
    row_loss = (
        row_peak[:, 0]
        + jnp.log(softmax_sum[:, 0])
        - jnp.sum(similarity_logits * target_rows, axis=-1)
    )
    loss_total = jnp.sum(row_loss) / query_count
    score_grad = (exp_scores / softmax_sum - target_rows) / query_count
    score_side = jnp.where(is_query, score_grad, score_grad.T)
    start_own = (my_index % (query_count // seqs_here)) * seqs_here
    score_own = lax.dynamic_slice_in_dim(score_side, start_own, seqs_here, axis=0)
    facing = jnp.where(is_query, documents, queries).astype(jnp.float32)
    embed_grad = (
        jnp.einsum("sk,kd->sd", score_own, facing, precision=topmost_precision)
        * logit_scale_factor
    )
    pooled_grad = inv_norm * embed_grad - pooled * inv_norm * inv_norm * inv_norm * jnp.sum(
        pooled * embed_grad, axis=-1, keepdims=True
    )
    state_grad = jnp.einsum(
        "ts,sd->td", member, pooled_grad / length_float, precision=topmost_precision
    )
    sums = [{}, {}]

    def pair_of(columns):
        own = jnp.concatenate([pair[0] for pair in columns], axis=1)
        far = jnp.concatenate([pair[1].astype(jnp.bfloat16) for pair in columns], axis=1)
        return own, far

    def folded(pair):
        return tuple(fold_rows(part, rows_shard) for part in pair)

    def wide_sum(gateup_pair, down_pair):
        return Scatter([gateup_pair, folded(down_pair)])

    def back_one(name, act, *grads):
        moves = sums[1]
        if name == "gateup":
            moves["wide"] = wide_sum(*grads)
            act = checkpoint(act, start=[moves["wide"]])
        elif name in ("first", "merged"):
            act = checkpoint(act, [moves["wide"]])
        elif name == "joint":
            moves["entry"] = Scatter([pair_of(grads[:2])])
            moves["norms"] = grads[2]
            act = checkpoint(act, start=[moves["entry"]])
        return act

    def back_zero(name, act, *grads):
        early, moves = [sums[1]["wide"], sums[1]["entry"]], sums[0]
        if name in ("second", "act"):
            act = checkpoint(act, early)
        elif name == "gateup":
            moves["wide"] = wide_sum(*grads)
            act = checkpoint(act, start=[moves["wide"]])
        elif name == "first":
            act = checkpoint(act, [moves["wide"]] + early)
        elif name == "merged":
            act = checkpoint(act, [moves["wide"]] + early)
        elif name == "joint":
            norm_cols = jnp.stack([grads[2], sums[1]["norms"]]).reshape(LAYERS * 4, D).T
            norm_cols = jnp.pad(norm_cols, ((0, 0), (0, 128 - LAYERS * 4)))
            moves["entry"] = Scatter([pair_of([grads[0], grads[1], (norm_cols, norm_cols)])])
            act = checkpoint(act, start=[moves["entry"]])
        return act

    state_grad, _ = layer_backward(
        state_grad, weights[1], kept_list[1], rotary, segment, first_core, back_one
    )
    state_grad, _ = layer_backward(
        state_grad, weights[0], kept_list[0], rotary, segment, first_core, back_zero
    )
    last = [layer[kind] for layer in sums[::-1] for kind in ("wide", "entry")]
    while not all(move.complete() for move in last):
        state_grad = checkpoint(state_grad, last)

    def columns_of(kind, start, stop):
        return [
            in_order(layer[kind].rows[:, start:stop], layer[kind].far[:, start:stop], first_core)
            for layer in sums
        ]

    def down_of(layer):
        move = layer["wide"]
        pair = (unfold_rows(v[:, FF:], rows_shard) for v in (move.rows, move.far))
        return in_order(*pair, first_core)

    half_entry = half_joint + half_output
    rows = (
        columns_of("entry", 0, half_joint),
        columns_of("entry", half_joint, half_entry),
        columns_of("wide", 0, FF),
        [down_of(layer) for layer in sums],
    )
    shards = [jnp.stack(pair).astype(jnp.float32) for pair in rows]
    norm_shard = sums[0]["entry"].rows[:, half_entry:][:, : LAYERS * 4].astype(jnp.float32)
    shards.append(norm_shard.T.reshape(LAYERS, 4, -1))
    step_float = optimizer_iteration_number[0].astype(jnp.float32)
    bias_first = 1.0 - jnp.power(beta_one, step_float)
    bias_second = 1.0 - jnp.power(beta_two, step_float)
    joint_weight, joint_moment, joint_square, joint_copy = adamw_update(
        shards[0],
        attention_entry_master,
        attention_entry_first_moment,
        attention_entry_second_moment,
        bias_first,
        bias_second,
        rate_matrix,
        decay_rate,
    )
    output_weight, output_moment, output_square, output_copy = adamw_update(
        shards[1],
        attention_exit_master,
        attention_exit_first_moment,
        attention_exit_second_moment,
        bias_first,
        bias_second,
        rate_matrix,
        decay_rate,
    )
    gateup_weight, gateup_moment, gateup_square, gateup_copy = adamw_update(
        shards[2],
        widening_projection_master,
        widening_first_moment,
        widening_second_moment,
        bias_first,
        bias_second,
        rate_matrix,
        decay_rate,
    )
    down_weight, down_moment, down_square, down_copy = adamw_update(
        shards[3],
        lowering_projection_master,
        lowering_first_moment,
        lowering_second_moment,
        bias_first,
        bias_second,
        rate_matrix,
        decay_rate,
    )
    norms_weight, norms_moment, norms_square, norms_copy = adamw_update(
        shards[4],
        layernorm_affine_master,
        layernorm_affine_first_moment,
        layernorm_affine_second_moment,
        bias_first,
        bias_second,
        rate_norms,
        0.0,
    )
    loss_value = jnp.reshape(loss_total, (1,))
    return (
        hidden_out,
        state_grad,
        loss_value,
        joint_weight,
        joint_moment,
        joint_square,
        joint_copy,
        output_weight,
        output_moment,
        output_square,
        output_copy,
        gateup_weight,
        gateup_moment,
        gateup_square,
        gateup_copy,
        down_weight,
        down_moment,
        down_square,
        down_copy,
        norms_weight,
        norms_moment,
        norms_square,
        norms_copy,
    )


def solution(mesh):
    return jax.shard_map(
        body,
        mesh=mesh,
        in_specs=(
            P(("grp", "dp"), None),
            P(("grp", "dp")),
            P(),
            P(),
            P(),
            P(None, "dp", None),
            P(None, "dp", None),
            P(None, "dp", None),
            P(None, "dp", None),
            P(None, "dp", None),
            P(None, "dp", None),
            P(None, "dp", None),
            P(None, "dp", None),
            P(None, "dp", None),
            P(None, "dp", None),
            P(None, "dp", None),
            P(None, "dp", None),
            P(None, None, "dp"),
            P(None, None, "dp"),
            P(None, None, "dp"),
        ),
        out_specs=(
            P(("grp", "dp"), None),
            P(("grp", "dp"), None),
            P(),
            P(None, "dp", None),
            P(None, "dp", None),
            P(None, "dp", None),
            P(None, "dp", None),
            P(None, "dp", None),
            P(None, "dp", None),
            P(None, "dp", None),
            P(None, "dp", None),
            P(None, "dp", None),
            P(None, "dp", None),
            P(None, "dp", None),
            P(None, "dp", None),
            P(None, "dp", None),
            P(None, "dp", None),
            P(None, "dp", None),
            P(None, "dp", None),
            P(None, None, "dp"),
            P(None, None, "dp"),
            P(None, None, "dp"),
            P(None, None, "dp"),
        ),
        check_vma=False,
    )
```
